128 devices in a mesh: grp: 4 (over x_lo, core), tile: 32 (over y, z, x_hi).
Axes of the slice: x: 4 (x_hi: 2, x_lo: 2; x = x_hi * 2 + x_lo), y: 4, z: 4, core: 2. Of those that a mesh axis runs over, the one named last changes fastest.
Arguments:
- raw: bfloat16 [16, 256, 15360], P('grp', 'tile'), may hold values from 0.25 to 4
- scales: bfloat16 [16, 64, 480], P('grp', 'tile'), may hold values from 0.29882812 to 1.1953125
- flat: float32 [256, 15360], P(None, 'tile'), may hold values from 0.25 to 1.75
- spectrum: float32 [32, 2, 256, 512], P('tile'), may hold values from -5 to 5
- pupil: float32 [2, 64, 128], replicated, may hold values from -5 to 5
- patterns: int32 [16, 4], replicated, may hold values from 0 to 31, all different within a row
- led_row: int32 [32], replicated, may hold values from 0 to 192
- led_col: int32 [32], replicated, may hold values from 0 to 384
Outputs:
- new_spectrum: float32 [32, 2, 256, 512], P('tile')
- stitched: float32 [2, 256, 15360], P(None, None, 'tile')
The draws below stay inside these ranges and needn't reach their ends.
Inputs may be any that keep to these rules, and one draw needn't show every extreme that they name: `patterns`: each frame lights 4 different LEDs, and every LED is lit in some frame.
All inputs are finite; a program needn't handle non-finite values.
Results may differ from the reference program's by a relative error of at most 0.0003.
Values may be sent and summed in bfloat16 or wider, within the bound.
A program may use at most 128 MiB of HBM per device.

```python
import math
import jax
import jax.numpy as jnp
from jax import lax

TH = 256
TW = 512
OV = 32
BR = 4
BC = 32
PR = 64
PC = 128
LEDS = 4
NLED = 32
TILES = 32
W = 15360
FRAMES = 16


def plant(entries, rng, least, high):
    extent = entries.shape
    spot = [jax.random.randint(jax.random.fold_in(rng, axis), (), 0, extent[axis]) for axis in range(len(extent))]
    entries = entries.at[tuple(spot)].set(least)
    longest = extent.index(max(extent))
    spot[longest] = (spot[longest] + 1) % extent[longest]
    return entries.at[tuple(spot)].set(high)


def shard_levels(rng, dims, split, least, top_value):
    def one(axis_at, shards_of):
        draws = jax.random.uniform(jax.random.fold_in(jax.random.fold_in(rng, 6), axis_at), (shards_of,), jnp.float32, least / len(split), top_value / len(split))
        return jnp.repeat(jnp.exp(draws), dims[axis_at] // shards_of).reshape((-1,) + (1,) * (len(dims) - axis_at - 1))

    loudness = one(*split[0])
    for cut in split[1:]:
        loudness = loudness * one(*cut)
    return loudness


def picks_of(own_key, rows, amount, top, lift):
    order = jax.random.permutation(jax.random.fold_in(own_key, 1), amount)
    pull = order
    for power in range(3):
        pull = pull * pull // amount
    pull = pull * lift // amount
    chance = jax.random.randint(jax.random.fold_in(own_key, 2), (rows, amount), 0, 4096) + pull
    holders = jax.random.permutation(jax.random.fold_in(own_key, 3), rows)[jnp.arange(amount) % rows]
    chance = jnp.where(jnp.arange(rows)[:, None] == holders[None, :], 1 << 14, chance)
    priority = chance * amount + jnp.arange(amount)
    return lax.top_k(priority.astype(jnp.int32), top)[1].astype(jnp.int32)


def gaussian(own_key, extent, scale, bound, shards=(), kind=jnp.bfloat16):
    drawn = scale * jax.random.normal(own_key, extent, jnp.float32)
    if shards:
        drawn = drawn * shard_levels(own_key, extent, shards, -0.22, 0.18)
    return jnp.clip(drawn, -bound, bound).astype(kind)


def setup_inputs(seed: int = 0) -> dict:
    key_of = jax.random.split(jax.random.key(seed), 9)
    return {
        "raw": jnp.clip(0.25 + 3.75 * jax.random.uniform(key_of[0], (FRAMES, TH, W), jnp.float32) ** shard_levels(key_of[0], (FRAMES, TH, W), ((0, 4), (1, 32)), -0.2, 0.2), 0.25, 4.0).astype(jnp.bfloat16),
        "scales": jnp.clip(jnp.exp(math.log(1.1953125) - 1.3862944 * jax.random.uniform(key_of[1], (FRAMES, TH // BR, W // BC), jnp.float32) ** shard_levels(key_of[1], (FRAMES, TH // BR, W // BC), ((0, 4), (1, 32)), -0.2, 0.2)), 0.29882812, 1.1953125).astype(jnp.bfloat16),
        "flat": jnp.clip(1.0 + 0.15 * jax.random.normal(key_of[2], (TH, W), jnp.float32), 0.25, 1.75),
        "spectrum": gaussian(key_of[3], (TILES, 2, TH, TW), 0.7, 5.0, ((0, 32),), jnp.float32),
        "pupil": gaussian(key_of[4], (2, PR, PC), 0.7, 5.0, (), jnp.float32),
        "patterns": picks_of(key_of[5], FRAMES, NLED, LEDS, 0),
        "led_row": plant(jax.random.randint(key_of[6], (NLED,), 0, TH - PR + 1), jax.random.fold_in(key_of[6], 1), 0, TH - PR).astype(jnp.int32),
        "led_col": plant(jax.random.randint(key_of[7], (NLED,), 0, TW - PC + 1), jax.random.fold_in(key_of[7], 1), 0, TW - PC).astype(jnp.int32),
    }


step_size = 0.02
highest = lax.Precision.HIGHEST

def wave_table(length, band):
    places = jnp.arange(length, dtype=jnp.int32)[:, None]
    freqs = jnp.arange(band, dtype=jnp.int32)[None, :] - band // 2
    turns = places * freqs % length
    angle = turns.astype(jnp.float32) * (2.0 * math.pi / length)
    factor = 1.0 / math.sqrt(band)
    return (jnp.cos(angle) * factor, jnp.sin(angle) * factor)

def complex_product(form, left_pair, right_pair):
    left_re, left_im = left_pair
    right_re, right_im = right_pair

    def einsum_pair(first, second):
        return jnp.einsum(form, first, second, precision=highest)
    return (einsum_pair(left_re, right_re) - einsum_pair(left_im, right_im), einsum_pair(left_re, right_im) + einsum_pair(left_im, right_re))

def remove_tilt(flattened):
    rows_n = flattened.shape[1]
    cols_n = flattened.shape[2]
    ycentre = jnp.arange(rows_n, dtype=jnp.float32) - (rows_n - 1) / 2.0
    xcentre = jnp.arange(cols_n, dtype=jnp.float32) - (cols_n - 1) / 2.0
    slope_y = lax.optimization_barrier(jnp.sum(flattened * ycentre[None, :, None], axis=(1, 2))) / (jnp.sum(ycentre * ycentre) * cols_n)
    slope_x = lax.optimization_barrier(jnp.sum(flattened * xcentre[None, None, :], axis=(1, 2))) / (jnp.sum(xcentre * xcentre) * rows_n)
    return flattened - slope_y[:, None, None] * ycentre[None, :, None] - slope_x[:, None, None] * xcentre[None, None, :]

def box_gradients(spectrum_tile, window, pupil, row_starts, col_starts, lit_count):
    band_rows = pupil.shape[1]
    band_cols = pupil.shape[2]
    height = window.shape[1]
    width = window.shape[2]
    frames_n = window.shape[0]
    anchor = jnp.zeros((), jnp.int32)

    def cut_box(row_top, col_left):
        return lax.dynamic_slice(spectrum_tile, (anchor, row_top, col_left), (2, band_rows, band_cols))
    boxes = jax.vmap(cut_box)(row_starts, col_starts)
    pupil_re = pupil[0]
    pupil_im = pupil[1]
    lit_re = pupil_re * boxes[:, 0] - pupil_im * boxes[:, 1]
    lit_im = pupil_re * boxes[:, 1] + pupil_im * boxes[:, 0]
    rows_re, rows_im = wave_table(height, band_rows)
    cols_re, cols_im = wave_table(width, band_cols)
    spread = complex_product('bup,xp->bux', (lit_re, lit_im), (cols_re, cols_im))
    field_re, field_im = complex_product('yu,bux->byx', (rows_re, rows_im), spread)
    field_re = field_re.reshape(frames_n, lit_count, height, width)
    field_im = field_im.reshape(frames_n, lit_count, height, width)
    estimate = lax.optimization_barrier(jnp.sum(field_re * field_re + field_im * field_im, axis=1))
    misfit = estimate - window
    weighted_re = (misfit[:, None] * field_re).reshape(frames_n * lit_count, height, width)
    weighted_im = (misfit[:, None] * field_im).reshape(frames_n * lit_count, height, width)
    back = complex_product('yu,byx->bux', (rows_re, -rows_im), (weighted_re, weighted_im))
    tile_re, tile_im = complex_product('bux,xp->bup', back, (cols_re, -cols_im))
    grad_re = pupil_re * tile_re + pupil_im * tile_im
    grad_im = pupil_re * tile_im - pupil_im * tile_re
    return jnp.stack([grad_re, grad_im], axis=1)

def place_boxes(grads, row_starts, col_starts, height, width):
    anchor = jnp.zeros((), jnp.int32)

    def add_box(number, total):
        corner = (anchor, row_starts[number], col_starts[number])
        current = lax.dynamic_slice(total, corner, grads.shape[1:])
        return lax.dynamic_update_slice(total, current + grads[number], corner)
    return lax.fori_loop(0, grads.shape[0], add_box, jnp.zeros((2, height, width), jnp.float32))

def object_tile(spectrum_tile):
    height = spectrum_tile.shape[1]
    width = spectrum_tile.shape[2]
    rows_re, rows_im = wave_table(height, height)
    cols_re, cols_im = wave_table(width, width)
    partial_field = complex_product('yu,uv->yv', (rows_re, rows_im), (spectrum_tile[0], spectrum_tile[1]))
    return jnp.stack(complex_product('yv,xv->yx', partial_field, (cols_re, cols_im)))

def blend_core(own, left_part, right_part, has_left, has_right, core):
    margin = left_part.shape[-1]
    correlation = 2 * margin
    positions = jnp.arange(margin, dtype=jnp.float32)
    left_own = (positions + margin + 0.5) / correlation
    left_other = (margin - positions - 0.5) / correlation
    right_own = (correlation - positions - 0.5) / correlation
    right_other = (positions + 0.5) / correlation
    middle = own[..., margin:margin + core]
    head = middle[..., :margin] * (left_own * has_left + (1.0 - has_left)) + left_part * (left_other * has_left)
    tail = middle[..., core - margin:] * (right_own * has_right + (1.0 - has_right)) + right_part * (right_other * has_right)
    return jnp.concatenate([head, middle[..., margin:core - margin], tail], axis=-1)

def reference(raw, scales, flat, spectrum, pupil, patterns, led_row, led_col):
    tiles_n = spectrum.shape[0]
    core = TW - OV
    margin = OV // 2
    anchor = jnp.zeros((), jnp.int32)

    def measure(tile_number):
        start = tile_number * core
        codes = lax.dynamic_slice(raw, (anchor, anchor, start), (FRAMES, TH, core)).astype(jnp.float32)
        factors = lax.dynamic_slice(scales, (anchor, anchor, tile_number * (core // BC)), (FRAMES, TH // BR, core // BC)).astype(jnp.float32)
        factors = jnp.repeat(jnp.repeat(factors, BR, axis=1), BC, axis=2)
        gains = lax.dynamic_slice(flat, (anchor, start), (TH, core))
        return remove_tilt(codes * factors * gains[None])
    measured = lax.map(measure, jnp.arange(tiles_n, dtype=jnp.int32))
    blank = jnp.zeros_like(measured[:1, :, :, :margin])
    from_left = jnp.concatenate([blank, measured[:-1, :, :, core - margin:]], axis=0)
    from_right = jnp.concatenate([measured[1:, :, :, :margin], blank], axis=0)
    windows = jnp.concatenate([from_left, measured, from_right], axis=-1)
    lit_ids = patterns.reshape(-1)
    row_starts = led_row[lit_ids].astype(jnp.int32)
    col_starts = led_col[lit_ids].astype(jnp.int32)

    def update(pieces):
        spectrum_tile, window = pieces
        grads = box_gradients(spectrum_tile, window, pupil, row_starts, col_starts, LEDS)
        total = place_boxes(grads, row_starts, col_starts, TH, TW)
        fresh = spectrum_tile - step_size * total
        return (fresh, object_tile(fresh))
    new_spectrum, objects = lax.map(update, (spectrum, windows))
    flags = jnp.arange(tiles_n, dtype=jnp.int32)
    has_left = (flags > 0).astype(jnp.float32)[:, None, None, None]
    has_right = (flags < tiles_n - 1).astype(jnp.float32)[:, None, None, None]
    empty_part = jnp.zeros_like(objects[:1, :, :, :margin])
    left_parts = jnp.concatenate([empty_part, objects[:-1, :, :, TW - margin:]], axis=0)
    right_parts = jnp.concatenate([objects[1:, :, :, :margin], empty_part], axis=0)
    cores = blend_core(objects, left_parts, right_parts, has_left, has_right, core)
    stitched = jnp.transpose(cores, (1, 2, 0, 3)).reshape(2, TH, tiles_n * core)
    return (new_spectrum, stitched)
```

```python
import functools
import math

import jax
import jax.numpy as jnp
import ml_dtypes
import numpy as np
from jax import lax
from jax.experimental import pallas as pl
from jax.experimental.pallas import tpu as pltpu
from jax.sharding import PartitionSpec as P

TH = 256
TW = 512
OV = 32
BR = 4
BC = 32
PR = 64
PC = 128
FR_G = 4
LEDS = 4
HALF = TH // 2
HR = PR // 2
RB = HR + 8
STEP = 0.02
F32 = jnp.float32
BF16 = jnp.bfloat16


def split_np(table):
    hi = table.astype(ml_dtypes.bfloat16)
    lo = (table - hi.astype(np.float64)).astype(ml_dtypes.bfloat16)
    return hi, lo


def wave_np(length, band):
    places = np.arange(length)[:, None]
    freqs = np.arange(band)[None, :] - band // 2
    angle = (places * freqs % length) * (2.0 * np.pi / length)
    return np.cos(angle) / math.sqrt(band), np.sin(angle) / math.sqrt(band)


def band_tables():
    col_re, col_im = (part.T for part in wave_np(TW, PC))
    cols = np.block([[col_re, col_im], [-col_im, col_re]])
    col_hi, col_lo = split_np(cols)
    row_re, row_im = wave_np(TH, PR)
    spread, gather = [], []
    for parity in (0, 1):
        re = row_re[:HALF, parity::2]
        im = row_im[:HALF, parity::2]
        rows_hi, rows_lo = split_np(np.block([[re, -im], [im, re]]))
        spread.append(np.concatenate([rows_hi, rows_hi, rows_lo, rows_lo], axis=1))
        gather.append(np.concatenate([rows_hi.T, rows_lo.T], axis=0))
    return np.stack([col_hi, col_lo]), np.stack(spread), np.stack(gather)


def split(x):
    hi = x.astype(BF16)
    return hi, (x - hi.astype(F32)).astype(BF16)


def dot(a, b):
    return jnp.dot(a, b, preferred_element_type=F32)


def dot_t(a, b):
    return lax.dot_general(a, b, (((1,), (1,)), ((), ())), preferred_element_type=F32)


def box_place(pat, lrow, lcol, frame, j):
    led = pat[frame, j]
    row = lrow[led]
    col = lcol[led]
    offset = col & 127
    lane = pl.multiple_of((col >> 7) * 128, 128)
    return row, offset, lane


def half_rows(row, parity):
    start = (row + parity) >> 1
    return pl.multiple_of((start >> 3) * 8, 8), start & 7, (row + parity) & 1


def load_halves(spec, pup, stage, sp, pd):
    sp[...] = jnp.zeros_like(sp)
    for c in (0, 1):
        for parity in (0, 1):
            for k in range(TW // 128):
                if parity == 0:
                    stage[c, k] = spec[c, :, k * 128 : (k + 1) * 128]
                sp[c, parity, :HALF, k * 128 : (k + 1) * 128] = stage[
                    c, k, pl.ds(parity, HALF, stride=2), :
                ]
            pd[c, parity] = pup[c, pl.ds(parity, HR, stride=2), :]


def forward_frame(frame, pat, lrow, lcol, sp, pd, cols, spread, lit, mid, field):
    for j in range(LEDS):
        row, offset, lane = box_place(pat, lrow, lcol, frame, j)
        back = (256 - offset) & 255
        for parity in (0, 1):
            base, shift, which = half_rows(row, parity)
            up = jnp.where(shift == 0, 0, RB - shift)
            box = [
                pltpu.roll(
                    pltpu.roll(sp[c, which, pl.ds(base, RB), pl.ds(lane, 256)], back, 1)[:, :PC],
                    up,
                    0,
                )[:HR]
                for c in (0, 1)
            ]
            p_re, p_im = pd[0, parity], pd[1, parity]
            rows = pl.ds(j * PR + parity * HR, HR)
            lit[rows, :PC] = p_re * box[0] - p_im * box[1]
            lit[rows, PC:] = p_re * box[1] + p_im * box[0]
    hi, lo = split(lit[...])
    mid[...] = dot(hi, cols[0]) + dot(lo, cols[0]) + dot(hi, cols[1])
    estimate = None
    for j in range(LEDS):
        parts = []
        for parity in (0, 1):
            rows = pl.ds(j * PR + parity * HR, HR)
            re_hi, re_lo = split(mid[rows, :TW])
            im_hi, im_lo = split(mid[rows, TW:])
            both = jnp.concatenate([re_hi, im_hi, re_lo, im_lo], axis=0)
            parts.append(dot(spread[parity], jnp.concatenate([both, both], axis=0)))
        upper = parts[0] + parts[1]
        lower = parts[0] - parts[1]
        field[j, 0, :HALF] = upper[:HALF]
        field[j, 0, HALF:] = lower[:HALF]
        field[j, 1, :HALF] = upper[HALF:]
        field[j, 1, HALF:] = lower[HALF:]
        power = jnp.concatenate(
            [
                upper[:HALF] * upper[:HALF] + upper[HALF:] * upper[HALF:],
                lower[:HALF] * lower[:HALF] + lower[HALF:] * lower[HALF:],
            ],
            axis=0,
        )
        estimate = power if estimate is None else estimate + power
    return estimate


def backward_frame(frame, misfit, pat, lrow, lcol, pd, cols, gather, field, low, acc):
    for j in range(LEDS):
        weighted = [misfit * field[j, c] for c in (0, 1)]
        for parity in (0, 1):
            mix = [
                w[:HALF] + w[HALF:] if parity == 0 else w[:HALF] - w[HALF:] for w in weighted
            ]
            hi, lo = split(jnp.concatenate(mix, axis=0))
            table = gather[parity]
            first = dot(table, hi)
            total = first[:PR] + first[PR:] + dot(table[:PR], lo)
            rows = pl.ds(j * PR + parity * HR, HR)
            low[rows, :TW] = total[:HR]
            low[rows, TW:] = total[HR:]
    hi, lo = split(low[...])
    grads = dot_t(hi, cols[0]) + dot_t(lo, cols[0]) + dot_t(hi, cols[1])
    for j in range(LEDS):
        row, offset, lane = box_place(pat, lrow, lcol, frame, j)
        for parity in (0, 1):
            base, shift, which = half_rows(row, parity)
            first = j * PR + parity * HR
            g_re = grads[first : first + HR, :PC]
            g_im = grads[first : first + HR, PC:]
            p_re, p_im = pd[0, parity], pd[1, parity]
            for c, value in (
                (0, p_re * g_re + p_im * g_im),
                (1, p_re * g_im - p_im * g_re),
            ):
                tall = jnp.concatenate([value, jnp.zeros((RB - HR, PC), F32)], axis=0)
                tall = pltpu.roll(tall, shift, 0)
                wide = jnp.concatenate([tall, jnp.zeros_like(tall)], axis=1)
                place = (c, which, pl.ds(base, RB), pl.ds(lane, 256))
                acc[place] += pltpu.roll(wide, offset, 1)


def gradient_kernel(
    pat, lrow, lcol, spec, pup, win, cols, spread, gather, out, stage, sp, pd, acc, lit, mid, field, low
):
    step = pl.program_id(0)
    frame = lax.axis_index("grp") * FR_G + step

    @pl.when(step == 0)
    def _():
        load_halves(spec, pup, stage, sp, pd)
        acc[...] = jnp.zeros_like(acc)

    estimate = forward_frame(frame, pat, lrow, lcol, sp, pd, cols, spread, lit, mid, field)
    misfit = estimate - win[0]
    backward_frame(frame, misfit, pat, lrow, lcol, pd, cols, gather, field, low, acc)

    @pl.when(step == FR_G - 1)
    def _():
        for c in (0, 1):
            for parity in (0, 1):
                for k in range(TW // 128):
                    stage[c, k, pl.ds(parity, HALF, stride=2), :] = acc[
                        c, parity, :HALF, k * 128 : (k + 1) * 128
                    ]
                    if parity == 1:
                        out[c, :, k * 128 : (k + 1) * 128] = stage[c, k]


def tile_gradient(spectrum, pupil, window, patterns, led_row, led_col):
    cols, spread, gather = (jnp.asarray(t) for t in band_tables())

    def whole(array):
        return pl.BlockSpec(array.shape, lambda s: (0,) * array.ndim)

    smem = pl.BlockSpec(memory_space=pltpu.SMEM)
    return pl.pallas_call(
        gradient_kernel,
        grid=(FR_G,),
        in_specs=[
            smem,
            smem,
            smem,
            whole(spectrum),
            whole(pupil),
            pl.BlockSpec((1, TH, TW), lambda s: (s, 0, 0)),
            whole(cols),
            whole(spread),
            whole(gather),
        ],
        out_specs=pl.BlockSpec((2, TH, TW), lambda s: (0, 0, 0)),
        out_shape=jax.ShapeDtypeStruct((2, TH, TW), F32),
        scratch_shapes=[
            pltpu.VMEM((2, TW // 128, TH, 128), F32),
            pltpu.VMEM((2, 2, HALF + 8, TW + 128), F32),
            pltpu.VMEM((2, 2, HR, PC), F32),
            pltpu.VMEM((2, 2, HALF + 8, TW + 128), F32),
            pltpu.VMEM((LEDS * PR, 2 * PC), F32),
            pltpu.VMEM((LEDS * PR, 2 * TW), F32),
            pltpu.VMEM((LEDS, 2, TH, TW), F32),
            pltpu.VMEM((LEDS * PR, 2 * TW), F32),
        ],
        compiler_params=pltpu.CompilerParams(vmem_limit_bytes=48 * 2**20),
        name="gradient",
    )(patterns, led_row, led_col, spectrum, pupil, window, cols, spread, gather)


highest = lax.Precision.HIGHEST


def padded(block, sides, width):
    for axis, dim in sides:
        count = lax.axis_size(axis)
        forward = [(i, i + 1) for i in range(count - 1)]
        backward = [(target, source) for source, target in forward]
        low = lax.ppermute(
            lax.slice_in_dim(block, block.shape[dim] - width, None, axis=dim), axis, forward
        )
        high = lax.ppermute(lax.slice_in_dim(block, 0, width, axis=dim), axis, backward)
        block = jnp.concatenate([low, block, high], axis=dim)
    return block


def wave_table(length, band):
    places = jnp.arange(length, dtype=jnp.int32)[:, None]
    freqs = jnp.arange(band, dtype=jnp.int32)[None, :] - band // 2
    turns = places * freqs % length
    angle = turns.astype(jnp.float32) * (2.0 * math.pi / length)
    factor = 1.0 / math.sqrt(band)
    return (jnp.cos(angle) * factor, jnp.sin(angle) * factor)


def complex_product(form, left_pair, right_pair):
    left_re, left_im = left_pair
    right_re, right_im = right_pair

    def einsum_pair(first, second):
        return jnp.einsum(form, first, second, precision=highest)

    return (
        einsum_pair(left_re, right_re) - einsum_pair(left_im, right_im),
        einsum_pair(left_re, right_im) + einsum_pair(left_im, right_re),
    )


def remove_tilt(flattened):
    rows_n = flattened.shape[1]
    cols_n = flattened.shape[2]
    ycentre = jnp.arange(rows_n, dtype=jnp.float32) - (rows_n - 1) / 2.0
    xcentre = jnp.arange(cols_n, dtype=jnp.float32) - (cols_n - 1) / 2.0
    slope_y = jnp.sum(flattened * ycentre[None, :, None], axis=(1, 2)) / (
        jnp.sum(ycentre * ycentre) * cols_n
    )
    slope_x = jnp.sum(flattened * xcentre[None, None, :], axis=(1, 2)) / (
        jnp.sum(xcentre * xcentre) * rows_n
    )
    return (
        flattened
        - slope_y[:, None, None] * ycentre[None, :, None]
        - slope_x[:, None, None] * xcentre[None, None, :]
    )


def object_tile(spectrum_tile):
    height = spectrum_tile.shape[1]
    width = spectrum_tile.shape[2]
    rows_re, rows_im = wave_table(height, height)
    cols_re, cols_im = wave_table(width, width)
    partial_field = complex_product(
        "yu,uv->yv", (rows_re, rows_im), (spectrum_tile[0], spectrum_tile[1])
    )
    return jnp.stack(complex_product("yv,xv->yx", partial_field, (cols_re, cols_im)))


def blend_core(own, left_part, right_part, has_left, has_right, core):
    margin = left_part.shape[-1]
    correlation = 2 * margin
    positions = jnp.arange(margin, dtype=jnp.float32)
    left_own = (positions + margin + 0.5) / correlation
    left_other = (margin - positions - 0.5) / correlation
    right_own = (correlation - positions - 0.5) / correlation
    right_other = (positions + 0.5) / correlation
    middle = own[..., margin : margin + core]
    head = middle[..., :margin] * (left_own * has_left + (1.0 - has_left)) + left_part * (
        left_other * has_left
    )
    tail = middle[..., core - margin :] * (
        right_own * has_right + (1.0 - has_right)
    ) + right_part * (right_other * has_right)
    return jnp.concatenate([head, middle[..., margin : core - margin], tail], axis=-1)


def spread_factors(coarse):
    return jnp.repeat(jnp.repeat(coarse.astype(jnp.float32), BR, axis=1), BC, axis=2)


def body(raw, scales, flat, spectrum, pupil, patterns, led_row, led_col):
    core = TW - OV
    margin = OV // 2
    tile_count = lax.axis_size("tile")
    tile_number = lax.axis_index("tile")
    rows_here = raw.shape[1]
    frames_here = raw.shape[0]
    dequant = raw.astype(jnp.float32) * spread_factors(scales)
    value_blocks = dequant.reshape(frames_here, rows_here, tile_count, core)
    arrived = lax.all_to_all(
        value_blocks.astype(jnp.bfloat16), "tile", split_axis=2, concat_axis=1, tiled=True
    ).astype(value_blocks.dtype)
    values = arrived.reshape(frames_here, TH, arrived.shape[-1])
    measured = remove_tilt(values * flat[None])
    window = padded(measured.astype(jnp.bfloat16), (("tile", 2),), margin).astype(measured.dtype)
    spectrum_tile = spectrum[0]
    local_total = tile_gradient(spectrum_tile, pupil, window, patterns, led_row, led_col)
    total = lax.psum(local_total, "grp")
    fresh = spectrum_tile - STEP * total
    image = object_tile(fresh)
    extended = padded(image, (("tile", 2),), margin)
    has_left = (tile_number > 0).astype(jnp.float32)
    has_right = (tile_number < tile_count - 1).astype(jnp.float32)
    stitched = blend_core(
        image, extended[..., :margin], extended[..., margin + TW :], has_left, has_right, core
    )
    return (fresh[None], stitched)


def solution(mesh):
    return jax.shard_map(
        body,
        mesh=mesh,
        in_specs=(
            P("grp", "tile", None),
            P("grp", "tile", None),
            P(None, "tile"),
            P("tile", None, None, None),
            P(),
            P(),
            P(),
            P(),
        ),
        out_specs=(P("tile", None, None, None), P(None, None, "tile")),
        check_vma=False,
    )
```

```python
import functools
import math

import jax
import jax.numpy as jnp
import ml_dtypes
import numpy as np
from jax import lax
from jax.experimental import pallas as pl
from jax.experimental.pallas import tpu as pltpu
from jax.sharding import PartitionSpec as P

TH = 256
TW = 512
OV = 32
BR = 4
BC = 32
PR = 64
PC = 128
FR_G = 4
LEDS = 4
HALF = TH // 2
HR = PR // 2
MARGIN = OV // 2
CORE = TW - OV
LANES = 128
BLOCKS = TW // LANES
MESH = pl.DeviceIdType.MESH
RB = HR + 8
STEP = 0.02
F32 = jnp.float32
BF16 = jnp.bfloat16


def split_np(table):
    hi = table.astype(ml_dtypes.bfloat16)
    lo = (table - hi.astype(np.float64)).astype(ml_dtypes.bfloat16)
    return hi, lo


def wave_np(length, band):
    places = np.arange(length)[:, None]
    freqs = np.arange(band)[None, :] - band // 2
    angle = (places * freqs % length) * (2.0 * np.pi / length)
    return np.cos(angle) / math.sqrt(band), np.sin(angle) / math.sqrt(band)


def object_tables():
    re, im = wave_np(TH, TH)
    rows = []
    for parity in (0, 1):
        a, b = re[:HALF, parity::2], im[:HALF, parity::2]
        rows.append(np.stack(split_np(np.block([[a, -b], [b, a]]))))
    re, im = (np.roll(part.T, -MARGIN, axis=1)[:TH] for part in wave_np(TW, TW))
    cols = np.stack([np.stack(split_np(re)), np.stack(split_np(im))], axis=1)
    return np.stack(rows), cols


def band_tables():
    col_re, col_im = (np.roll(part.T, -MARGIN, axis=1) for part in wave_np(TW, PC))
    cols = np.block([[col_re, col_im], [-col_im, col_re]])
    col_hi, col_lo = split_np(cols)
    row_re, row_im = wave_np(TH, PR)
    spread, gather = [], []
    for parity in (0, 1):
        re = row_re[:HALF, parity::2]
        im = row_im[:HALF, parity::2]
        rows_hi, rows_lo = split_np(np.block([[re, -im], [im, re]]))
        spread.append(np.concatenate([rows_hi, rows_hi, rows_lo, rows_lo], axis=1))
        gather.append(np.concatenate([rows_hi.T, rows_lo.T], axis=0))
    return np.stack([col_hi, col_lo]), np.stack(spread), np.stack(gather)


def split(x):
    hi = x.astype(BF16)
    return hi, (x - hi.astype(F32)).astype(BF16)


def dot(a, b):
    return jnp.dot(a, b, preferred_element_type=F32)


def dot_t(a, b):
    return lax.dot_general(a, b, (((1,), (1,)), ((), ())), preferred_element_type=F32)


def box_place(pat, lrow, lcol, frame, j):
    led = pat[frame, j]
    row = lrow[led]
    col = lcol[led]
    offset = col & 127
    lane = pl.multiple_of((col >> 7) * 128, 128)
    return row, offset, lane


def half_rows(row, parity):
    start = (row + parity) >> 1
    return pl.multiple_of((start >> 3) * 8, 8), start & 7, (row + parity) & 1


def load_halves(spec, pup, stage, sp, pd):
    sp[...] = jnp.zeros_like(sp)
    for c in (0, 1):
        for parity in (0, 1):
            for k in range(TW // 128):
                if parity == 0:
                    stage[c, k] = spec[c, :, k * 128 : (k + 1) * 128]
                sp[c, parity, :HALF, k * 128 : (k + 1) * 128] = stage[
                    c, k, pl.ds(parity, HALF, stride=2), :
                ]
            pd[c, parity] = pup[c, pl.ds(parity, HR, stride=2), :]


def forward_frame(frame, pat, lrow, lcol, sp, pd, cols, spread, lit, mid, field):
    for j in range(LEDS):
        row, offset, lane = box_place(pat, lrow, lcol, frame, j)
        back = (256 - offset) & 255
        for parity in (0, 1):
            base, shift, which = half_rows(row, parity)
            up = jnp.where(shift == 0, 0, RB - shift)
            box = [
                pltpu.roll(
                    pltpu.roll(sp[c, which, pl.ds(base, RB), pl.ds(lane, 256)], back, 1)[:, :PC],
                    up,
                    0,
                )[:HR]
                for c in (0, 1)
            ]
            p_re, p_im = pd[0, parity], pd[1, parity]
            rows = pl.ds(j * PR + parity * HR, HR)
            lit[rows, :PC] = p_re * box[0] - p_im * box[1]
            lit[rows, PC:] = p_re * box[1] + p_im * box[0]
    hi, lo = split(lit[...])
    mid[...] = dot(hi, cols[0]) + dot(lo, cols[0]) + dot(hi, cols[1])
    estimate = None
    for j in range(LEDS):
        parts = []
        for parity in (0, 1):
            rows = pl.ds(j * PR + parity * HR, HR)
            re_hi, re_lo = split(mid[rows, :TW])
            im_hi, im_lo = split(mid[rows, TW:])
            both = jnp.concatenate([re_hi, im_hi, re_lo, im_lo], axis=0)
            parts.append(dot(spread[parity], jnp.concatenate([both, both], axis=0)))
        upper = parts[0] + parts[1]
        lower = parts[0] - parts[1]
        field[j, 0, :HALF] = upper[:HALF]
        field[j, 0, HALF:] = lower[:HALF]
        field[j, 1, :HALF] = upper[HALF:]
        field[j, 1, HALF:] = lower[HALF:]
        power = jnp.concatenate(
            [
                upper[:HALF] * upper[:HALF] + upper[HALF:] * upper[HALF:],
                lower[:HALF] * lower[:HALF] + lower[HALF:] * lower[HALF:],
            ],
            axis=0,
        )
        estimate = power if estimate is None else estimate + power
    return estimate


def backward_frame(frame, misfit, pat, lrow, lcol, pd, cols, gather, field, low, acc):
    for j in range(LEDS):
        weighted = [misfit * field[j, c] for c in (0, 1)]
        for parity in (0, 1):
            mix = [
                w[:HALF] + w[HALF:] if parity == 0 else w[:HALF] - w[HALF:] for w in weighted
            ]
            hi, lo = split(jnp.concatenate(mix, axis=0))
            table = gather[parity]
            first = dot(table, hi)
            total = first[:PR] + first[PR:] + dot(table[:PR], lo)
            rows = pl.ds(j * PR + parity * HR, HR)
            low[rows, :TW] = total[:HR]
            low[rows, TW:] = total[HR:]
    hi, lo = split(low[...])
    grads = dot_t(hi, cols[0]) + dot_t(lo, cols[0]) + dot_t(hi, cols[1])
    for j in range(LEDS):
        row, offset, lane = box_place(pat, lrow, lcol, frame, j)
        for parity in (0, 1):
            base, shift, which = half_rows(row, parity)
            first = j * PR + parity * HR
            g_re = grads[first : first + HR, :PC]
            g_im = grads[first : first + HR, PC:]
            p_re, p_im = pd[0, parity], pd[1, parity]
            for c, value in (
                (0, p_re * g_re + p_im * g_im),
                (1, p_re * g_im - p_im * g_re),
            ):
                tall = jnp.concatenate([value, jnp.zeros((RB - HR, PC), F32)], axis=0)
                tall = pltpu.roll(tall, shift, 0)
                wide = jnp.concatenate([tall, jnp.zeros_like(tall)], axis=1)
                place = (c, which, pl.ds(base, RB), pl.ds(lane, 256))
                acc[place] += pltpu.roll(wide, offset, 1)


def gradient_kernel(
    pat, lrow, lcol, spec, pup, win, cols, spread, gather, out, stage, sp, pd, acc, lit, mid, field, low
):
    step = pl.program_id(0)
    frame = lax.axis_index("grp") * FR_G + step

    @pl.when(step == 0)
    def _():
        load_halves(spec, pup, stage, sp, pd)
        acc[...] = jnp.zeros_like(acc)

    estimate = forward_frame(frame, pat, lrow, lcol, sp, pd, cols, spread, lit, mid, field)
    misfit = estimate - win[0]
    backward_frame(frame, misfit, pat, lrow, lcol, pd, cols, gather, field, low, acc)

    @pl.when(step == FR_G - 1)
    def _():
        for c in (0, 1):
            for parity in (0, 1):
                for k in range(TW // 128):
                    out[k, c, pl.ds(parity, HALF, stride=2), :] = acc[
                        c, parity, :HALF, k * 128 : (k + 1) * 128
                    ]


def tile_gradient(spectrum, pupil, window, patterns, led_row, led_col):
    cols, spread, gather = (jnp.asarray(t) for t in band_tables())

    def whole(array):
        return pl.BlockSpec(array.shape, lambda s: (0,) * array.ndim)

    smem = pl.BlockSpec(memory_space=pltpu.SMEM)
    return pl.pallas_call(
        gradient_kernel,
        grid=(FR_G,),
        in_specs=[
            smem,
            smem,
            smem,
            whole(spectrum),
            whole(pupil),
            pl.BlockSpec((1, TH, TW), lambda s: (s, 0, 0)),
            whole(cols),
            whole(spread),
            whole(gather),
        ],
        out_specs=pl.BlockSpec((BLOCKS, 2, TH, LANES), lambda s: (0, 0, 0, 0)),
        out_shape=jax.ShapeDtypeStruct((BLOCKS, 2, TH, LANES), F32),
        scratch_shapes=[
            pltpu.VMEM((2, TW // 128, TH, 128), F32),
            pltpu.VMEM((2, 2, HALF + 8, TW + 128), F32),
            pltpu.VMEM((2, 2, HR, PC), F32),
            pltpu.VMEM((2, 2, HALF + 8, TW + 128), F32),
            pltpu.VMEM((LEDS * PR, 2 * PC), F32),
            pltpu.VMEM((LEDS * PR, 2 * TW), F32),
            pltpu.VMEM((LEDS, 2, TH, TW), F32),
            pltpu.VMEM((LEDS * PR, 2 * TW), F32),
        ],
        compiler_params=pltpu.CompilerParams(vmem_limit_bytes=48 * 2**20),
        name="gradient",
    )(patterns, led_row, led_col, spectrum, pupil, window, cols, spread, gather)


def build_columns(half, table):
    lane = lax.broadcasted_iota(jnp.int32, (1, TW), 1)
    sign = (1 - 2 * (lane & 1)).astype(F32)
    for i in (0, 1):
        rows = pl.ds(i * LANES, LANES)
        for h in (0, 1):
            re = half[h, 0, rows, :].astype(F32)
            im = half[h, 1, rows, :].astype(F32)
            for n, factor in ((0, None), (1, sign)):
                a = re if factor is None else re * factor
                b = im if factor is None else im * factor
                upper = pl.ds(n * LANES, LANES)
                lower = pl.ds((2 + n) * LANES, LANES)
                for k in range(BLOCKS):
                    cut = slice(k * LANES, (k + 1) * LANES)
                    table[i, h, k, upper, :LANES] = a[:, cut].astype(BF16)
                    table[i, h, k, upper, LANES:] = b[:, cut].astype(BF16)
                    table[i, h, k, lower, :LANES] = (-b[:, cut]).astype(BF16)
                    table[i, h, k, lower, LANES:] = a[:, cut].astype(BF16)


def object_rows(i, new, rows_table, lhs):
    parts = []
    for parity in (0, 1):
        data = [
            jnp.concatenate(
                [new[k, c, pl.ds(parity, HALF, stride=2), :] for k in (i, i + 2)], axis=1
            )
            for c in (0, 1)
        ]
        hi, lo = split(jnp.concatenate(data, axis=0))
        t_hi, t_lo = rows_table[parity, 0], rows_table[parity, 1]
        parts.append(dot(t_hi, hi) + dot(t_hi, lo) + dot(t_lo, hi))
    for n, value in enumerate((parts[0] + parts[1], parts[0] - parts[1])):
        hi, lo = split(value)
        rows = pl.ds(n * HALF, HALF)
        for h, part in enumerate((hi, lo)):
            lhs[h, rows, : 2 * LANES] = part[:HALF]
            lhs[h, rows, 2 * LANES :] = part[HALF:]


def object_block(i, k, lhs, table):
    hi, lo = lhs[0], lhs[1]
    return dot(hi, table[i, 0, k]) + dot(lo, table[i, 0, k]) + dot(hi, table[i, 1, k])


def pack_edge(value, first):
    lane = lax.broadcasted_iota(jnp.int32, (TH // 8, LANES), 1) // MARGIN
    packed = jnp.zeros((TH // 8, LANES), F32)
    for b in range(8):
        piece = value[b * 32 : (b + 1) * 32]
        piece = pltpu.roll(piece, (MARGIN * b - first) % LANES, 1)
        packed = jnp.where(lane == b, piece, packed)
    return packed


def unpack_edge(packed, first):
    return jnp.concatenate(
        [pltpu.roll(packed, (first - MARGIN * b) % LANES, 1) for b in range(8)], axis=0
    )


def finish_kernel(
    tiles,
    grad,
    spec,
    rows_table,
    half,
    fresh,
    stitched,
    got,
    pair,
    far,
    new,
    table,
    lhs,
    image,
    edge_out,
    edge_in,
    send,
    recv,
):
    group = lax.axis_index("grp")
    tile = lax.axis_index("tile")
    core = lax.rem(group, 2)
    mate = {"grp": group + 1 - 2 * core}
    partner = {"grp": group + 2 - 4 * lax.div(group, 2)}
    right = {"tile": lax.rem(tile + 1, tiles)}
    left = {"tile": lax.rem(tile + tiles - 1, tiles)}

    def remote(number, src, dst, device):
        return pltpu.make_async_remote_copy(
            src_ref=src,
            dst_ref=dst,
            send_sem=send.at[number],
            recv_sem=recv.at[number],
            device_id=device,
            device_id_type=MESH,
        )

    barrier = pltpu.get_barrier_semaphore()
    for device in (mate, partner, left, right):
        pl.semaphore_signal(barrier, inc=1, device_id=device, device_id_type=MESH)
    pl.semaphore_wait(barrier, 4)

    first = [remote(i, grad.at[2 - 2 * core + i], got.at[i], mate) for i in (0, 1)]
    for copy in first:
        copy.start()
    second = []
    for i in (0, 1):
        first[i].wait_recv()
        pair[i] = grad[2 * core + i] + got[i]
        second.append(remote(2 + i, pair.at[i], far.at[i], partner))
        second[i].start()
    build_columns(half, table)
    third = []
    for i in (0, 1):
        second[i].wait_recv()
        mine = 2 * core + i
        lanes = pl.ds(pl.multiple_of(mine * LANES, LANES), LANES)
        new[mine] = spec[:, :, lanes] - STEP * (pair[i] + far[i])
        third.append(remote(4 + i, new.at[mine], new.at[mine], mate))
        third[i].start()
        third[i].wait_recv()
        for k in (i, i + 2):
            fresh[:, :, k * LANES : (k + 1) * LANES] = new[k]
        object_rows(i, new, rows_table, lhs)
        if i == 0:
            for k in range(BLOCKS):
                image[k] = object_block(i, k, lhs, table)
    image[3] += object_block(1, 3, lhs, table)
    for c in (0, 1):
        value = image[3, :, c * LANES : (c + 1) * LANES]
        edge_out[0, c] = pack_edge(value, 96)
        edge_out[1, c] = pack_edge(value, 112)
    edges = [
        remote(6, edge_out.at[0], edge_in.at[0], right),
        remote(7, edge_out.at[1], edge_in.at[1], left),
    ]
    for copy in edges:
        copy.start()
    for k in range(BLOCKS - 1):
        image[k] += object_block(1, k, lhs, table)
    for c in (0, 1):
        for k in (1, 2):
            stitched[c, :, k * LANES : (k + 1) * LANES] = image[k, :, c * LANES : (c + 1) * LANES]
    lane = lax.broadcasted_iota(jnp.int32, (1, LANES), 1)
    place = lane.astype(F32)
    at_head = (lane < MARGIN) & (tile > 0)
    at_tail = (lane >= 80) & (lane < 96) & (tile < tiles - 1)
    for copy in edges:
        copy.wait_recv()
    for c in (0, 1):
        own = image[0, :, c * LANES : (c + 1) * LANES]
        other = unpack_edge(edge_in[0, c], 0)
        blend = own * ((place + 16.5) / OV) + other * ((15.5 - place) / OV)
        stitched[c, :, :LANES] = jnp.where(at_head, blend, own)
        own = image[3, :, c * LANES : (c + 1) * LANES]
        other = unpack_edge(edge_in[1, c], 80)
        blend = own * ((111.5 - place) / OV) + other * ((place - 79.5) / OV)
        stitched[c, :, 3 * LANES :] = jnp.where(at_tail, blend, own)[:, : CORE - 3 * LANES]
    for copy in first + second + third + edges:
        copy.wait_send()


def finish(grad, spectrum):
    rows_table, half = (jnp.asarray(t) for t in object_tables())
    vmem = pl.BlockSpec(memory_space=pltpu.VMEM)
    part = (2, TH, LANES)
    return pl.pallas_call(
        functools.partial(finish_kernel, lax.axis_size("tile")),
        in_specs=[vmem] * 4,
        out_specs=[vmem] * 2,
        out_shape=[
            jax.ShapeDtypeStruct((2, TH, TW), F32),
            jax.ShapeDtypeStruct((2, TH, CORE), F32),
        ],
        scratch_shapes=[
            pltpu.VMEM((2,) + part, F32),
            pltpu.VMEM((2,) + part, F32),
            pltpu.VMEM((2,) + part, F32),
            pltpu.VMEM((BLOCKS,) + part, F32),
            pltpu.VMEM((2, 2, BLOCKS, TW, 2 * LANES), BF16),
            pltpu.VMEM((2, TH, TW), BF16),
            pltpu.VMEM((BLOCKS, TH, 2 * LANES), F32),
            pltpu.VMEM((2, 2, TH // 8, LANES), F32),
            pltpu.VMEM((2, 2, TH // 8, LANES), F32),
            pltpu.SemaphoreType.DMA((8,)),
            pltpu.SemaphoreType.DMA((8,)),
        ],
        compiler_params=pltpu.CompilerParams(
            collective_id=1, has_side_effects=True, vmem_limit_bytes=48 * 2**20
        ),
        name="finish",
    )(grad, spectrum, rows_table, half)


def padded(block, sides, width):
    for axis, dim in sides:
        count = lax.axis_size(axis)
        forward = [(i, i + 1) for i in range(count - 1)]
        backward = [(target, source) for source, target in forward]
        low = lax.ppermute(
            lax.slice_in_dim(block, block.shape[dim] - width, None, axis=dim), axis, forward
        )
        high = lax.ppermute(lax.slice_in_dim(block, 0, width, axis=dim), axis, backward)
        block = jnp.concatenate([low, block, high], axis=dim)
    return block


def remove_tilt(flattened):
    rows_n = flattened.shape[1]
    cols_n = flattened.shape[2]
    ycentre = jnp.arange(rows_n, dtype=jnp.float32) - (rows_n - 1) / 2.0
    xcentre = jnp.arange(cols_n, dtype=jnp.float32) - (cols_n - 1) / 2.0
    slope_y = jnp.sum(flattened * ycentre[None, :, None], axis=(1, 2)) / (
        jnp.sum(ycentre * ycentre) * cols_n
    )
    slope_x = jnp.sum(flattened * xcentre[None, None, :], axis=(1, 2)) / (
        jnp.sum(xcentre * xcentre) * rows_n
    )
    return (
        flattened
        - slope_y[:, None, None] * ycentre[None, :, None]
        - slope_x[:, None, None] * xcentre[None, None, :]
    )


def spread_factors(coarse):
    return jnp.repeat(jnp.repeat(coarse.astype(jnp.float32), BR, axis=1), BC, axis=2)


def body(raw, scales, flat, spectrum, pupil, patterns, led_row, led_col):
    core = TW - OV
    margin = OV // 2
    tile_count = lax.axis_size("tile")
    rows_here = raw.shape[1]
    frames_here = raw.shape[0]
    dequant = raw.astype(jnp.float32) * spread_factors(scales)
    value_blocks = dequant.reshape(frames_here, rows_here, tile_count, core)
    arrived = lax.all_to_all(
        value_blocks.astype(jnp.bfloat16), "tile", split_axis=2, concat_axis=1, tiled=True
    ).astype(value_blocks.dtype)
    values = arrived.reshape(frames_here, TH, arrived.shape[-1])
    measured = remove_tilt(values * flat[None])
    window = padded(measured.astype(jnp.bfloat16), (("tile", 2),), margin).astype(measured.dtype)
    spectrum_tile = spectrum[0]
    window = jnp.roll(window, -margin, axis=2)
    local_total = tile_gradient(spectrum_tile, pupil, window, patterns, led_row, led_col)
    fresh, stitched = finish(local_total, spectrum_tile)
    return (fresh[None], stitched)


def solution(mesh):
    return jax.shard_map(
        body,
        mesh=mesh,
        in_specs=(
            P("grp", "tile", None),
            P("grp", "tile", None),
            P(None, "tile"),
            P("tile", None, None, None),
            P(),
            P(),
            P(),
            P(),
        ),
        out_specs=(P("tile", None, None, None), P(None, None, "tile")),
        check_vma=False,
    )
```

```python
import functools
import math

import jax
import jax.numpy as jnp
import ml_dtypes
import numpy as np
from jax import lax
from jax.experimental import pallas as pl
from jax.experimental.pallas import tpu as pltpu
from jax.sharding import PartitionSpec as P

TH = 256
TW = 512
OV = 32
BR = 4
BC = 32
PR = 64
PC = 128
FR_G = 4
LEDS = 4
HALF = TH // 2
HR = PR // 2
MARGIN = OV // 2
CORE = TW - OV
LANES = 128
BLOCKS = TW // LANES
MESH = pl.DeviceIdType.MESH
RB = HR + 8
STEP = 0.02
F32 = jnp.float32
BF16 = jnp.bfloat16


def split_np(table):
    hi = table.astype(ml_dtypes.bfloat16)
    lo = (table - hi.astype(np.float64)).astype(ml_dtypes.bfloat16)
    return hi, lo


def wave_np(length, band):
    places = np.arange(length)[:, None]
    freqs = np.arange(band)[None, :] - band // 2
    angle = (places * freqs % length) * (2.0 * np.pi / length)
    return np.cos(angle) / math.sqrt(band), np.sin(angle) / math.sqrt(band)


def object_tables():
    re, im = wave_np(TH, TH)
    rows = []
    for parity in (0, 1):
        a, b = re[:HALF, parity::2], im[:HALF, parity::2]
        rows.append(np.stack(split_np(np.block([[a, -b], [b, a]]))))
    re, im = (np.roll(part.T, -MARGIN, axis=1)[:TH] for part in wave_np(TW, TW))
    cols = np.stack([np.stack(split_np(re)), np.stack(split_np(im))], axis=1)
    return np.stack(rows), cols


def band_tables():
    col_re, col_im = (np.roll(part.T, -MARGIN, axis=1) for part in wave_np(TW, PC))
    cols = np.block([[col_re, col_im], [-col_im, col_re]])
    col_hi, col_lo = split_np(cols)
    row_re, row_im = wave_np(TH, PR)
    spread, gather = [], []
    for parity in (0, 1):
        re = row_re[:HALF, parity::2]
        im = row_im[:HALF, parity::2]
        rows_hi, rows_lo = split_np(np.block([[re, -im], [im, re]]))
        spread.append(np.concatenate([rows_hi, rows_hi, rows_lo, rows_lo], axis=1))
        gather.append(np.concatenate([rows_hi.T, rows_lo.T], axis=0))
    return np.stack([col_hi, col_lo]), np.stack(spread), np.stack(gather)


def split(x):
    hi = x.astype(BF16)
    return hi, (x - hi.astype(F32)).astype(BF16)


def dot(a, b):
    return jnp.dot(a, b, preferred_element_type=F32)


def dot_t(a, b):
    return lax.dot_general(a, b, (((1,), (1,)), ((), ())), preferred_element_type=F32)


def box_place(pat, lrow, lcol, frame, j):
    led = pat[frame, j]
    row = lrow[led]
    col = lcol[led]
    offset = col & 127
    lane = pl.multiple_of((col >> 7) * 128, 128)
    return row, offset, lane


def half_rows(row, parity):
    start = (row + parity) >> 1
    return pl.multiple_of((start >> 3) * 8, 8), start & 7, (row + parity) & 1


def load_halves(spec, pup, stage, sp, pd):
    sp[...] = jnp.zeros_like(sp)
    for c in (0, 1):
        for parity in (0, 1):
            for k in range(TW // 128):
                if parity == 0:
                    stage[c, k] = spec[c, :, k * 128 : (k + 1) * 128]
                sp[c, parity, :HALF, k * 128 : (k + 1) * 128] = stage[
                    c, k, pl.ds(parity, HALF, stride=2), :
                ]
            pd[c, parity] = pup[c, pl.ds(parity, HR, stride=2), :]


def forward_frame(frame, pat, lrow, lcol, sp, pd, cols, spread, lit, mid, field):
    for j in range(LEDS):
        row, offset, lane = box_place(pat, lrow, lcol, frame, j)
        back = (256 - offset) & 255
        for parity in (0, 1):
            base, shift, which = half_rows(row, parity)
            up = jnp.where(shift == 0, 0, RB - shift)
            box = [
                pltpu.roll(
                    pltpu.roll(sp[c, which, pl.ds(base, RB), pl.ds(lane, 256)], back, 1)[:, :PC],
                    up,
                    0,
                )[:HR]
                for c in (0, 1)
            ]
            p_re, p_im = pd[0, parity], pd[1, parity]
            rows = pl.ds(j * PR + parity * HR, HR)
            lit[rows, :PC] = p_re * box[0] - p_im * box[1]
            lit[rows, PC:] = p_re * box[1] + p_im * box[0]
    hi, lo = split(lit[...])
    mid[...] = dot(hi, cols[0]) + dot(lo, cols[0]) + dot(hi, cols[1])
    estimate = None
    for j in range(LEDS):
        parts = []
        for parity in (0, 1):
            rows = pl.ds(j * PR + parity * HR, HR)
            re_hi, re_lo = split(mid[rows, :TW])
            im_hi, im_lo = split(mid[rows, TW:])
            both = jnp.concatenate([re_hi, im_hi, re_lo, im_lo], axis=0)
            parts.append(dot(spread[parity], jnp.concatenate([both, both], axis=0)))
        upper = parts[0] + parts[1]
        lower = parts[0] - parts[1]
        field[j, 0, :HALF] = upper[:HALF]
        field[j, 0, HALF:] = lower[:HALF]
        field[j, 1, :HALF] = upper[HALF:]
        field[j, 1, HALF:] = lower[HALF:]
        power = jnp.concatenate(
            [
                upper[:HALF] * upper[:HALF] + upper[HALF:] * upper[HALF:],
                lower[:HALF] * lower[:HALF] + lower[HALF:] * lower[HALF:],
            ],
            axis=0,
        )
        estimate = power if estimate is None else estimate + power
    return estimate


def backward_frame(frame, misfit, pat, lrow, lcol, pd, cols, gather, field, low, acc):
    for j in range(LEDS):
        weighted = [misfit * field[j, c] for c in (0, 1)]
        for parity in (0, 1):
            mix = [
                w[:HALF] + w[HALF:] if parity == 0 else w[:HALF] - w[HALF:] for w in weighted
            ]
            hi, lo = split(jnp.concatenate(mix, axis=0))
            table = gather[parity]
            first = dot(table, hi)
            total = first[:PR] + first[PR:] + dot(table[:PR], lo)
            rows = pl.ds(j * PR + parity * HR, HR)
            low[rows, :TW] = total[:HR]
            low[rows, TW:] = total[HR:]
    hi, lo = split(low[...])
    grads = dot_t(hi, cols[0]) + dot_t(lo, cols[0]) + dot_t(hi, cols[1])
    for j in range(LEDS):
        row, offset, lane = box_place(pat, lrow, lcol, frame, j)
        for parity in (0, 1):
            base, shift, which = half_rows(row, parity)
            first = j * PR + parity * HR
            g_re = grads[first : first + HR, :PC]
            g_im = grads[first : first + HR, PC:]
            p_re, p_im = pd[0, parity], pd[1, parity]
            for c, value in (
                (0, p_re * g_re + p_im * g_im),
                (1, p_re * g_im - p_im * g_re),
            ):
                tall = jnp.concatenate([value, jnp.zeros((RB - HR, PC), F32)], axis=0)
                tall = pltpu.roll(tall, shift, 0)
                wide = jnp.concatenate([tall, jnp.zeros_like(tall)], axis=1)
                place = (c, which, pl.ds(base, RB), pl.ds(lane, 256))
                acc[place] += pltpu.roll(wide, offset, 1)


def gradient_kernel(
    pat, lrow, lcol, spec, pup, win, cols, spread, gather, out, stage, sp, pd, acc, lit, mid, field, low
):
    step = pl.program_id(0)
    frame = lax.axis_index("grp") * FR_G + step

    @pl.when(step == 0)
    def _():
        load_halves(spec, pup, stage, sp, pd)
        acc[...] = jnp.zeros_like(acc)

    estimate = forward_frame(frame, pat, lrow, lcol, sp, pd, cols, spread, lit, mid, field)
    misfit = estimate - win[0]
    backward_frame(frame, misfit, pat, lrow, lcol, pd, cols, gather, field, low, acc)

    @pl.when(step == FR_G - 1)
    def _():
        for c in (0, 1):
            for parity in (0, 1):
                for k in range(TW // 128):
                    out[k, c, pl.ds(parity, HALF, stride=2), :] = acc[
                        c, parity, :HALF, k * 128 : (k + 1) * 128
                    ]


def tile_gradient(spectrum, pupil, window, patterns, led_row, led_col):
    cols, spread, gather = (jnp.asarray(t) for t in band_tables())

    def whole(array):
        return pl.BlockSpec(array.shape, lambda s: (0,) * array.ndim)

    smem = pl.BlockSpec(memory_space=pltpu.SMEM)
    return pl.pallas_call(
        gradient_kernel,
        grid=(FR_G,),
        in_specs=[
            smem,
            smem,
            smem,
            whole(spectrum),
            whole(pupil),
            pl.BlockSpec((1, TH, TW), lambda s: (s, 0, 0)),
            whole(cols),
            whole(spread),
            whole(gather),
        ],
        out_specs=pl.BlockSpec((BLOCKS, 2, TH, LANES), lambda s: (0, 0, 0, 0)),
        out_shape=jax.ShapeDtypeStruct((BLOCKS, 2, TH, LANES), F32),
        scratch_shapes=[
            pltpu.VMEM((2, TW // 128, TH, 128), F32),
            pltpu.VMEM((2, 2, HALF + 8, TW + 128), F32),
            pltpu.VMEM((2, 2, HR, PC), F32),
            pltpu.VMEM((2, 2, HALF + 8, TW + 128), F32),
            pltpu.VMEM((LEDS * PR, 2 * PC), F32),
            pltpu.VMEM((LEDS * PR, 2 * TW), F32),
            pltpu.VMEM((LEDS, 2, TH, TW), F32),
            pltpu.VMEM((LEDS * PR, 2 * TW), F32),
        ],
        compiler_params=pltpu.CompilerParams(vmem_limit_bytes=48 * 2**20),
        name="gradient",
    )(patterns, led_row, led_col, spectrum, pupil, window, cols, spread, gather)


def pack_edge(value, first):
    lane = lax.broadcasted_iota(jnp.int32, (TH // 8, LANES), 1) // MARGIN
    packed = jnp.zeros((TH // 8, LANES), F32)
    for b in range(8):
        piece = value[b * 32 : (b + 1) * 32]
        piece = pltpu.roll(piece, (MARGIN * b - first) % LANES, 1)
        packed = jnp.where(lane == b, piece, packed)
    return packed


def unpack_edge(packed, first):
    return jnp.concatenate(
        [pltpu.roll(packed, (first - MARGIN * b) % LANES, 1) for b in range(8)], axis=0
    )


def dequantize(raw, scales, dequant):
    frames, rows, width = raw.shape
    dequant[:, :LANES] = jnp.zeros((frames * rows, LANES), F32)
    dequant[:, LANES + width :] = jnp.zeros((frames * rows, LANES), F32)
    lane = lax.broadcasted_iota(jnp.int32, (rows, LANES), 1) // BC
    upper = lax.broadcasted_iota(jnp.int32, (rows, LANES), 0) < BR
    blocks = scales.shape[2]
    per = LANES // BC
    for first in range(0, blocks, LANES):
        count = min(LANES, blocks - first)
        for f in range(frames):
            pair = scales[f, :, first : first + count].astype(F32)
            if count < LANES:
                pair = jnp.concatenate([pair, jnp.zeros((2, LANES - count), F32)], axis=1)
            factors = jnp.where(
                upper,
                jnp.broadcast_to(pair[0:1], (rows, LANES)),
                jnp.broadcast_to(pair[1:2], (rows, LANES)),
            )
            for k in range(count // per):
                column = (first // per + k) * LANES
                spread = jnp.take_along_axis(factors, lane + per * k, axis=1)
                codes = raw[f, :, column : column + LANES].astype(F32)
                dequant[f * rows : (f + 1) * rows, LANES + column : 2 * LANES + column] = (
                    codes * spread
                )


def cut_message(dequant, tile):
    start = CORE * tile - MARGIN + LANES
    aligned = pl.multiple_of(start // LANES * LANES, LANES)
    offset = start - aligned + MARGIN
    wide = dequant[:, pl.ds(aligned, TW + LANES)]
    wide = pltpu.roll(wide, TW + LANES - offset, 1)
    lane = lax.broadcasted_iota(jnp.int32, (1, LANES), 1)
    last = jnp.where(lane < LANES - MARGIN, wide[:, TW - LANES : TW], wide[:, TW:])
    return jnp.concatenate([wide[:, : TW - LANES], last], axis=1).astype(BF16)


def centred():
    y = lax.broadcasted_iota(jnp.int32, (TH, 1), 0).astype(F32) - (TH - 1) / 2.0
    lane = lax.broadcasted_iota(jnp.int32, (1, TW), 1)
    x = lane.astype(F32) - (CORE - 1) / 2.0
    return y, x, lane


Y_NORM = float(np.sum((np.arange(TH) - (TH - 1) / 2.0) ** 2) * CORE)
X_NORM = float(np.sum((np.arange(CORE) - (CORE - 1) / 2.0) ** 2) * TH)


def measure_kernel(
    tiles,
    raw,
    scales,
    flat,
    window,
    dequant,
    message,
    arrived,
    gains,
    flat_out,
    flat_in,
    slope_out,
    slope_in,
    send,
    recv,
    side_send,
    side_recv,
):
    frames = raw.shape[0]
    rows = raw.shape[1]
    tile = lax.axis_index("tile")
    right = {"tile": lax.rem(tile + 1, tiles)}
    left = {"tile": lax.rem(tile + tiles - 1, tiles)}

    def side(number, src, dst, device):
        return pltpu.make_async_remote_copy(
            src_ref=src,
            dst_ref=dst,
            send_sem=side_send.at[number],
            recv_sem=side_recv.at[number],
            device_id=device,
            device_id_type=MESH,
        )

    def block(source, target):
        return pltpu.make_async_remote_copy(
            src_ref=message.at[target],
            dst_ref=arrived.at[source],
            send_sem=send.at[target],
            recv_sem=recv.at[source],
            device_id={"tile": target},
            device_id_type=MESH,
        )

    barrier = pltpu.get_barrier_semaphore()

    @pl.loop(1, tiles)
    def _(i):
        pl.semaphore_signal(
            barrier, inc=1, device_id={"tile": lax.rem(tile + i, tiles)}, device_id_type=MESH
        )

    dequantize(raw, scales, dequant)
    tail = jnp.concatenate(
        [flat[:, 3 * LANES :], jnp.zeros((TH, TW - CORE), F32)], axis=1
    )
    flat_out[0] = pack_edge(tail, 80)
    flat_out[1] = pack_edge(flat[:, :LANES], 0)
    pl.semaphore_wait(barrier, tiles - 1)

    @pl.loop(1, tiles)
    def _(i):
        target = lax.rem(tile + i, tiles)
        message[target] = cut_message(dequant, target)
        block(tile, target).start()

    arrived[tile] = cut_message(dequant, tile)
    flats = [side(0, flat_out.at[0], flat_in.at[0], right), side(1, flat_out.at[1], flat_in.at[1], left)]
    for copy in flats:
        copy.start()
    y, x, lane = centred()
    edge = lane[:, 3 * LANES :]
    for copy in flats:
        copy.wait_recv()
    gains[:, : 3 * LANES] = flat[:, : 3 * LANES]
    outer = jnp.where(
        edge < CORE + MARGIN, unpack_edge(flat_in[1], 96), unpack_edge(flat_in[0], 112)
    )
    gains[:, 3 * LANES :] = jnp.where(edge < CORE, tail, outer)

    @pl.loop(1, tiles + 1)
    def _(i):
        source = lax.rem(tile + tiles - i, tiles)

        @pl.when(i < tiles)
        def _():
            block(source, tile).wait_recv()

        here = pl.ds(pl.multiple_of(source * rows, rows), rows)
        values = arrived[source].astype(F32)
        for f in range(frames):
            window[f, here, :] = values[f * rows : (f + 1) * rows] * gains[here, :]

    inside = (lane < CORE).astype(F32)
    slopes = []
    for f in range(frames):
        flattened = window[f]
        columns = jnp.sum(flattened, axis=0, keepdims=True)
        tilted = jnp.sum(flattened * y, axis=0, keepdims=True)
        slope_y = jnp.sum(tilted * inside, axis=1, keepdims=True) / Y_NORM
        slope_x = jnp.sum(columns * (x * inside), axis=1, keepdims=True) / X_NORM
        slopes.append((slope_y, slope_x))
        slope_out[f : f + 1] = jnp.broadcast_to(slope_y, (1, LANES))
        slope_out[frames + f : frames + f + 1] = jnp.broadcast_to(slope_x, (1, LANES))
    copies = [side(2, slope_out, slope_in.at[0], right), side(3, slope_out, slope_in.at[1], left)]
    for copy in copies:
        copy.start()
    for f in range(frames):
        slope_y, slope_x = slopes[f]
        for k in range(BLOCKS - 1):
            cut = slice(k * LANES, (k + 1) * LANES)
            window[f, :, cut] = window[f, :, cut] - slope_y * y - slope_x * x[:, cut]
    for copy in copies:
        copy.wait_recv()
    x_edge = x[:, 3 * LANES :]
    own = edge < CORE
    after = edge < CORE + MARGIN
    blank = ((~own) & after & (tile == tiles - 1)) | ((~after) & (tile == 0))
    for f in range(frames):
        slope_y, slope_x = slopes[f]
        row_y = jnp.where(
            own, slope_y, jnp.where(after, slope_in[1, f : f + 1], slope_in[0, f : f + 1])
        )
        row_x = jnp.where(
            own,
            slope_x * x_edge,
            jnp.where(
                after,
                slope_in[1, frames + f : frames + f + 1] * (x_edge - CORE),
                slope_in[0, frames + f : frames + f + 1] * (x_edge - 32.0),
            ),
        )
        value = window[f, :, 3 * LANES :] - row_y * y - row_x
        window[f, :, 3 * LANES :] = jnp.where(blank, 0.0, value)
    for copy in flats + copies:
        copy.wait_send()

    @pl.loop(1, tiles)
    def _(i):
        block(tile, lax.rem(tile + i, tiles)).wait_send()


def measure(raw, scales, flat):
    vmem = pl.BlockSpec(memory_space=pltpu.VMEM)
    tiles = lax.axis_size("tile")
    frames, rows, width = raw.shape
    deep = frames * rows
    small = (TH // 8, LANES)
    return pl.pallas_call(
        functools.partial(measure_kernel, tiles),
        in_specs=[vmem] * 3,
        out_specs=vmem,
        out_shape=jax.ShapeDtypeStruct((frames, TH, TW), F32),
        scratch_shapes=[
            pltpu.VMEM((deep, width + 2 * LANES), F32),
            pltpu.VMEM((tiles, deep, TW), BF16),
            pltpu.VMEM((tiles, deep, TW), BF16),
            pltpu.VMEM((TH, TW), F32),
            pltpu.VMEM((2,) + small, F32),
            pltpu.VMEM((2,) + small, F32),
            pltpu.VMEM((2 * frames, LANES), F32),
            pltpu.VMEM((2, 2 * frames, LANES), F32),
            pltpu.SemaphoreType.DMA((tiles,)),
            pltpu.SemaphoreType.DMA((tiles,)),
            pltpu.SemaphoreType.DMA((4,)),
            pltpu.SemaphoreType.DMA((4,)),
        ],
        compiler_params=pltpu.CompilerParams(
            collective_id=2, has_side_effects=True, vmem_limit_bytes=48 * 2**20
        ),
        name="measure",
    )(raw, scales, flat)


def build_columns(half, table):
    lane = lax.broadcasted_iota(jnp.int32, (1, TW), 1)
    sign = (1 - 2 * (lane & 1)).astype(F32)
    for i in (0, 1):
        rows = pl.ds(i * LANES, LANES)
        for h in (0, 1):
            re = half[h, 0, rows, :].astype(F32)
            im = half[h, 1, rows, :].astype(F32)
            for n, factor in ((0, None), (1, sign)):
                a = re if factor is None else re * factor
                b = im if factor is None else im * factor
                upper = pl.ds(n * LANES, LANES)
                lower = pl.ds((2 + n) * LANES, LANES)
                for k in range(BLOCKS):
                    cut = slice(k * LANES, (k + 1) * LANES)
                    table[i, h, k, upper, :LANES] = a[:, cut].astype(BF16)
                    table[i, h, k, upper, LANES:] = b[:, cut].astype(BF16)
                    table[i, h, k, lower, :LANES] = (-b[:, cut]).astype(BF16)
                    table[i, h, k, lower, LANES:] = a[:, cut].astype(BF16)


def object_rows(i, new, rows_table, lhs):
    parts = []
    for parity in (0, 1):
        data = [
            jnp.concatenate(
                [new[k, c, pl.ds(parity, HALF, stride=2), :] for k in (i, i + 2)], axis=1
            )
            for c in (0, 1)
        ]
        hi, lo = split(jnp.concatenate(data, axis=0))
        t_hi, t_lo = rows_table[parity, 0], rows_table[parity, 1]
        parts.append(dot(t_hi, hi) + dot(t_hi, lo) + dot(t_lo, hi))
    for n, value in enumerate((parts[0] + parts[1], parts[0] - parts[1])):
        hi, lo = split(value)
        rows = pl.ds(n * HALF, HALF)
        for h, part in enumerate((hi, lo)):
            lhs[h, rows, : 2 * LANES] = part[:HALF]
            lhs[h, rows, 2 * LANES :] = part[HALF:]


def object_block(i, k, lhs, table):
    hi, lo = lhs[0], lhs[1]
    return dot(hi, table[i, 0, k]) + dot(lo, table[i, 0, k]) + dot(hi, table[i, 1, k])


def finish_kernel(
    tiles,
    grad,
    spec,
    rows_table,
    half,
    fresh,
    stitched,
    got,
    pair,
    far,
    new,
    table,
    lhs,
    image,
    edge_out,
    edge_in,
    send,
    recv,
):
    group = lax.axis_index("grp")
    tile = lax.axis_index("tile")
    core = lax.rem(group, 2)
    mate = {"grp": group + 1 - 2 * core}
    partner = {"grp": group + 2 - 4 * lax.div(group, 2)}
    right = {"tile": lax.rem(tile + 1, tiles)}
    left = {"tile": lax.rem(tile + tiles - 1, tiles)}

    def remote(number, src, dst, device):
        return pltpu.make_async_remote_copy(
            src_ref=src,
            dst_ref=dst,
            send_sem=send.at[number],
            recv_sem=recv.at[number],
            device_id=device,
            device_id_type=MESH,
        )

    barrier = pltpu.get_barrier_semaphore()
    for device in (mate, partner, left, right):
        pl.semaphore_signal(barrier, inc=1, device_id=device, device_id_type=MESH)
    pl.semaphore_wait(barrier, 4)

    first = [remote(i, grad.at[2 - 2 * core + i], got.at[i], mate) for i in (0, 1)]
    for copy in first:
        copy.start()
    second = []
    for i in (0, 1):
        first[i].wait_recv()
        pair[i] = grad[2 * core + i] + got[i]
        second.append(remote(2 + i, pair.at[i], far.at[i], partner))
        second[i].start()
    build_columns(half, table)
    third = []
    for i in (0, 1):
        second[i].wait_recv()
        mine = 2 * core + i
        lanes = pl.ds(pl.multiple_of(mine * LANES, LANES), LANES)
        new[mine] = spec[:, :, lanes] - STEP * (pair[i] + far[i])
        third.append(remote(4 + i, new.at[mine], new.at[mine], mate))
        third[i].start()
        third[i].wait_recv()
        for k in (i, i + 2):
            fresh[:, :, k * LANES : (k + 1) * LANES] = new[k]
        object_rows(i, new, rows_table, lhs)
        if i == 0:
            for k in range(BLOCKS):
                image[k] = object_block(i, k, lhs, table)
    image[3] += object_block(1, 3, lhs, table)
    for c in (0, 1):
        value = image[3, :, c * LANES : (c + 1) * LANES]
        edge_out[0, c] = pack_edge(value, 96)
        edge_out[1, c] = pack_edge(value, 112)
    edges = [
        remote(6, edge_out.at[0], edge_in.at[0], right),
        remote(7, edge_out.at[1], edge_in.at[1], left),
    ]
    for copy in edges:
        copy.start()
    for k in range(BLOCKS - 1):
        image[k] += object_block(1, k, lhs, table)
    for c in (0, 1):
        for k in (1, 2):
            stitched[c, :, k * LANES : (k + 1) * LANES] = image[k, :, c * LANES : (c + 1) * LANES]
    lane = lax.broadcasted_iota(jnp.int32, (1, LANES), 1)
    place = lane.astype(F32)
    at_head = (lane < MARGIN) & (tile > 0)
    at_tail = (lane >= 80) & (lane < 96) & (tile < tiles - 1)
    for copy in edges:
        copy.wait_recv()
    for c in (0, 1):
        own = image[0, :, c * LANES : (c + 1) * LANES]
        other = unpack_edge(edge_in[0, c], 0)
        blend = own * ((place + 16.5) / OV) + other * ((15.5 - place) / OV)
        stitched[c, :, :LANES] = jnp.where(at_head, blend, own)
        own = image[3, :, c * LANES : (c + 1) * LANES]
        other = unpack_edge(edge_in[1, c], 80)
        blend = own * ((111.5 - place) / OV) + other * ((place - 79.5) / OV)
        stitched[c, :, 3 * LANES :] = jnp.where(at_tail, blend, own)[:, : CORE - 3 * LANES]
    for copy in first + second + third + edges:
        copy.wait_send()


def finish(grad, spectrum):
    rows_table, half = (jnp.asarray(t) for t in object_tables())
    vmem = pl.BlockSpec(memory_space=pltpu.VMEM)
    part = (2, TH, LANES)
    return pl.pallas_call(
        functools.partial(finish_kernel, lax.axis_size("tile")),
        in_specs=[vmem] * 4,
        out_specs=[vmem] * 2,
        out_shape=[
            jax.ShapeDtypeStruct((2, TH, TW), F32),
            jax.ShapeDtypeStruct((2, TH, CORE), F32),
        ],
        scratch_shapes=[
            pltpu.VMEM((2,) + part, F32),
            pltpu.VMEM((2,) + part, F32),
            pltpu.VMEM((2,) + part, F32),
            pltpu.VMEM((BLOCKS,) + part, F32),
            pltpu.VMEM((2, 2, BLOCKS, TW, 2 * LANES), BF16),
            pltpu.VMEM((2, TH, TW), BF16),
            pltpu.VMEM((BLOCKS, TH, 2 * LANES), F32),
            pltpu.VMEM((2, 2, TH // 8, LANES), F32),
            pltpu.VMEM((2, 2, TH // 8, LANES), F32),
            pltpu.SemaphoreType.DMA((8,)),
            pltpu.SemaphoreType.DMA((8,)),
        ],
        compiler_params=pltpu.CompilerParams(
            collective_id=1, has_side_effects=True, vmem_limit_bytes=48 * 2**20
        ),
        name="finish",
    )(grad, spectrum, rows_table, half)


def body(raw, scales, flat, spectrum, pupil, patterns, led_row, led_col):
    window = measure(raw, scales, flat)
    spectrum_tile = spectrum[0]
    local_total = tile_gradient(spectrum_tile, pupil, window, patterns, led_row, led_col)
    fresh, stitched = finish(local_total, spectrum_tile)
    return (fresh[None], stitched)


def solution(mesh):
    return jax.shard_map(
        body,
        mesh=mesh,
        in_specs=(
            P("grp", "tile", None),
            P("grp", "tile", None),
            P(None, "tile"),
            P("tile", None, None, None),
            P(),
            P(),
            P(),
            P(),
        ),
        out_specs=(P("tile", None, None, None), P(None, None, "tile")),
        check_vma=False,
    )
```

```python
import functools
import math

import jax
import jax.numpy as jnp
import ml_dtypes
import numpy as np
from jax import lax
from jax.experimental import pallas as pl
from jax.experimental.pallas import tpu as pltpu
from jax.sharding import PartitionSpec as P

TH = 256
TW = 512
OV = 32
BR = 4
BC = 32
PR = 64
PC = 128
FR_G = 4
LEDS = 4
HALF = TH // 2
HR = PR // 2
MARGIN = OV // 2
CORE = TW - OV
LANES = 128
BLOCKS = TW // LANES
MESH = pl.DeviceIdType.MESH
STEP = 0.02
F32 = jnp.float32
BF16 = jnp.bfloat16


def split_np(table):
    hi = table.astype(ml_dtypes.bfloat16)
    lo = (table - hi.astype(np.float64)).astype(ml_dtypes.bfloat16)
    return hi, lo


def wave_np(length, band):
    places = np.arange(length)[:, None]
    freqs = np.arange(band)[None, :] - band // 2
    angle = (places * freqs % length) * (2.0 * np.pi / length)
    return np.cos(angle) / math.sqrt(band), np.sin(angle) / math.sqrt(band)


def object_tables():
    re, im = wave_np(TH, TH)
    rows = []
    for parity in (0, 1):
        a, b = re[:HALF, parity::2], im[:HALF, parity::2]
        rows.append(np.stack(split_np(np.block([[a, -b], [b, a]]))))
    re, im = (np.roll(part.T, -MARGIN, axis=1)[:TH] for part in wave_np(TW, TW))
    cols = np.stack([np.stack(split_np(re)), np.stack(split_np(im))], axis=1)
    return np.stack(rows), cols


def band_tables():
    col_re, col_im = (np.roll(part.T, -MARGIN, axis=1) for part in wave_np(TW, PC))
    cols = np.block([[col_re, col_im], [-col_im, col_re]])
    col_hi, col_lo = split_np(cols)
    row_re, row_im = wave_np(TH, PR)
    spread, gather = [], []
    for parity in (0, 1):
        re = row_re[:HALF, parity::2]
        im = row_im[:HALF, parity::2]
        rows_hi, rows_lo = split_np(np.block([[re, -im], [im, re]]))
        spread.append(np.concatenate([rows_hi, rows_hi, rows_lo, rows_lo], axis=1))
        gather.append(np.concatenate([rows_hi.T, rows_lo.T], axis=0))
    return np.stack([col_hi, col_lo]), np.stack(spread), np.stack(gather)


def split(x):
    hi = x.astype(BF16)
    return hi, (x - hi.astype(F32)).astype(BF16)


def dot(a, b):
    return jnp.dot(a, b, preferred_element_type=F32)


def dot_t(a, b):
    return lax.dot_general(a, b, (((1,), (1,)), ((), ())), preferred_element_type=F32)


def box_corner(pat, lrow, lcol, frame, j):
    led = pat[j, frame]
    return lrow[led], lcol[led]


def row_order(index):
    return jnp.where(index < HR, 2 * index, 2 * index - (PR - 1))


def ones_where(condition):
    return jnp.where(condition, 1.0, 0.0).astype(BF16)


def column_select(col):
    x = lax.broadcasted_iota(jnp.int32, (TW, PC), 0)
    v = lax.broadcasted_iota(jnp.int32, (TW, PC), 1)
    return ones_where(x - v == col)


def load_halves(spec, pup, halves, pd):
    for c in (0, 1):
        hi, lo = split(spec[c])
        halves[0, :, c * TW : (c + 1) * TW] = hi
        halves[1, :, c * TW : (c + 1) * TW] = lo
        for parity in (0, 1):
            pd[c, parity * HR : (parity + 1) * HR] = pup[c, pl.ds(parity, HR, stride=2), :]


def forward_frame(f, frame, pat, lrow, lcol, halves, pd, cols, spread, picked, lit, mid, field):
    y = lax.broadcasted_iota(jnp.int32, (PR, TH), 1)
    order = row_order(lax.broadcasted_iota(jnp.int32, (PR, TH), 0))
    corners = [box_corner(pat, lrow, lcol, frame, j) for j in range(LEDS)]
    choose = jnp.concatenate([ones_where(y - order == row) for row, _ in corners], axis=0)
    for h in (0, 1):
        picked[h] = dot(choose, halves[h]).astype(BF16)
    p_re, p_im = pd[0], pd[1]
    for j in range(LEDS):
        rows = pl.ds(j * PR, PR)
        stack = jnp.concatenate(
            [picked[h, rows, c * TW : (c + 1) * TW] for h in (0, 1) for c in (0, 1)], axis=0
        )
        cut = dot(stack, column_select(corners[j][1]))
        b_re = cut[:PR] + cut[2 * PR : 3 * PR]
        b_im = cut[PR : 2 * PR] + cut[3 * PR :]
        lit[rows, :PC] = p_re * b_re - p_im * b_im
        lit[rows, PC:] = p_re * b_im + p_im * b_re
    hi, lo = split(lit[...])
    mid[...] = dot(hi, cols[0]) + dot(lo, cols[0]) + dot(hi, cols[1])
    estimate = None
    for j in range(LEDS):
        parts = []
        for parity in (0, 1):
            rows = pl.ds(j * PR + parity * HR, HR)
            re_hi, re_lo = split(mid[rows, :TW])
            im_hi, im_lo = split(mid[rows, TW:])
            both = jnp.concatenate([re_hi, im_hi, re_lo, im_lo], axis=0)
            parts.append(dot(spread[parity], jnp.concatenate([both, both], axis=0)))
        upper = parts[0] + parts[1]
        lower = parts[0] - parts[1]
        field[f, j, 0, :HALF] = upper[:HALF]
        field[f, j, 0, HALF:] = lower[:HALF]
        field[f, j, 1, :HALF] = upper[HALF:]
        field[f, j, 1, HALF:] = lower[HALF:]
        power = jnp.concatenate(
            [
                upper[:HALF] * upper[:HALF] + upper[HALF:] * upper[HALF:],
                lower[:HALF] * lower[:HALF] + lower[HALF:] * lower[HALF:],
            ],
            axis=0,
        )
        estimate = power if estimate is None else estimate + power
    return estimate


def backward_frame(
    f, frame, misfit, pat, lrow, lcol, pd, cols, gather, field, low, wide, grad
):
    for j in range(LEDS):
        weighted = [misfit * field[f, j, c] for c in (0, 1)]
        for parity in (0, 1):
            mix = [
                w[:HALF] + w[HALF:] if parity == 0 else w[:HALF] - w[HALF:] for w in weighted
            ]
            hi, lo = split(jnp.concatenate(mix, axis=0))
            table = gather[parity]
            first = dot(table, hi)
            total = first[:PR] + first[PR:] + dot(table[:PR], lo)
            rows = pl.ds(j * PR + parity * HR, HR)
            low[rows, :TW] = total[:HR]
            low[rows, TW:] = total[HR:]
    hi, lo = split(low[...])
    grads = dot_t(hi, cols[0]) + dot_t(lo, cols[0]) + dot_t(hi, cols[1])
    p_re, p_im = pd[0], pd[1]
    lane = lax.broadcasted_iota(jnp.int32, (1, LEDS * PR), 1)
    target = row_order(lane & (PR - 1))
    for j in range(LEDS):
        row, col = box_corner(pat, lrow, lcol, frame, j)
        target = target + jnp.where((lane >= j * PR) & (lane < (j + 1) * PR), row, 0)
        rows = pl.ds(j * PR, PR)
        g_re = grads[j * PR : (j + 1) * PR, :PC]
        g_im = grads[j * PR : (j + 1) * PR, PC:]
        re_hi, re_lo = split(p_re * g_re + p_im * g_im)
        im_hi, im_lo = split(p_re * g_im - p_im * g_re)
        stack = jnp.concatenate([re_hi, im_hi, re_lo, im_lo], axis=0)
        placed = dot_t(stack, column_select(col)).astype(BF16)
        for h in (0, 1):
            for c in (0, 1):
                n = 2 * h + c
                wide[h, rows, c * TW : (c + 1) * TW] = placed[n * PR : (n + 1) * PR]
    y = lax.broadcasted_iota(jnp.int32, (TH, LEDS * PR), 0)
    choose = ones_where(y == target)
    total = dot(choose, wide[0]) + dot(choose, wide[1])
    for c in (0, 1):
        for k in range(BLOCKS):
            first = c * TW + k * LANES
            grad[k, c] += total[:, first : first + LANES]


def pack_edge(value, first):
    lane = lax.broadcasted_iota(jnp.int32, (TH // 8, LANES), 1) // MARGIN
    packed = jnp.zeros((TH // 8, LANES), F32)
    for b in range(8):
        piece = value[b * 32 : (b + 1) * 32]
        piece = pltpu.roll(piece, (MARGIN * b - first) % LANES, 1)
        packed = jnp.where(lane == b, piece, packed)
    return packed


def unpack_edge(packed, first):
    return jnp.concatenate(
        [pltpu.roll(packed, (first - MARGIN * b) % LANES, 1) for b in range(8)], axis=0
    )


def dequantize(raw, scales, dequant):
    frames, rows, width = raw.shape
    dequant[:, :LANES] = jnp.zeros((frames * rows, LANES), F32)
    dequant[:, LANES + width :] = jnp.zeros((frames * rows, LANES), F32)
    lane = lax.broadcasted_iota(jnp.int32, (rows, LANES), 1) // BC
    upper = lax.broadcasted_iota(jnp.int32, (rows, LANES), 0) < BR
    blocks = scales.shape[2]
    per = LANES // BC
    for first in range(0, blocks, LANES):
        count = min(LANES, blocks - first)
        for f in range(frames):
            pair = scales[f, :, first : first + count].astype(F32)
            if count < LANES:
                pair = jnp.concatenate([pair, jnp.zeros((2, LANES - count), F32)], axis=1)
            factors = jnp.where(
                upper,
                jnp.broadcast_to(pair[0:1], (rows, LANES)),
                jnp.broadcast_to(pair[1:2], (rows, LANES)),
            )
            for k in range(count // per):
                column = (first // per + k) * LANES
                spread = jnp.take_along_axis(factors, lane + per * k, axis=1)
                codes = raw[f, :, column : column + LANES].astype(F32)
                dequant[f * rows : (f + 1) * rows, LANES + column : 2 * LANES + column] = (
                    codes * spread
                )


def cut_message(dequant, tile):
    start = CORE * tile - MARGIN + LANES
    aligned = pl.multiple_of(start // LANES * LANES, LANES)
    offset = start - aligned + MARGIN
    wide = dequant[:, pl.ds(aligned, TW + LANES)]
    wide = pltpu.roll(wide, TW + LANES - offset, 1)
    lane = lax.broadcasted_iota(jnp.int32, (1, LANES), 1)
    last = jnp.where(lane < LANES - MARGIN, wide[:, TW - LANES : TW], wide[:, TW:])
    return jnp.concatenate([wide[:, : TW - LANES], last], axis=1).astype(BF16)


def centred():
    y = lax.broadcasted_iota(jnp.int32, (TH, 1), 0).astype(F32) - (TH - 1) / 2.0
    lane = lax.broadcasted_iota(jnp.int32, (1, TW), 1)
    x = lane.astype(F32) - (CORE - 1) / 2.0
    return y, x, lane


Y_NORM = float(np.sum((np.arange(TH) - (TH - 1) / 2.0) ** 2) * CORE)
X_NORM = float(np.sum((np.arange(CORE) - (CORE - 1) / 2.0) ** 2) * TH)


def build_columns(half, table):
    lane = lax.broadcasted_iota(jnp.int32, (1, TW), 1)
    sign = (1 - 2 * (lane & 1)).astype(F32)
    for i in (0, 1):
        rows = pl.ds(i * LANES, LANES)
        for h in (0, 1):
            re = half[h, 0, rows, :].astype(F32)
            im = half[h, 1, rows, :].astype(F32)
            for n, factor in ((0, None), (1, sign)):
                a = re if factor is None else re * factor
                b = im if factor is None else im * factor
                upper = pl.ds(n * LANES, LANES)
                lower = pl.ds((2 + n) * LANES, LANES)
                for k in range(BLOCKS):
                    cut = slice(k * LANES, (k + 1) * LANES)
                    table[i, h, k, upper, :LANES] = a[:, cut].astype(BF16)
                    table[i, h, k, upper, LANES:] = b[:, cut].astype(BF16)
                    table[i, h, k, lower, :LANES] = (-b[:, cut]).astype(BF16)
                    table[i, h, k, lower, LANES:] = a[:, cut].astype(BF16)


def object_rows(i, new, rows_table, lhs):
    parts = []
    for parity in (0, 1):
        data = [
            jnp.concatenate(
                [new[k, c, pl.ds(parity, HALF, stride=2), :] for k in (i, i + 2)], axis=1
            )
            for c in (0, 1)
        ]
        hi, lo = split(jnp.concatenate(data, axis=0))
        t_hi, t_lo = rows_table[parity, 0], rows_table[parity, 1]
        parts.append(dot(t_hi, hi) + dot(t_hi, lo) + dot(t_lo, hi))
    for n, value in enumerate((parts[0] + parts[1], parts[0] - parts[1])):
        hi, lo = split(value)
        rows = pl.ds(n * HALF, HALF)
        for h, part in enumerate((hi, lo)):
            lhs[h, rows, : 2 * LANES] = part[:HALF]
            lhs[h, rows, 2 * LANES :] = part[HALF:]


def object_block(i, k, lhs, table):
    hi, lo = lhs[0], lhs[1]
    return dot(hi, table[i, 0, k]) + dot(lo, table[i, 0, k]) + dot(hi, table[i, 1, k])


def update_kernel(
    tiles,
    pat,
    lrow,
    lcol,
    raw_h,
    scales_h,
    flat_h,
    spec_h,
    pup_h,
    cols_h,
    spread_h,
    gather_h,
    rows_h,
    half_h,
    fresh,
    stitched,
    raw,
    scales,
    flat,
    spec,
    pup,
    cols,
    spread,
    gather,
    rows_table,
    half,
    dequant,
    message,
    arrived,
    window,
    gains,
    flat_out,
    flat_in,
    slope_out,
    slope_in,
    halves,
    pd,
    picked,
    lit,
    mid,
    field,
    estimate,
    grad,
    got,
    pair,
    far,
    new,
    table,
    lhs,
    image,
    strip,
    edge_out,
    edge_in,
    load,
    store,
    send,
    recv,
    side_send,
    side_recv,
):
    frames = raw.shape[0]
    rows = raw.shape[1]
    group = lax.axis_index("grp")
    tile = lax.axis_index("tile")
    core = lax.rem(group, 2)
    mate = {"grp": group + 1 - 2 * core}
    partner = {"grp": group + 2 - 4 * lax.div(group, 2)}
    right = {"tile": lax.rem(tile + 1, tiles)}
    left = {"tile": lax.rem(tile + tiles - 1, tiles)}

    def side(number, src, dst, device):
        return pltpu.make_async_remote_copy(
            src_ref=src,
            dst_ref=dst,
            send_sem=side_send.at[number],
            recv_sem=side_recv.at[number],
            device_id=device,
            device_id_type=MESH,
        )

    def block(source, target):
        return pltpu.make_async_remote_copy(
            src_ref=message.at[target],
            dst_ref=arrived.at[source],
            send_sem=send.at[target],
            recv_sem=recv.at[source],
            device_id={"tile": target},
            device_id_type=MESH,
        )

    loads = [
        pltpu.make_async_copy(src, dst, load.at[n])
        for n, (src, dst) in enumerate(
            (
                (raw_h, raw),
                (scales_h, scales),
                (flat_h, flat),
                (spec_h, spec),
                (pup_h, pup),
                (cols_h, cols),
                (spread_h, spread),
                (gather_h, gather),
                (half_h, half),
                (rows_h, rows_table),
            )
        )
    ]
    for copy in loads:
        copy.start()
    barrier = pltpu.get_barrier_semaphore()

    @pl.loop(1, tiles)
    def _(i):
        pl.semaphore_signal(
            barrier, inc=1, device_id={"tile": lax.rem(tile + i, tiles)}, device_id_type=MESH
        )

    for device in (mate, partner):
        pl.semaphore_signal(barrier, inc=1, device_id=device, device_id_type=MESH)

    loads[0].wait()
    loads[1].wait()
    dequantize(raw, scales, dequant)
    pl.semaphore_wait(barrier, tiles + 1)

    @pl.loop(1, tiles)
    def _(i):
        target = lax.rem(tile + i, tiles)
        message[target] = cut_message(dequant, target)
        block(tile, target).start()

    arrived[tile] = cut_message(dequant, tile)
    loads[2].wait()
    for k in range(BLOCKS - 1):
        gains[:, k * LANES : (k + 1) * LANES] = flat[k * LANES : (k + 1) * LANES, :].T
    tail = jnp.concatenate(
        [flat[3 * LANES :, :], jnp.zeros((TW - CORE, TH), F32)], axis=0
    ).T
    gains[:, 3 * LANES :] = tail
    flat_out[0] = pack_edge(tail, 80)
    flat_out[1] = pack_edge(gains[:, :LANES], 0)
    flats = [
        side(0, flat_out.at[0], flat_in.at[0], right),
        side(1, flat_out.at[1], flat_in.at[1], left),
    ]
    for copy in flats:
        copy.start()

    for copy in loads[3:8]:
        copy.wait()
    load_halves(spec, pup, halves, pd)
    first_frame = group * frames

    def forward(f):
        estimate[f] = forward_frame(
            f, first_frame + f, pat, lrow, lcol, halves, pd, cols, spread, picked, lit, mid, field
        )

    pl.loop(0, frames - 1)(forward)
    grad[...] = jnp.zeros_like(grad)
    for copy in loads[8:]:
        copy.wait()
    build_columns(half, table)

    y, x, lane = centred()
    edge = lane[:, 3 * LANES :]
    for copy in flats:
        copy.wait_recv()
    outer = jnp.where(
        edge < CORE + MARGIN, unpack_edge(flat_in[1], 96), unpack_edge(flat_in[0], 112)
    )
    gains[:, 3 * LANES :] = jnp.where(edge < CORE, gains[:, 3 * LANES :], outer)

    @pl.loop(1, tiles + 1)
    def _(i):
        source = lax.rem(tile + tiles - i, tiles)

        @pl.when(i < tiles)
        def _():
            block(source, tile).wait_recv()

        here = pl.ds(pl.multiple_of(source * rows, rows), rows)
        values = arrived[source].astype(F32)
        for f in range(frames):
            window[f, here, :] = values[f * rows : (f + 1) * rows] * gains[here, :]

    inside = (lane < CORE).astype(F32)
    slopes = []
    for f in range(frames):
        flattened = window[f]
        columns = jnp.sum(flattened, axis=0, keepdims=True)
        tilted = jnp.sum(flattened * y, axis=0, keepdims=True)
        slope_y = jnp.sum(tilted * inside, axis=1, keepdims=True) / Y_NORM
        slope_x = jnp.sum(columns * (x * inside), axis=1, keepdims=True) / X_NORM
        slopes.append((slope_y, slope_x))
        slope_out[f : f + 1] = jnp.broadcast_to(slope_y, (1, LANES))
        slope_out[frames + f : frames + f + 1] = jnp.broadcast_to(slope_x, (1, LANES))
    copies = [side(2, slope_out, slope_in.at[0], right), side(3, slope_out, slope_in.at[1], left)]
    for copy in copies:
        copy.start()
    forward(frames - 1)
    for copy in copies:
        copy.wait_recv()
    x_edge = x[:, 3 * LANES :]
    own = edge < CORE
    after = edge < CORE + MARGIN
    blank = ((~own) & after & (tile == tiles - 1)) | ((~after) & (tile == 0))
    for f in range(frames):
        slope_y, slope_x = slopes[f]
        for k in range(BLOCKS - 1):
            cut = slice(k * LANES, (k + 1) * LANES)
            window[f, :, cut] = window[f, :, cut] - slope_y * y - slope_x * x[:, cut]
        row_y = jnp.where(
            own, slope_y, jnp.where(after, slope_in[1, f : f + 1], slope_in[0, f : f + 1])
        )
        row_x = jnp.where(
            own,
            slope_x * x_edge,
            jnp.where(
                after,
                slope_in[1, frames + f : frames + f + 1] * (x_edge - CORE),
                slope_in[0, frames + f : frames + f + 1] * (x_edge - 32.0),
            ),
        )
        value = window[f, :, 3 * LANES :] - row_y * y - row_x
        window[f, :, 3 * LANES :] = jnp.where(blank, 0.0, value)

    @pl.loop(0, frames)
    def _(f):
        misfit = estimate[f] - window[f]
        backward_frame(
            f, first_frame + f, misfit, pat, lrow, lcol, pd, cols, gather, field, mid, picked, grad
        )

    pieces = [(i, c) for i in (0, 1) for c in (0, 1)]
    first = [
        side(4 + n, grad.at[2 - 2 * core + i, c], got.at[i, c], mate)
        for n, (i, c) in enumerate(pieces)
    ]
    for copy in first:
        copy.start()
    second = []
    for n, (i, c) in enumerate(pieces):
        first[n].wait_recv()
        pair[i, c] = grad[2 * core + i, c] + got[i, c]
        second.append(side(8 + n, pair.at[i, c], far.at[i, c], partner))
        second[n].start()
    third = []
    out = []
    for i in (0, 1):
        mine = 2 * core + i
        lanes = pl.ds(pl.multiple_of(mine * LANES, LANES), LANES)
        for c in (0, 1):
            n = 2 * i + c
            second[n].wait_recv()
            new[mine, c] = spec[c, :, lanes] - STEP * (pair[i, c] + far[i, c])
            third.append(side(12 + n, new.at[mine, c], new.at[mine, c], mate))
            third[n].start()
        for c in (0, 1):
            third[2 * i + c].wait_recv()
        for k in (i, i + 2):
            out.append(
                pltpu.make_async_copy(
                    new.at[k], fresh.at[:, :, k * LANES : (k + 1) * LANES], store.at[k]
                )
            )
            out[-1].start()
        object_rows(i, new, rows_table, lhs)
        if i == 0:
            for k in range(BLOCKS):
                image[k] = object_block(i, k, lhs, table)
    image[3] += object_block(1, 3, lhs, table)
    for c in (0, 1):
        value = image[3, :, c * LANES : (c + 1) * LANES]
        edge_out[0, c] = pack_edge(value, 96)
        edge_out[1, c] = pack_edge(value, 112)
    edges = [
        side(16, edge_out.at[0], edge_in.at[0], right),
        side(17, edge_out.at[1], edge_in.at[1], left),
    ]
    for copy in edges:
        copy.start()
    for k in range(BLOCKS - 1):
        image[k] += object_block(1, k, lhs, table)
    for c in (0, 1):
        for k in (1, 2):
            strip[c, k * LANES : (k + 1) * LANES, :] = image[
                k, :, c * LANES : (c + 1) * LANES
            ].T
    place = edge.astype(F32) - float(3 * LANES)
    at_head = (place < MARGIN) & (tile > 0)
    at_tail = (place >= 80) & (place < 96) & (tile < tiles - 1)
    for copy in edges:
        copy.wait_recv()
    for c in (0, 1):
        mine = image[0, :, c * LANES : (c + 1) * LANES]
        other = unpack_edge(edge_in[0, c], 0)
        blend = mine * ((place + 16.5) / OV) + other * ((15.5 - place) / OV)
        strip[c, :LANES, :] = jnp.where(at_head, blend, mine).T
        mine = image[3, :, c * LANES : (c + 1) * LANES]
        other = unpack_edge(edge_in[1, c], 80)
        blend = mine * ((111.5 - place) / OV) + other * ((place - 79.5) / OV)
        strip[c, 3 * LANES :, :] = jnp.where(at_tail, blend, mine).T[: CORE - 3 * LANES]
        out.append(pltpu.make_async_copy(strip.at[c], stitched.at[c], store.at[4 + c]))
        out[-1].start()
    for copy in flats + copies + first + second + third + edges:
        copy.wait_send()

    @pl.loop(1, tiles)
    def _(i):
        block(tile, lax.rem(tile + i, tiles)).wait_send()

    for copy in out:
        copy.wait()


def update(raw, scales, flat, spectrum, pupil, patterns, led_row, led_col):
    tiles = lax.axis_size("tile")
    frames, rows, width = raw.shape
    deep = frames * rows
    tables = [jnp.asarray(t) for t in band_tables() + object_tables()]
    smem = pl.BlockSpec(memory_space=pltpu.SMEM)
    hbm = pl.BlockSpec(memory_space=pltpu.MemorySpace.HBM)
    arrays = [raw, scales, flat, spectrum, pupil] + tables
    small = (TH // 8, LANES)
    part = (2, TH, LANES)
    scratch = [pltpu.VMEM(a.shape, a.dtype) for a in arrays]
    scratch += [
        pltpu.VMEM((deep, width + 2 * LANES), F32),
        pltpu.VMEM((tiles, deep, TW), BF16),
        pltpu.VMEM((tiles, deep, TW), BF16),
        pltpu.VMEM((frames, TH, TW), F32),
        pltpu.VMEM((TH, TW), F32),
        pltpu.VMEM((2,) + small, F32),
        pltpu.VMEM((2,) + small, F32),
        pltpu.VMEM((2 * frames, LANES), F32),
        pltpu.VMEM((2, 2 * frames, LANES), F32),
        pltpu.VMEM((2, TH, 2 * TW), BF16),
        pltpu.VMEM((2, PR, PC), F32),
        pltpu.VMEM((2, LEDS * PR, 2 * TW), BF16),
        pltpu.VMEM((LEDS * PR, 2 * PC), F32),
        pltpu.VMEM((LEDS * PR, 2 * TW), F32),
        pltpu.VMEM((frames, LEDS, 2, TH, TW), F32),
        pltpu.VMEM((frames, TH, TW), F32),
        pltpu.VMEM((BLOCKS,) + part, F32),
        pltpu.VMEM((2,) + part, F32),
        pltpu.VMEM((2,) + part, F32),
        pltpu.VMEM((2,) + part, F32),
        pltpu.VMEM((BLOCKS,) + part, F32),
        pltpu.VMEM((2, 2, BLOCKS, TW, 2 * LANES), BF16),
        pltpu.VMEM((2, TH, TW), BF16),
        pltpu.VMEM((BLOCKS, TH, 2 * LANES), F32),
        pltpu.VMEM((2, CORE, TH), F32),
        pltpu.VMEM((2, 2) + small, F32),
        pltpu.VMEM((2, 2) + small, F32),
        pltpu.SemaphoreType.DMA((10,)),
        pltpu.SemaphoreType.DMA((6,)),
        pltpu.SemaphoreType.DMA((tiles,)),
        pltpu.SemaphoreType.DMA((tiles,)),
        pltpu.SemaphoreType.DMA((18,)),
        pltpu.SemaphoreType.DMA((18,)),
    ]
    return pl.pallas_call(
        functools.partial(update_kernel, tiles),
        in_specs=[smem] * 3 + [hbm] * len(arrays),
        out_specs=[hbm] * 2,
        out_shape=[
            jax.ShapeDtypeStruct((2, TH, TW), F32),
            jax.ShapeDtypeStruct((2, CORE, TH), F32),
        ],
        scratch_shapes=scratch,
        compiler_params=pltpu.CompilerParams(
            collective_id=1, has_side_effects=True, vmem_limit_bytes=62 * 2**20
        ),
        name="update",
    )(patterns, led_row, led_col, *arrays)


def body(raw, scales, flat, spectrum, pupil, patterns, led_row, led_col):
    fresh, stitched = update(
        raw, scales, flat.T, spectrum[0], pupil, patterns.T, led_row, led_col
    )
    return (fresh[None], jnp.swapaxes(stitched, 1, 2))


def solution(mesh):
    return jax.shard_map(
        body,
        mesh=mesh,
        in_specs=(
            P("grp", "tile", None),
            P("grp", "tile", None),
            P(None, "tile"),
            P("tile", None, None, None),
            P(),
            P(),
            P(),
            P(),
        ),
        out_specs=(P("tile", None, None, None), P(None, None, "tile")),
        check_vma=False,
    )
```

```python
import functools
import math

import jax
import jax.numpy as jnp
import ml_dtypes
import numpy as np
from jax import lax
from jax.experimental import pallas as pl
from jax.experimental.pallas import tpu as pltpu
from jax.sharding import PartitionSpec as P

TH = 256
TW = 512
OV = 32
BR = 4
BC = 32
PR = 64
PC = 128
FR_G = 4
LEDS = 4
HALF = TH // 2
HR = PR // 2
MARGIN = OV // 2
CORE = TW - OV
LANES = 128
BLOCKS = TW // LANES
MESH = pl.DeviceIdType.MESH
CODE_ROWS = 32
CODE_TOP = 32767.0
STEP = 0.02
F32 = jnp.float32
BF16 = jnp.bfloat16


def split_np(table):
    hi = table.astype(ml_dtypes.bfloat16)
    lo = (table - hi.astype(np.float64)).astype(ml_dtypes.bfloat16)
    return hi, lo


def wave_np(length, band):
    places = np.arange(length)[:, None]
    freqs = np.arange(band)[None, :] - band // 2
    angle = (places * freqs % length) * (2.0 * np.pi / length)
    return np.cos(angle) / math.sqrt(band), np.sin(angle) / math.sqrt(band)


def object_tables():
    re, im = wave_np(TH, TH)
    rows = []
    for parity in (0, 1):
        a, b = re[:HALF, parity::2], im[:HALF, parity::2]
        rows.append(np.stack(split_np(np.block([[a, -b], [b, a]]))))
    re, im = (np.roll(part.T, -MARGIN, axis=1)[:TH] for part in wave_np(TW, TW))
    cols = np.stack([np.stack(split_np(re)), np.stack(split_np(im))], axis=1)
    return np.stack(rows), cols


def band_tables():
    row_re, row_im = wave_np(TH, PR)
    spread, gather = [], []
    for parity in (0, 1):
        re = row_re[:HALF, parity::2]
        im = row_im[:HALF, parity::2]
        rows_hi, rows_lo = split_np(np.block([[re, -im], [im, re]]))
        spread.append(np.concatenate([rows_hi, rows_hi, rows_lo, rows_lo], axis=1))
        gather.append(np.concatenate([rows_hi.T, rows_lo.T], axis=0))
    return np.stack(spread), np.stack(gather)


def split(x):
    hi = x.astype(BF16)
    return hi, (x - hi.astype(F32)).astype(BF16)


def dot(a, b):
    return jnp.dot(a, b, preferred_element_type=F32)


def box_corner(pat, lrow, lcol, frame, j):
    led = pat[j, frame]
    return lrow[led], lcol[led]


def row_order(index):
    return jnp.where(index < HR, 2 * index, 2 * index - (PR - 1))


def ones_where(condition):
    return jnp.where(condition, 1.0, 0.0).astype(BF16)


def column_select(col):
    x = lax.broadcasted_iota(jnp.int32, (TW, PC), 0)
    v = lax.broadcasted_iota(jnp.int32, (TW, PC), 1)
    return ones_where(x - v == col)


def column_place(col):
    v = lax.broadcasted_iota(jnp.int32, (PC, TW), 0)
    x = lax.broadcasted_iota(jnp.int32, (PC, TW), 1)
    return ones_where(x - v == col)


def load_halves(spec, pup, halves, pd):
    for c in (0, 1):
        hi, lo = split(spec[c])
        halves[0, :, c * TW : (c + 1) * TW] = hi
        halves[1, :, c * TW : (c + 1) * TW] = lo
        for parity in (0, 1):
            pd[c, parity * HR : (parity + 1) * HR] = pup[c, pl.ds(parity, HR, stride=2), :]


def forward_frame(f, frame, pat, lrow, lcol, halves, pd, cols, spread, picked, lit, mid, field):
    y = lax.broadcasted_iota(jnp.int32, (PR, TH), 1)
    order = row_order(lax.broadcasted_iota(jnp.int32, (PR, TH), 0))
    corners = [box_corner(pat, lrow, lcol, frame, j) for j in range(LEDS)]
    choose = jnp.concatenate([ones_where(y - order == row) for row, _ in corners], axis=0)
    for h in (0, 1):
        picked[h] = dot(choose, halves[h]).astype(BF16)
    p_re, p_im = pd[0], pd[1]
    for j in range(LEDS):
        rows = pl.ds(j * PR, PR)
        stack = jnp.concatenate(
            [picked[h, rows, c * TW : (c + 1) * TW] for h in (0, 1) for c in (0, 1)], axis=0
        )
        cut = dot(stack, column_select(corners[j][1]))
        b_re = cut[:PR] + cut[2 * PR : 3 * PR]
        b_im = cut[PR : 2 * PR] + cut[3 * PR :]
        lit[rows, :PC] = p_re * b_re - p_im * b_im
        lit[rows, PC:] = p_re * b_im + p_im * b_re
    hi, lo = split(lit[...])
    mid[...] = dot(hi, cols[0]) + dot(lo, cols[0]) + dot(hi, cols[1])
    estimate = None
    for j in range(LEDS):
        parts = []
        for parity in (0, 1):
            rows = pl.ds(j * PR + parity * HR, HR)
            re_hi, re_lo = split(mid[rows, :TW])
            im_hi, im_lo = split(mid[rows, TW:])
            both = jnp.concatenate([re_hi, im_hi, re_lo, im_lo], axis=0)
            parts.append(dot(spread[parity], jnp.concatenate([both, both], axis=0)))
        upper = parts[0] + parts[1]
        lower = parts[0] - parts[1]
        field[f, j, 0, :HALF] = upper[:HALF]
        field[f, j, 0, HALF:] = lower[:HALF]
        field[f, j, 1, :HALF] = upper[HALF:]
        field[f, j, 1, HALF:] = lower[HALF:]
        power = jnp.concatenate(
            [
                upper[:HALF] * upper[:HALF] + upper[HALF:] * upper[HALF:],
                lower[:HALF] * lower[:HALF] + lower[HALF:] * lower[HALF:],
            ],
            axis=0,
        )
        estimate = power if estimate is None else estimate + power
    return estimate


def backward_frame(
    f, frame, misfit, pat, lrow, lcol, pd, cols, gather, field, low, wide, grad
):
    for j in range(LEDS):
        weighted = [misfit * field[f, j, c] for c in (0, 1)]
        for parity in (0, 1):
            mix = [
                w[:HALF] + w[HALF:] if parity == 0 else w[:HALF] - w[HALF:] for w in weighted
            ]
            hi, lo = split(jnp.concatenate(mix, axis=0))
            table = gather[parity]
            first = dot(table, hi)
            total = first[:PR] + first[PR:] + dot(table[:PR], lo)
            rows = pl.ds(j * PR + parity * HR, HR)
            low[rows, :TW] = total[:HR]
            low[rows, TW:] = total[HR:]
    hi, lo = split(low[...])
    grads = dot(hi, cols[0]) + dot(lo, cols[0]) + dot(hi, cols[1])
    p_re, p_im = pd[0], pd[1]
    lane = lax.broadcasted_iota(jnp.int32, (1, LEDS * PR), 1)
    target = row_order(lane & (PR - 1))
    for j in range(LEDS):
        row, col = box_corner(pat, lrow, lcol, frame, j)
        target = target + jnp.where((lane >= j * PR) & (lane < (j + 1) * PR), row, 0)
        rows = pl.ds(j * PR, PR)
        g_re = grads[j * PR : (j + 1) * PR, :PC]
        g_im = grads[j * PR : (j + 1) * PR, PC:]
        re_hi, re_lo = split(p_re * g_re + p_im * g_im)
        im_hi, im_lo = split(p_re * g_im - p_im * g_re)
        stack = jnp.concatenate([re_hi, im_hi, re_lo, im_lo], axis=0)
        placed = dot(stack, column_place(col)).astype(BF16)
        for h in (0, 1):
            for c in (0, 1):
                n = 2 * h + c
                wide[h, rows, c * TW : (c + 1) * TW] = placed[n * PR : (n + 1) * PR]
    y = lax.broadcasted_iota(jnp.int32, (TH, LEDS * PR), 0)
    choose = ones_where(y == target)
    total = dot(choose, wide[0]) + dot(choose, wide[1])
    for c in (0, 1):
        for k in range(BLOCKS):
            first = c * TW + k * LANES
            grad[k, c] += total[:, first : first + LANES]


def pack_edge(value, first):
    lane = lax.broadcasted_iota(jnp.int32, (TH // 8, LANES), 1) // MARGIN
    packed = jnp.zeros((TH // 8, LANES), F32)
    for b in range(8):
        piece = value[b * 32 : (b + 1) * 32]
        piece = pltpu.roll(piece, (MARGIN * b - first) % LANES, 1)
        packed = jnp.where(lane == b, piece, packed)
    return packed


def unpack_edge(packed, first):
    return jnp.concatenate(
        [pltpu.roll(packed, (first - MARGIN * b) % LANES, 1) for b in range(8)], axis=0
    )


def dequantize(raw, scales, dequant):
    frames, rows, width = raw.shape
    dequant[:, :LANES] = jnp.zeros((frames * rows, LANES), F32)
    dequant[:, LANES + width :] = jnp.zeros((frames * rows, LANES), F32)
    lane = lax.broadcasted_iota(jnp.int32, (rows, LANES), 1) // BC
    upper = lax.broadcasted_iota(jnp.int32, (rows, LANES), 0) < BR
    blocks = scales.shape[2]
    per = LANES // BC
    for first in range(0, blocks, LANES):
        count = min(LANES, blocks - first)
        for f in range(frames):
            pair = scales[f, :, first : first + count].astype(F32)
            if count < LANES:
                pair = jnp.concatenate([pair, jnp.zeros((2, LANES - count), F32)], axis=1)
            factors = jnp.where(
                upper,
                jnp.broadcast_to(pair[0:1], (rows, LANES)),
                jnp.broadcast_to(pair[1:2], (rows, LANES)),
            )
            for k in range(count // per):
                column = (first // per + k) * LANES
                spread = jnp.take_along_axis(factors, lane + per * k, axis=1)
                codes = raw[f, :, column : column + LANES].astype(F32)
                dequant[f * rows : (f + 1) * rows, LANES + column : 2 * LANES + column] = (
                    codes * spread
                )


def cut_message(dequant, tile):
    start = CORE * tile - MARGIN + LANES
    aligned = pl.multiple_of(start // LANES * LANES, LANES)
    offset = start - aligned + MARGIN
    wide = dequant[:, pl.ds(aligned, TW + LANES)]
    wide = pltpu.roll(wide, TW + LANES - offset, 1)
    lane = lax.broadcasted_iota(jnp.int32, (1, LANES), 1)
    last = jnp.where(lane < LANES - MARGIN, wide[:, TW - LANES : TW], wide[:, TW:])
    return jnp.concatenate([wide[:, : TW - LANES], last], axis=1).astype(BF16)


def centred():
    y = lax.broadcasted_iota(jnp.int32, (TH, 1), 0).astype(F32) - (TH - 1) / 2.0
    lane = lax.broadcasted_iota(jnp.int32, (1, TW), 1)
    x = lane.astype(F32) - (CORE - 1) / 2.0
    return y, x, lane


Y_NORM = float(np.sum((np.arange(TH) - (TH - 1) / 2.0) ** 2) * CORE)
X_NORM = float(np.sum((np.arange(CORE) - (CORE - 1) / 2.0) ** 2) * TH)


def build_band(half, cols, cols_t):
    lane = lax.broadcasted_iota(jnp.int32, (1, TW), 1)
    sign = (2 - 4 * (lane & 1)).astype(F32)
    for h in (0, 1):
        re, im = (
            jnp.concatenate(
                [
                    half[h, c, TH - PC // 2 :, :].astype(F32) * 2.0,
                    half[h, c, : PC // 2, :].astype(F32) * sign,
                ],
                axis=0,
            )
            for c in (0, 1)
        )
        cols[h, :PC, :TW] = re.astype(BF16)
        cols[h, :PC, TW:] = im.astype(BF16)
        cols[h, PC:, :TW] = (-im).astype(BF16)
        cols[h, PC:, TW:] = re.astype(BF16)
        re, im = re.T, im.T
        cols_t[h, :TW, :PC] = re.astype(BF16)
        cols_t[h, :TW, PC:] = (-im).astype(BF16)
        cols_t[h, TW:, :PC] = im.astype(BF16)
        cols_t[h, TW:, PC:] = re.astype(BF16)


def build_columns(half, table):
    lane = lax.broadcasted_iota(jnp.int32, (1, TW), 1)
    sign = (1 - 2 * (lane & 1)).astype(F32)
    for i in (0, 1):
        rows = pl.ds(i * LANES, LANES)
        for h in (0, 1):
            re = half[h, 0, rows, :].astype(F32)
            im = half[h, 1, rows, :].astype(F32)
            for n, factor in ((0, None), (1, sign)):
                a = re if factor is None else re * factor
                b = im if factor is None else im * factor
                upper = pl.ds(n * LANES, LANES)
                lower = pl.ds((2 + n) * LANES, LANES)
                for k in range(BLOCKS):
                    cut = slice(k * LANES, (k + 1) * LANES)
                    table[i, h, k, upper, :LANES] = a[:, cut].astype(BF16)
                    table[i, h, k, upper, LANES:] = b[:, cut].astype(BF16)
                    table[i, h, k, lower, :LANES] = (-b[:, cut]).astype(BF16)
                    table[i, h, k, lower, LANES:] = a[:, cut].astype(BF16)


def object_rows(i, new, rows_table, lhs):
    parts = []
    for parity in (0, 1):
        data = [
            jnp.concatenate(
                [new[k, c, pl.ds(parity, HALF, stride=2), :] for k in (i, i + 2)], axis=1
            )
            for c in (0, 1)
        ]
        hi, lo = split(jnp.concatenate(data, axis=0))
        t_hi, t_lo = rows_table[parity, 0], rows_table[parity, 1]
        parts.append(dot(t_hi, hi) + dot(t_hi, lo) + dot(t_lo, hi))
    for n, value in enumerate((parts[0] + parts[1], parts[0] - parts[1])):
        hi, lo = split(value)
        rows = pl.ds(n * HALF, HALF)
        for h, part in enumerate((hi, lo)):
            lhs[h, rows, : 2 * LANES] = part[:HALF]
            lhs[h, rows, 2 * LANES :] = part[HALF:]


def object_block(i, k, lhs, table):
    hi, lo = lhs[0], lhs[1]
    return dot(hi, table[i, 0, k]) + dot(lo, table[i, 0, k]) + dot(hi, table[i, 1, k])


def encode(value, code, unit):
    for g in range(TH // CODE_ROWS):
        rows = slice(g * CODE_ROWS, (g + 1) * CODE_ROWS)
        piece = value[rows]
        top = jnp.max(jnp.abs(piece), axis=0, keepdims=True)
        unit[g : g + 1] = top * (1.0 / CODE_TOP)
        ratio = jnp.where(top > 0.0, CODE_TOP / top, 0.0)
        whole = jnp.clip(jnp.round(piece * ratio), -CODE_TOP, CODE_TOP)
        code[rows] = whole.astype(jnp.int32).astype(jnp.int16)


def decode(code, unit):
    return jnp.concatenate(
        [
            code[g * CODE_ROWS : (g + 1) * CODE_ROWS].astype(jnp.int32).astype(F32)
            * unit[g : g + 1]
            for g in range(TH // CODE_ROWS)
        ],
        axis=0,
    )


def update_kernel(
    tiles,
    pat,
    lrow,
    lcol,
    raw_h,
    scales_h,
    flat_h,
    spec_h,
    pup_h,
    spread_h,
    gather_h,
    rows_h,
    half_h,
    fresh,
    stitched,
    raw,
    scales,
    flat,
    spec,
    pup,
    spread,
    gather,
    rows_table,
    half,
    cols,
    cols_t,
    dequant,
    message,
    arrived,
    window,
    gains,
    flat_out,
    flat_in,
    slope_out,
    slope_in,
    halves,
    pd,
    picked,
    lit,
    mid,
    field,
    estimate,
    grad,
    got,
    code,
    unit,
    far_code,
    far_unit,
    new,
    table,
    lhs,
    image,
    strip,
    edge_out,
    edge_in,
    load,
    store,
    send,
    recv,
    side_send,
    side_recv,
):
    frames = raw.shape[0]
    rows = raw.shape[1]
    group = lax.axis_index("grp")
    tile = lax.axis_index("tile")
    core = lax.rem(group, 2)
    mate = {"grp": group + 1 - 2 * core}
    partner = {"grp": group + 2 - 4 * lax.div(group, 2)}
    right = {"tile": lax.rem(tile + 1, tiles)}
    left = {"tile": lax.rem(tile + tiles - 1, tiles)}

    def side(number, src, dst, device):
        return pltpu.make_async_remote_copy(
            src_ref=src,
            dst_ref=dst,
            send_sem=side_send.at[number],
            recv_sem=side_recv.at[number],
            device_id=device,
            device_id_type=MESH,
        )

    def block(source, target):
        return pltpu.make_async_remote_copy(
            src_ref=message.at[target],
            dst_ref=arrived.at[source],
            send_sem=send.at[target],
            recv_sem=recv.at[source],
            device_id={"tile": target},
            device_id_type=MESH,
        )

    loads = [
        pltpu.make_async_copy(src, dst, load.at[n])
        for n, (src, dst) in enumerate(
            (
                (raw_h, raw),
                (scales_h, scales),
                (flat_h, flat),
                (spec_h, spec),
                (pup_h, pup),
                (half_h, half),
                (spread_h, spread),
                (gather_h, gather),
                (rows_h, rows_table),
            )
        )
    ]
    for copy in loads:
        copy.start()
    barrier = pltpu.get_barrier_semaphore()

    @pl.loop(1, tiles)
    def _(i):
        pl.semaphore_signal(
            barrier, inc=1, device_id={"tile": lax.rem(tile + i, tiles)}, device_id_type=MESH
        )

    for device in (mate, partner):
        pl.semaphore_signal(barrier, inc=1, device_id=device, device_id_type=MESH)

    loads[0].wait()
    loads[1].wait()
    dequantize(raw, scales, dequant)
    pl.semaphore_wait(barrier, tiles + 1)

    @pl.loop(1, tiles)
    def _(i):
        target = lax.rem(tile + i, tiles)
        message[target] = cut_message(dequant, target)
        block(tile, target).start()

    arrived[tile] = cut_message(dequant, tile)
    loads[2].wait()
    for k in range(BLOCKS - 1):
        gains[:, k * LANES : (k + 1) * LANES] = flat[k * LANES : (k + 1) * LANES, :].T
    tail = jnp.concatenate(
        [flat[3 * LANES :, :], jnp.zeros((TW - CORE, TH), F32)], axis=0
    ).T
    gains[:, 3 * LANES :] = tail
    flat_out[0] = pack_edge(tail, 80)
    flat_out[1] = pack_edge(gains[:, :LANES], 0)
    flats = [
        side(0, flat_out.at[0], flat_in.at[0], right),
        side(1, flat_out.at[1], flat_in.at[1], left),
    ]
    for copy in flats:
        copy.start()

    for copy in loads[3:9]:
        copy.wait()
    load_halves(spec, pup, halves, pd)
    build_band(half, cols, cols_t)
    first_frame = group * frames

    def forward(f):
        estimate[f] = forward_frame(
            f, first_frame + f, pat, lrow, lcol, halves, pd, cols, spread, picked, lit, mid, field
        )

    pl.loop(0, frames - 1)(forward)
    grad[...] = jnp.zeros_like(grad)
    build_columns(half, table)

    y, x, lane = centred()
    edge = lane[:, 3 * LANES :]
    for copy in flats:
        copy.wait_recv()
    outer = jnp.where(
        edge < CORE + MARGIN, unpack_edge(flat_in[1], 96), unpack_edge(flat_in[0], 112)
    )
    gains[:, 3 * LANES :] = jnp.where(edge < CORE, gains[:, 3 * LANES :], outer)

    @pl.loop(1, tiles + 1)
    def _(i):
        source = lax.rem(tile + tiles - i, tiles)

        @pl.when(i < tiles)
        def _():
            block(source, tile).wait_recv()

        here = pl.ds(pl.multiple_of(source * rows, rows), rows)
        values = arrived[source].astype(F32)
        for f in range(frames):
            window[f, here, :] = values[f * rows : (f + 1) * rows] * gains[here, :]

    inside = (lane < CORE).astype(F32)
    slopes = []
    for f in range(frames):
        flattened = window[f]
        columns = jnp.sum(flattened, axis=0, keepdims=True)
        tilted = jnp.sum(flattened * y, axis=0, keepdims=True)
        slope_y = jnp.sum(tilted * inside, axis=1, keepdims=True) / Y_NORM
        slope_x = jnp.sum(columns * (x * inside), axis=1, keepdims=True) / X_NORM
        slopes.append((slope_y, slope_x))
        slope_out[f : f + 1] = jnp.broadcast_to(slope_y, (1, LANES))
        slope_out[frames + f : frames + f + 1] = jnp.broadcast_to(slope_x, (1, LANES))
    copies = [side(2, slope_out, slope_in.at[0], right), side(3, slope_out, slope_in.at[1], left)]
    for copy in copies:
        copy.start()
    forward(frames - 1)
    for copy in copies:
        copy.wait_recv()
    x_edge = x[:, 3 * LANES :]
    own = edge < CORE
    after = edge < CORE + MARGIN
    blank = ((~own) & after & (tile == tiles - 1)) | ((~after) & (tile == 0))
    for f in range(frames):
        slope_y, slope_x = slopes[f]
        for k in range(BLOCKS - 1):
            cut = slice(k * LANES, (k + 1) * LANES)
            window[f, :, cut] = window[f, :, cut] - slope_y * y - slope_x * x[:, cut]
        row_y = jnp.where(
            own, slope_y, jnp.where(after, slope_in[1, f : f + 1], slope_in[0, f : f + 1])
        )
        row_x = jnp.where(
            own,
            slope_x * x_edge,
            jnp.where(
                after,
                slope_in[1, frames + f : frames + f + 1] * (x_edge - CORE),
                slope_in[0, frames + f : frames + f + 1] * (x_edge - 32.0),
            ),
        )
        value = window[f, :, 3 * LANES :] - row_y * y - row_x
        window[f, :, 3 * LANES :] = jnp.where(blank, 0.0, value)

    @pl.loop(0, frames)
    def _(f):
        misfit = estimate[f] - window[f]
        backward_frame(
            f, first_frame + f, misfit, pat, lrow, lcol, pd, cols_t, gather, field, mid, picked, grad
        )

    pieces = [(i, c) for i in (0, 1) for c in (0, 1)]
    first = [
        side(4 + n, grad.at[2 - 2 * core + i, c], got.at[i, c], mate)
        for n, (i, c) in enumerate(pieces)
    ]
    for copy in first:
        copy.start()
    second = []
    units = []
    for n, (i, c) in enumerate(pieces):
        first[n].wait_recv()
        encode(grad[2 * core + i, c] + got[i, c], code.at[n], unit.at[n])
        second.append(side(8 + n, code.at[n], far_code.at[n], partner))
        units.append(side(18 + n, unit.at[n], far_unit.at[n], partner))
        units[n].start()
        second[n].start()
    third = []
    out = []
    for i in (0, 1):
        mine = 2 * core + i
        lanes = pl.ds(pl.multiple_of(mine * LANES, LANES), LANES)
        for c in (0, 1):
            n = 2 * i + c
            units[n].wait_recv()
            second[n].wait_recv()
            total = decode(code.at[n], unit.at[n]) + decode(far_code.at[n], far_unit.at[n])
            new[mine, c] = spec[c, :, lanes] - STEP * total
            third.append(side(12 + n, new.at[mine, c], new.at[mine, c], mate))
            third[n].start()
        for c in (0, 1):
            third[2 * i + c].wait_recv()
        for k in (i, i + 2):
            out.append(
                pltpu.make_async_copy(
                    new.at[k], fresh.at[:, :, k * LANES : (k + 1) * LANES], store.at[k]
                )
            )
            out[-1].start()
        object_rows(i, new, rows_table, lhs)
        if i == 0:
            for k in range(BLOCKS):
                image[k] = object_block(i, k, lhs, table)
    image[3] += object_block(1, 3, lhs, table)
    for c in (0, 1):
        value = image[3, :, c * LANES : (c + 1) * LANES]
        edge_out[0, c] = pack_edge(value, 96)
        edge_out[1, c] = pack_edge(value, 112)
    edges = [
        side(16, edge_out.at[0], edge_in.at[0], right),
        side(17, edge_out.at[1], edge_in.at[1], left),
    ]
    for copy in edges:
        copy.start()
    for k in range(BLOCKS - 1):
        image[k] += object_block(1, k, lhs, table)
    for c in (0, 1):
        for k in (1, 2):
            strip[c, k * LANES : (k + 1) * LANES, :] = image[
                k, :, c * LANES : (c + 1) * LANES
            ].T
    place = edge.astype(F32) - float(3 * LANES)
    at_head = (place < MARGIN) & (tile > 0)
    at_tail = (place >= 80) & (place < 96) & (tile < tiles - 1)
    for copy in edges:
        copy.wait_recv()
    for c in (0, 1):
        mine = image[0, :, c * LANES : (c + 1) * LANES]
        other = unpack_edge(edge_in[0, c], 0)
        blend = mine * ((place + 16.5) / OV) + other * ((15.5 - place) / OV)
        strip[c, :LANES, :] = jnp.where(at_head, blend, mine).T
        mine = image[3, :, c * LANES : (c + 1) * LANES]
        other = unpack_edge(edge_in[1, c], 80)
        blend = mine * ((111.5 - place) / OV) + other * ((place - 79.5) / OV)
        strip[c, 3 * LANES :, :] = jnp.where(at_tail, blend, mine).T[: CORE - 3 * LANES]
        out.append(pltpu.make_async_copy(strip.at[c], stitched.at[c], store.at[4 + c]))
        out[-1].start()
    for copy in flats + copies + first + second + units + third + edges:
        copy.wait_send()

    @pl.loop(1, tiles)
    def _(i):
        block(tile, lax.rem(tile + i, tiles)).wait_send()

    for copy in out:
        copy.wait()


def update(raw, scales, flat, spectrum, pupil, patterns, led_row, led_col):
    tiles = lax.axis_size("tile")
    frames, rows, width = raw.shape
    deep = frames * rows
    tables = [jnp.asarray(t) for t in band_tables() + object_tables()]
    smem = pl.BlockSpec(memory_space=pltpu.SMEM)
    hbm = pl.BlockSpec(memory_space=pltpu.MemorySpace.HBM)
    arrays = [raw, scales, flat, spectrum, pupil] + tables
    small = (TH // 8, LANES)
    part = (2, TH, LANES)
    scratch = [pltpu.VMEM(a.shape, a.dtype) for a in arrays]
    scratch += [
        pltpu.VMEM((2, 2 * PC, 2 * TW), BF16),
        pltpu.VMEM((2, 2 * TW, 2 * PC), BF16),
        pltpu.VMEM((deep, width + 2 * LANES), F32),
        pltpu.VMEM((tiles, deep, TW), BF16),
        pltpu.VMEM((tiles, deep, TW), BF16),
        pltpu.VMEM((frames, TH, TW), F32),
        pltpu.VMEM((TH, TW), F32),
        pltpu.VMEM((2,) + small, F32),
        pltpu.VMEM((2,) + small, F32),
        pltpu.VMEM((2 * frames, LANES), F32),
        pltpu.VMEM((2, 2 * frames, LANES), F32),
        pltpu.VMEM((2, TH, 2 * TW), BF16),
        pltpu.VMEM((2, PR, PC), F32),
        pltpu.VMEM((2, LEDS * PR, 2 * TW), BF16),
        pltpu.VMEM((LEDS * PR, 2 * PC), F32),
        pltpu.VMEM((LEDS * PR, 2 * TW), F32),
        pltpu.VMEM((frames, LEDS, 2, TH, TW), F32),
        pltpu.VMEM((frames, TH, TW), F32),
        pltpu.VMEM((BLOCKS,) + part, F32),
        pltpu.VMEM((2,) + part, F32),
        pltpu.VMEM((4, TH, LANES), jnp.int16),
        pltpu.VMEM((4, TH // CODE_ROWS, LANES), F32),
        pltpu.VMEM((4, TH, LANES), jnp.int16),
        pltpu.VMEM((4, TH // CODE_ROWS, LANES), F32),
        pltpu.VMEM((BLOCKS,) + part, F32),
        pltpu.VMEM((2, 2, BLOCKS, TW, 2 * LANES), BF16),
        pltpu.VMEM((2, TH, TW), BF16),
        pltpu.VMEM((BLOCKS, TH, 2 * LANES), F32),
        pltpu.VMEM((2, CORE, TH), F32),
        pltpu.VMEM((2, 2) + small, F32),
        pltpu.VMEM((2, 2) + small, F32),
        pltpu.SemaphoreType.DMA((9,)),
        pltpu.SemaphoreType.DMA((6,)),
        pltpu.SemaphoreType.DMA((tiles,)),
        pltpu.SemaphoreType.DMA((tiles,)),
        pltpu.SemaphoreType.DMA((22,)),
        pltpu.SemaphoreType.DMA((22,)),
    ]
    return pl.pallas_call(
        functools.partial(update_kernel, tiles),
        in_specs=[smem] * 3 + [hbm] * len(arrays),
        out_specs=[hbm] * 2,
        out_shape=[
            jax.ShapeDtypeStruct((2, TH, TW), F32),
            jax.ShapeDtypeStruct((2, CORE, TH), F32),
        ],
        scratch_shapes=scratch,
        compiler_params=pltpu.CompilerParams(
            collective_id=1, has_side_effects=True, vmem_limit_bytes=62 * 2**20
        ),
        name="update",
    )(patterns, led_row, led_col, *arrays)


def hand_over(first, second, first_out, second_out, sem):
    copies = [
        pltpu.make_async_copy(src.at[c], dst.at[c], sem.at[2 * n + c])
        for n, (src, dst) in enumerate(((first, first_out), (second, second_out)))
        for c in (0, 1)
    ]
    for copy in copies:
        copy.start()
    for copy in copies:
        copy.wait()


def deliver(fresh, stitched):
    hbm = pl.BlockSpec(memory_space=pltpu.MemorySpace.HBM)
    return pl.pallas_call(
        hand_over,
        in_specs=[pl.BlockSpec(memory_space=pl.ANY)] * 2,
        out_specs=[hbm] * 2,
        out_shape=[jax.ShapeDtypeStruct(a.shape, a.dtype) for a in (fresh, stitched)],
        scratch_shapes=[pltpu.SemaphoreType.DMA((4,))],
        name="deliver",
    )(fresh, stitched)


def body(raw, scales, flat, spectrum, pupil, patterns, led_row, led_col):
    fresh, stitched = update(
        raw, scales, flat.T, spectrum[0], pupil, patterns.T, led_row, led_col
    )
    fresh, stitched = deliver(fresh, stitched)
    return (fresh[None], jnp.swapaxes(stitched, 1, 2))


def solution(mesh):
    return jax.shard_map(
        body,
        mesh=mesh,
        in_specs=(
            P("grp", "tile", None),
            P("grp", "tile", None),
            P(None, "tile"),
            P("tile", None, None, None),
            P(),
            P(),
            P(),
            P(),
        ),
        out_specs=(P("tile", None, None, None), P(None, None, "tile")),
        check_vma=False,
    )
```

```python
import functools
import math

import jax
import jax.numpy as jnp
import ml_dtypes
import numpy as np
from jax import lax
from jax.experimental import pallas as pl
from jax.experimental.pallas import tpu as pltpu
from jax.sharding import PartitionSpec as P

TH = 256
TW = 512
OV = 32
BR = 4
BC = 32
PR = 64
PC = 128
FR_G = 4
LEDS = 4
HALF = TH // 2
HR = PR // 2
MARGIN = OV // 2
CORE = TW - OV
LANES = 128
BLOCKS = TW // LANES
MESH = pl.DeviceIdType.MESH
CODE_ROWS = 32
CODE_TOP = 32767.0
STEP = 0.02
F32 = jnp.float32
BF16 = jnp.bfloat16


def split_np(table):
    hi = table.astype(ml_dtypes.bfloat16)
    lo = (table - hi.astype(np.float64)).astype(ml_dtypes.bfloat16)
    return hi, lo


def wave_np(length, band):
    places = np.arange(length)[:, None]
    freqs = np.arange(band)[None, :] - band // 2
    angle = (places * freqs % length) * (2.0 * np.pi / length)
    return np.cos(angle) / math.sqrt(band), np.sin(angle) / math.sqrt(band)


def object_tables():
    re, im = wave_np(TH, TH)
    rows = []
    for parity in (0, 1):
        a, b = re[:HALF, parity::2], im[:HALF, parity::2]
        rows.append(np.stack(split_np(np.block([[a, -b], [b, a]]))))
    re, im = (np.roll(part.T, -MARGIN, axis=1)[:TH] for part in wave_np(TW, TW))
    cols = np.stack([np.stack(split_np(re)), np.stack(split_np(im))], axis=1)
    return np.stack(rows), cols


def band_tables():
    row_re, row_im = wave_np(TH, PR)
    spread, gather = [], []
    for parity in (0, 1):
        re = row_re[:HALF, parity::2]
        im = row_im[:HALF, parity::2]
        rows_hi, rows_lo = split_np(np.block([[re, -im], [im, re]]))
        spread.append(np.concatenate([rows_hi, rows_hi, rows_lo, rows_lo], axis=1))
        gather.append(np.concatenate([rows_hi.T, rows_lo.T], axis=0))
    return np.stack(spread), np.stack(gather)


def split(x):
    hi = x.astype(BF16)
    return hi, (x - hi.astype(F32)).astype(BF16)


def dot(a, b):
    return jnp.dot(a, b, preferred_element_type=F32)


def box_corner(pat, lrow, lcol, frame, j):
    led = pat[j, frame]
    return lrow[led], lcol[led]


def row_order(index):
    return jnp.where(index < HR, 2 * index, 2 * index - (PR - 1))


def ones_where(condition):
    return jnp.where(condition, 1.0, 0.0).astype(BF16)


def column_select(col):
    x = lax.broadcasted_iota(jnp.int32, (TW, PC), 0)
    v = lax.broadcasted_iota(jnp.int32, (TW, PC), 1)
    return ones_where(x - v == col)


def column_place(col):
    v = lax.broadcasted_iota(jnp.int32, (PC, TW), 0)
    x = lax.broadcasted_iota(jnp.int32, (PC, TW), 1)
    return ones_where(x - v == col)


def load_halves(spec, pup, halves, pd):
    for c in (0, 1):
        hi, lo = split(spec[c])
        halves[0, :, c * TW : (c + 1) * TW] = hi
        halves[1, :, c * TW : (c + 1) * TW] = lo
        for parity in (0, 1):
            pd[c, parity * HR : (parity + 1) * HR] = pup[c, pl.ds(parity, HR, stride=2), :]


def forward_frame(f, frame, pat, lrow, lcol, halves, pd, cols, spread, picked, lit, mid, field):
    y = lax.broadcasted_iota(jnp.int32, (PR, TH), 1)
    order = row_order(lax.broadcasted_iota(jnp.int32, (PR, TH), 0))
    corners = [box_corner(pat, lrow, lcol, frame, j) for j in range(LEDS)]
    choose = jnp.concatenate([ones_where(y - order == row) for row, _ in corners], axis=0)
    for h in (0, 1):
        picked[h] = dot(choose, halves[h]).astype(BF16)
    p_re, p_im = pd[0], pd[1]
    for j in range(LEDS):
        rows = pl.ds(j * PR, PR)
        stack = jnp.concatenate(
            [picked[h, rows, c * TW : (c + 1) * TW] for h in (0, 1) for c in (0, 1)], axis=0
        )
        cut = dot(stack, column_select(corners[j][1]))
        b_re = cut[:PR] + cut[2 * PR : 3 * PR]
        b_im = cut[PR : 2 * PR] + cut[3 * PR :]
        lit[rows, :PC] = p_re * b_re - p_im * b_im
        lit[rows, PC:] = p_re * b_im + p_im * b_re
    hi, lo = split(lit[...])
    mid[...] = dot(hi, cols[0]) + dot(lo, cols[0]) + dot(hi, cols[1])
    estimate = None
    for j in range(LEDS):
        parts = []
        for parity in (0, 1):
            rows = pl.ds(j * PR + parity * HR, HR)
            re_hi, re_lo = split(mid[rows, :TW])
            im_hi, im_lo = split(mid[rows, TW:])
            both = jnp.concatenate([re_hi, im_hi, re_lo, im_lo], axis=0)
            parts.append(dot(spread[parity], jnp.concatenate([both, both], axis=0)))
        upper = parts[0] + parts[1]
        lower = parts[0] - parts[1]
        field[f, j, 0, :HALF] = upper[:HALF]
        field[f, j, 0, HALF:] = lower[:HALF]
        field[f, j, 1, :HALF] = upper[HALF:]
        field[f, j, 1, HALF:] = lower[HALF:]
        power = jnp.concatenate(
            [
                upper[:HALF] * upper[:HALF] + upper[HALF:] * upper[HALF:],
                lower[:HALF] * lower[:HALF] + lower[HALF:] * lower[HALF:],
            ],
            axis=0,
        )
        estimate = power if estimate is None else estimate + power
    return estimate


def backward_frame(
    f, frame, misfit, pat, lrow, lcol, pd, cols, gather, field, low, wide, grad
):
    for j in range(LEDS):
        weighted = [misfit * field[f, j, c] for c in (0, 1)]
        for parity in (0, 1):
            mix = [
                w[:HALF] + w[HALF:] if parity == 0 else w[:HALF] - w[HALF:] for w in weighted
            ]
            hi, lo = split(jnp.concatenate(mix, axis=0))
            table = gather[parity]
            first = dot(table, hi)
            total = first[:PR] + first[PR:] + dot(table[:PR], lo)
            rows = pl.ds(j * PR + parity * HR, HR)
            low[rows, :TW] = total[:HR]
            low[rows, TW:] = total[HR:]
    hi, lo = split(low[...])
    grads = dot(hi, cols[0]) + dot(lo, cols[0]) + dot(hi, cols[1])
    p_re, p_im = pd[0], pd[1]
    lane = lax.broadcasted_iota(jnp.int32, (1, LEDS * PR), 1)
    target = row_order(lane & (PR - 1))
    for j in range(LEDS):
        row, col = box_corner(pat, lrow, lcol, frame, j)
        target = target + jnp.where((lane >= j * PR) & (lane < (j + 1) * PR), row, 0)
        rows = pl.ds(j * PR, PR)
        g_re = grads[j * PR : (j + 1) * PR, :PC]
        g_im = grads[j * PR : (j + 1) * PR, PC:]
        re_hi, re_lo = split(p_re * g_re + p_im * g_im)
        im_hi, im_lo = split(p_re * g_im - p_im * g_re)
        stack = jnp.concatenate([re_hi, im_hi, re_lo, im_lo], axis=0)
        placed = dot(stack, column_place(col)).astype(BF16)
        for h in (0, 1):
            for c in (0, 1):
                n = 2 * h + c
                wide[h, rows, c * TW : (c + 1) * TW] = placed[n * PR : (n + 1) * PR]
    y = lax.broadcasted_iota(jnp.int32, (TH, LEDS * PR), 0)
    choose = ones_where(y == target)
    total = dot(choose, wide[0]) + dot(choose, wide[1])
    for c in (0, 1):
        for k in range(BLOCKS):
            first = c * TW + k * LANES
            grad[k, c] += total[:, first : first + LANES]


def pack_edge(value, first):
    lane = lax.broadcasted_iota(jnp.int32, (TH // 8, LANES), 1) // MARGIN
    packed = jnp.zeros((TH // 8, LANES), F32)
    for b in range(8):
        piece = value[b * 32 : (b + 1) * 32]
        piece = pltpu.roll(piece, (MARGIN * b - first) % LANES, 1)
        packed = jnp.where(lane == b, piece, packed)
    return packed


def unpack_edge(packed, first):
    return jnp.concatenate(
        [pltpu.roll(packed, (first - MARGIN * b) % LANES, 1) for b in range(8)], axis=0
    )


def dequantize(raw, scales, dequant):
    frames, rows, width = raw.shape
    dequant[:, :LANES] = jnp.zeros((frames * rows, LANES), F32)
    dequant[:, LANES + width :] = jnp.zeros((frames * rows, LANES), F32)
    lane = lax.broadcasted_iota(jnp.int32, (rows, LANES), 1) // BC
    upper = lax.broadcasted_iota(jnp.int32, (rows, LANES), 0) < BR
    blocks = scales.shape[2]
    per = LANES // BC
    for first in range(0, blocks, LANES):
        count = min(LANES, blocks - first)
        for f in range(frames):
            pair = scales[f, :, first : first + count].astype(F32)
            if count < LANES:
                pair = jnp.concatenate([pair, jnp.zeros((2, LANES - count), F32)], axis=1)
            factors = jnp.where(
                upper,
                jnp.broadcast_to(pair[0:1], (rows, LANES)),
                jnp.broadcast_to(pair[1:2], (rows, LANES)),
            )
            for k in range(count // per):
                column = (first // per + k) * LANES
                spread = jnp.take_along_axis(factors, lane + per * k, axis=1)
                codes = raw[f, :, column : column + LANES].astype(F32)
                dequant[f * rows : (f + 1) * rows, LANES + column : 2 * LANES + column] = (
                    codes * spread
                )


def cut_message(dequant, tile):
    start = CORE * tile - MARGIN + LANES
    aligned = pl.multiple_of(start // LANES * LANES, LANES)
    offset = start - aligned + MARGIN
    wide = dequant[:, pl.ds(aligned, TW + LANES)]
    wide = pltpu.roll(wide, TW + LANES - offset, 1)
    lane = lax.broadcasted_iota(jnp.int32, (1, LANES), 1)
    last = jnp.where(lane < LANES - MARGIN, wide[:, TW - LANES : TW], wide[:, TW:])
    return jnp.concatenate([wide[:, : TW - LANES], last], axis=1).astype(BF16)


def centred():
    y = lax.broadcasted_iota(jnp.int32, (TH, 1), 0).astype(F32) - (TH - 1) / 2.0
    lane = lax.broadcasted_iota(jnp.int32, (1, TW), 1)
    x = lane.astype(F32) - (CORE - 1) / 2.0
    return y, x, lane


Y_NORM = float(np.sum((np.arange(TH) - (TH - 1) / 2.0) ** 2) * CORE)
X_NORM = float(np.sum((np.arange(CORE) - (CORE - 1) / 2.0) ** 2) * TH)


def build_band(half, cols, cols_t):
    lane = lax.broadcasted_iota(jnp.int32, (1, TW), 1)
    sign = (2 - 4 * (lane & 1)).astype(F32)
    for h in (0, 1):
        re, im = (
            jnp.concatenate(
                [
                    half[h, c, TH - PC // 2 :, :].astype(F32) * 2.0,
                    half[h, c, : PC // 2, :].astype(F32) * sign,
                ],
                axis=0,
            )
            for c in (0, 1)
        )
        cols[h, :PC, :TW] = re.astype(BF16)
        cols[h, :PC, TW:] = im.astype(BF16)
        cols[h, PC:, :TW] = (-im).astype(BF16)
        cols[h, PC:, TW:] = re.astype(BF16)
        re, im = re.T, im.T
        cols_t[h, :TW, :PC] = re.astype(BF16)
        cols_t[h, :TW, PC:] = (-im).astype(BF16)
        cols_t[h, TW:, :PC] = im.astype(BF16)
        cols_t[h, TW:, PC:] = re.astype(BF16)


def build_columns(half, table):
    lane = lax.broadcasted_iota(jnp.int32, (1, TW), 1)
    sign = (1 - 2 * (lane & 1)).astype(F32)
    for i in (0, 1):
        rows = pl.ds(i * LANES, LANES)
        for h in (0, 1):
            re = half[h, 0, rows, :].astype(F32)
            im = half[h, 1, rows, :].astype(F32)
            for n, factor in ((0, None), (1, sign)):
                a = re if factor is None else re * factor
                b = im if factor is None else im * factor
                upper = pl.ds(n * LANES, LANES)
                lower = pl.ds((2 + n) * LANES, LANES)
                for k in range(BLOCKS):
                    cut = slice(k * LANES, (k + 1) * LANES)
                    table[i, h, k, upper, :LANES] = a[:, cut].astype(BF16)
                    table[i, h, k, upper, LANES:] = b[:, cut].astype(BF16)
                    table[i, h, k, lower, :LANES] = (-b[:, cut]).astype(BF16)
                    table[i, h, k, lower, LANES:] = a[:, cut].astype(BF16)


def object_rows(i, new, rows_table, lhs):
    parts = []
    for parity in (0, 1):
        data = [
            jnp.concatenate(
                [new[k, c, pl.ds(parity, HALF, stride=2), :] for k in (i, i + 2)], axis=1
            )
            for c in (0, 1)
        ]
        hi, lo = split(jnp.concatenate(data, axis=0))
        t_hi, t_lo = rows_table[parity, 0], rows_table[parity, 1]
        parts.append(dot(t_hi, hi) + dot(t_hi, lo) + dot(t_lo, hi))
    for n, value in enumerate((parts[0] + parts[1], parts[0] - parts[1])):
        hi, lo = split(value)
        rows = pl.ds(n * HALF, HALF)
        for h, part in enumerate((hi, lo)):
            lhs[h, rows, : 2 * LANES] = part[:HALF]
            lhs[h, rows, 2 * LANES :] = part[HALF:]


def object_block(i, k, lhs, table):
    hi, lo = lhs[0], lhs[1]
    return dot(hi, table[i, 0, k]) + dot(lo, table[i, 0, k]) + dot(hi, table[i, 1, k])


def encode(value, code, unit):
    for g in range(TH // CODE_ROWS):
        rows = slice(g * CODE_ROWS, (g + 1) * CODE_ROWS)
        piece = value[rows]
        top = jnp.max(jnp.abs(piece), axis=0, keepdims=True)
        unit[g : g + 1] = top * (1.0 / CODE_TOP)
        ratio = jnp.where(top > 0.0, CODE_TOP / top, 0.0)
        whole = jnp.clip(jnp.round(piece * ratio), -CODE_TOP, CODE_TOP)
        code[rows] = whole.astype(jnp.int32).astype(jnp.int16)


def decode(code, unit):
    return jnp.concatenate(
        [
            code[g * CODE_ROWS : (g + 1) * CODE_ROWS].astype(jnp.int32).astype(F32)
            * unit[g : g + 1]
            for g in range(TH // CODE_ROWS)
        ],
        axis=0,
    )


def update_kernel(
    tiles,
    pat_h,
    lrow_h,
    lcol_h,
    raw_h,
    scales_h,
    flat_h,
    spec_h,
    pup_h,
    spread_h,
    gather_h,
    rows_h,
    half_h,
    fresh,
    stitched,
    pat,
    lrow,
    lcol,
    raw,
    scales,
    flat,
    spec,
    pup,
    spread,
    gather,
    rows_table,
    half,
    cols,
    cols_t,
    dequant,
    message,
    arrived,
    window,
    gains,
    flat_out,
    flat_in,
    slope_out,
    slope_in,
    halves,
    pd,
    picked,
    lit,
    mid,
    field,
    estimate,
    grad,
    got,
    code,
    unit,
    far_code,
    far_unit,
    new,
    table,
    lhs,
    image,
    edge_out,
    edge_in,
    load,
    send,
    recv,
    side_send,
    side_recv,
):
    frames = raw.shape[0]
    rows = raw.shape[1]
    group = lax.axis_index("grp")
    tile = lax.axis_index("tile")
    core = lax.rem(group, 2)
    mate = {"grp": group + 1 - 2 * core}
    partner = {"grp": group + 2 - 4 * lax.div(group, 2)}
    right = {"tile": lax.rem(tile + 1, tiles)}
    left = {"tile": lax.rem(tile + tiles - 1, tiles)}

    def side(number, src, dst, device):
        return pltpu.make_async_remote_copy(
            src_ref=src,
            dst_ref=dst,
            send_sem=side_send.at[number],
            recv_sem=side_recv.at[number],
            device_id=device,
            device_id_type=MESH,
        )

    def block(source, target):
        return pltpu.make_async_remote_copy(
            src_ref=message.at[target],
            dst_ref=arrived.at[source],
            send_sem=send.at[target],
            recv_sem=recv.at[source],
            device_id={"tile": target},
            device_id_type=MESH,
        )

    loads = [
        pltpu.make_async_copy(src, dst, load.at[n])
        for n, (src, dst) in enumerate(
            (
                (raw_h, raw),
                (scales_h, scales),
                (pat_h, pat),
                (lrow_h, lrow),
                (lcol_h, lcol),
                (flat_h, flat),
                (spec_h, spec),
                (pup_h, pup),
                (half_h, half),
                (spread_h, spread),
                (gather_h, gather),
                (rows_h, rows_table),
            )
        )
    ]
    for copy in loads:
        copy.start()
    barrier = pltpu.get_barrier_semaphore()

    @pl.loop(1, tiles)
    def _(i):
        pl.semaphore_signal(
            barrier, inc=1, device_id={"tile": lax.rem(tile + i, tiles)}, device_id_type=MESH
        )

    for device in (mate, partner):
        pl.semaphore_signal(barrier, inc=1, device_id=device, device_id_type=MESH)

    loads[0].wait()
    loads[1].wait()
    dequantize(raw, scales, dequant)
    pl.semaphore_wait(barrier, tiles + 1)

    @pl.loop(1, tiles)
    def _(i):
        target = lax.rem(tile + i, tiles)
        message[target] = cut_message(dequant, target)
        block(tile, target).start()

    arrived[tile] = cut_message(dequant, tile)
    loads[5].wait()
    for k in range(BLOCKS - 1):
        gains[:, k * LANES : (k + 1) * LANES] = flat[k * LANES : (k + 1) * LANES, :].T
    tail = jnp.concatenate(
        [flat[3 * LANES :, :], jnp.zeros((TW - CORE, TH), F32)], axis=0
    ).T
    gains[:, 3 * LANES :] = tail
    flat_out[0] = pack_edge(tail, 80)
    flat_out[1] = pack_edge(gains[:, :LANES], 0)
    flats = [
        side(0, flat_out.at[0], flat_in.at[0], right),
        side(1, flat_out.at[1], flat_in.at[1], left),
    ]
    for copy in flats:
        copy.start()

    for copy in loads[2:5] + loads[6:]:
        copy.wait()
    load_halves(spec, pup, halves, pd)
    build_band(half, cols, cols_t)
    first_frame = group * frames

    def forward(f):
        estimate[f] = forward_frame(
            f, first_frame + f, pat, lrow, lcol, halves, pd, cols, spread, picked, lit, mid, field
        )

    pl.loop(0, frames - 1)(forward)
    grad[...] = jnp.zeros_like(grad)
    build_columns(half, table)

    y, x, lane = centred()
    edge = lane[:, 3 * LANES :]
    for copy in flats:
        copy.wait_recv()
    outer = jnp.where(
        edge < CORE + MARGIN, unpack_edge(flat_in[1], 96), unpack_edge(flat_in[0], 112)
    )
    gains[:, 3 * LANES :] = jnp.where(edge < CORE, gains[:, 3 * LANES :], outer)

    @pl.loop(1, tiles + 1)
    def _(i):
        source = lax.rem(tile + tiles - i, tiles)

        @pl.when(i < tiles)
        def _():
            block(source, tile).wait_recv()

        here = pl.ds(pl.multiple_of(source * rows, rows), rows)
        values = arrived[source].astype(F32)
        for f in range(frames):
            window[f, here, :] = values[f * rows : (f + 1) * rows] * gains[here, :]

    inside = (lane < CORE).astype(F32)
    slopes = []
    for f in range(frames):
        flattened = window[f]
        columns = jnp.sum(flattened, axis=0, keepdims=True)
        tilted = jnp.sum(flattened * y, axis=0, keepdims=True)
        slope_y = jnp.sum(tilted * inside, axis=1, keepdims=True) / Y_NORM
        slope_x = jnp.sum(columns * (x * inside), axis=1, keepdims=True) / X_NORM
        slopes.append((slope_y, slope_x))
        slope_out[f : f + 1] = jnp.broadcast_to(slope_y, (1, LANES))
        slope_out[frames + f : frames + f + 1] = jnp.broadcast_to(slope_x, (1, LANES))
    copies = [side(2, slope_out, slope_in.at[0], right), side(3, slope_out, slope_in.at[1], left)]
    for copy in copies:
        copy.start()
    forward(frames - 1)
    for copy in copies:
        copy.wait_recv()
    x_edge = x[:, 3 * LANES :]
    own = edge < CORE
    after = edge < CORE + MARGIN
    blank = ((~own) & after & (tile == tiles - 1)) | ((~after) & (tile == 0))
    for f in range(frames):
        slope_y, slope_x = slopes[f]
        for k in range(BLOCKS - 1):
            cut = slice(k * LANES, (k + 1) * LANES)
            window[f, :, cut] = window[f, :, cut] - slope_y * y - slope_x * x[:, cut]
        row_y = jnp.where(
            own, slope_y, jnp.where(after, slope_in[1, f : f + 1], slope_in[0, f : f + 1])
        )
        row_x = jnp.where(
            own,
            slope_x * x_edge,
            jnp.where(
                after,
                slope_in[1, frames + f : frames + f + 1] * (x_edge - CORE),
                slope_in[0, frames + f : frames + f + 1] * (x_edge - 32.0),
            ),
        )
        value = window[f, :, 3 * LANES :] - row_y * y - row_x
        window[f, :, 3 * LANES :] = jnp.where(blank, 0.0, value)

    @pl.loop(0, frames)
    def _(f):
        misfit = estimate[f] - window[f]
        backward_frame(
            f, first_frame + f, misfit, pat, lrow, lcol, pd, cols_t, gather, field, mid, picked, grad
        )

    pieces = [(i, c) for i in (0, 1) for c in (0, 1)]
    first = [
        side(4 + n, grad.at[2 - 2 * core + i, c], got.at[i, c], mate)
        for n, (i, c) in enumerate(pieces)
    ]
    for copy in first:
        copy.start()
    second = []
    units = []
    for n, (i, c) in enumerate(pieces):
        first[n].wait_recv()
        encode(grad[2 * core + i, c] + got[i, c], code.at[n], unit.at[n])
        second.append(side(8 + n, code.at[n], far_code.at[n], partner))
        units.append(side(18 + n, unit.at[n], far_unit.at[n], partner))
        units[n].start()
        second[n].start()
    third = []
    for i in (0, 1):
        mine = 2 * core + i
        lanes = pl.ds(pl.multiple_of(mine * LANES, LANES), LANES)
        for c in (0, 1):
            n = 2 * i + c
            units[n].wait_recv()
            second[n].wait_recv()
            total = decode(code.at[n], unit.at[n]) + decode(far_code.at[n], far_unit.at[n])
            new[mine, c] = spec[c, :, lanes] - STEP * total
            third.append(side(12 + n, new.at[mine, c], new.at[mine, c], mate))
            third[n].start()
        for c in (0, 1):
            third[2 * i + c].wait_recv()
        for k in (i, i + 2):
            fresh[:, :, k * LANES : (k + 1) * LANES] = new[k]
        object_rows(i, new, rows_table, lhs)
        if i == 0:
            for k in range(BLOCKS):
                image[k] = object_block(i, k, lhs, table)
    image[3] += object_block(1, 3, lhs, table)
    for c in (0, 1):
        value = image[3, :, c * LANES : (c + 1) * LANES]
        edge_out[0, c] = pack_edge(value, 96)
        edge_out[1, c] = pack_edge(value, 112)
    edges = [
        side(16, edge_out.at[0], edge_in.at[0], right),
        side(17, edge_out.at[1], edge_in.at[1], left),
    ]
    for copy in edges:
        copy.start()
    for k in range(BLOCKS - 1):
        image[k] += object_block(1, k, lhs, table)
    for c in (0, 1):
        for k in (1, 2):
            stitched[c, k * LANES : (k + 1) * LANES, :] = image[
                k, :, c * LANES : (c + 1) * LANES
            ].T
    place = edge.astype(F32) - float(3 * LANES)
    at_head = (place < MARGIN) & (tile > 0)
    at_tail = (place >= 80) & (place < 96) & (tile < tiles - 1)
    for copy in edges:
        copy.wait_recv()
    for c in (0, 1):
        mine = image[0, :, c * LANES : (c + 1) * LANES]
        other = unpack_edge(edge_in[0, c], 0)
        blend = mine * ((place + 16.5) / OV) + other * ((15.5 - place) / OV)
        stitched[c, :LANES, :] = jnp.where(at_head, blend, mine).T
        mine = image[3, :, c * LANES : (c + 1) * LANES]
        other = unpack_edge(edge_in[1, c], 80)
        blend = mine * ((111.5 - place) / OV) + other * ((place - 79.5) / OV)
        stitched[c, 3 * LANES :, :] = jnp.where(at_tail, blend, mine).T[: CORE - 3 * LANES]
    for copy in flats + copies + first + second + units + third + edges:
        copy.wait_send()

    @pl.loop(1, tiles)
    def _(i):
        block(tile, lax.rem(tile + i, tiles)).wait_send()


def update(raw, scales, flat, spectrum, pupil, patterns, led_row, led_col):
    tiles = lax.axis_size("tile")
    frames, rows, width = raw.shape
    deep = frames * rows
    tables = [jnp.asarray(t) for t in band_tables() + object_tables()]
    picks = [patterns, led_row, led_col]
    hbm = pl.BlockSpec(memory_space=pltpu.MemorySpace.HBM)
    arrays = [
        pltpu.with_memory_space_constraint(a, pltpu.MemorySpace.HBM)
        for a in picks + [raw, scales, flat, spectrum, pupil] + tables
    ]
    small = (TH // 8, LANES)
    part = (2, TH, LANES)
    scratch = [pltpu.SMEM(a.shape, a.dtype) for a in picks]
    scratch += [pltpu.VMEM(a.shape, a.dtype) for a in arrays[3:]]
    scratch += [
        pltpu.VMEM((2, 2 * PC, 2 * TW), BF16),
        pltpu.VMEM((2, 2 * TW, 2 * PC), BF16),
        pltpu.VMEM((deep, width + 2 * LANES), F32),
        pltpu.VMEM((tiles, deep, TW), BF16),
        pltpu.VMEM((tiles, deep, TW), BF16),
        pltpu.VMEM((frames, TH, TW), F32),
        pltpu.VMEM((TH, TW), F32),
        pltpu.VMEM((2,) + small, F32),
        pltpu.VMEM((2,) + small, F32),
        pltpu.VMEM((2 * frames, LANES), F32),
        pltpu.VMEM((2, 2 * frames, LANES), F32),
        pltpu.VMEM((2, TH, 2 * TW), BF16),
        pltpu.VMEM((2, PR, PC), F32),
        pltpu.VMEM((2, LEDS * PR, 2 * TW), BF16),
        pltpu.VMEM((LEDS * PR, 2 * PC), F32),
        pltpu.VMEM((LEDS * PR, 2 * TW), F32),
        pltpu.VMEM((frames, LEDS, 2, TH, TW), F32),
        pltpu.VMEM((frames, TH, TW), F32),
        pltpu.VMEM((BLOCKS,) + part, F32),
        pltpu.VMEM((2,) + part, F32),
        pltpu.VMEM((4, TH, LANES), jnp.int16),
        pltpu.VMEM((4, TH // CODE_ROWS, LANES), F32),
        pltpu.VMEM((4, TH, LANES), jnp.int16),
        pltpu.VMEM((4, TH // CODE_ROWS, LANES), F32),
        pltpu.VMEM((BLOCKS,) + part, F32),
        pltpu.VMEM((2, 2, BLOCKS, TW, 2 * LANES), BF16),
        pltpu.VMEM((2, TH, TW), BF16),
        pltpu.VMEM((BLOCKS, TH, 2 * LANES), F32),
        pltpu.VMEM((2, 2) + small, F32),
        pltpu.VMEM((2, 2) + small, F32),
        pltpu.SemaphoreType.DMA((12,)),
        pltpu.SemaphoreType.DMA((tiles,)),
        pltpu.SemaphoreType.DMA((tiles,)),
        pltpu.SemaphoreType.DMA((22,)),
        pltpu.SemaphoreType.DMA((22,)),
    ]
    return pl.pallas_call(
        functools.partial(update_kernel, tiles),
        in_specs=[hbm] * len(arrays),
        out_specs=[pl.BlockSpec(memory_space=pltpu.VMEM)] * 2,
        out_shape=[
            jax.ShapeDtypeStruct((2, TH, TW), F32),
            jax.ShapeDtypeStruct((2, CORE, TH), F32),
        ],
        scratch_shapes=scratch,
        compiler_params=pltpu.CompilerParams(
            collective_id=1, has_side_effects=True, vmem_limit_bytes=48 * 2**20
        ),
        name="update",
    )(*arrays)


def hand_over(first, second, first_out, second_out, sem):
    copies = [
        pltpu.make_async_copy(src.at[c], dst.at[c], sem.at[2 * n + c])
        for n, (src, dst) in enumerate(((first, first_out), (second, second_out)))
        for c in (0, 1)
    ]
    for copy in copies:
        copy.start()
    for copy in copies:
        copy.wait()


def deliver(fresh, stitched):
    hbm = pl.BlockSpec(memory_space=pltpu.MemorySpace.HBM)
    return pl.pallas_call(
        hand_over,
        in_specs=[pl.BlockSpec(memory_space=pltpu.VMEM)] * 2,
        out_specs=[hbm] * 2,
        out_shape=[jax.ShapeDtypeStruct(a.shape, a.dtype) for a in (fresh, stitched)],
        scratch_shapes=[pltpu.SemaphoreType.DMA((4,))],
        compiler_params=pltpu.CompilerParams(vmem_limit_bytes=4 * 2**20),
        name="deliver",
    )(fresh, stitched)


def body(raw, scales, flat, spectrum, pupil, patterns, led_row, led_col):
    fresh, stitched = update(
        raw, scales, flat.T, spectrum[0], pupil, patterns.T, led_row, led_col
    )
    fresh, stitched = deliver(fresh, stitched)
    return (fresh[None], jnp.swapaxes(stitched, 1, 2))


def solution(mesh):
    return jax.shard_map(
        body,
        mesh=mesh,
        in_specs=(
            P("grp", "tile", None),
            P("grp", "tile", None),
            P(None, "tile"),
            P("tile", None, None, None),
            P(),
            P(),
            P(),
            P(),
        ),
        out_specs=(P("tile", None, None, None), P(None, None, "tile")),
        check_vma=False,
    )
```

```python
import functools
import math

import jax
import jax.numpy as jnp
import ml_dtypes
import numpy as np
from jax import lax
from jax.experimental import pallas as pl
from jax.experimental.pallas import tpu as pltpu
from jax.sharding import PartitionSpec as P

TH = 256
TW = 512
OV = 32
BR = 4
BC = 32
PR = 64
PC = 128
FR_G = 4
LEDS = 4
HALF = TH // 2
HR = PR // 2
MARGIN = OV // 2
CORE = TW - OV
LANES = 128
BLOCKS = TW // LANES
MESH = pl.DeviceIdType.MESH
CODE_ROWS = 32
CODE_TOP = 32767.0
STEP = 0.02
F32 = jnp.float32
BF16 = jnp.bfloat16


def split_np(table):
    hi = table.astype(ml_dtypes.bfloat16)
    lo = (table - hi.astype(np.float64)).astype(ml_dtypes.bfloat16)
    return hi, lo


def wave_np(length, band):
    places = np.arange(length)[:, None]
    freqs = np.arange(band)[None, :] - band // 2
    angle = (places * freqs % length) * (2.0 * np.pi / length)
    return np.cos(angle) / math.sqrt(band), np.sin(angle) / math.sqrt(band)


def object_tables():
    re, im = wave_np(TH, TH)
    rows = []
    for parity in (0, 1):
        a, b = re[:HALF, parity::2], im[:HALF, parity::2]
        rows.append(np.stack(split_np(np.block([[a, -b], [b, a]]))))
    re, im = (np.roll(part.T, -MARGIN, axis=1)[:TH] for part in wave_np(TW, TW))
    cols = np.stack([np.stack(split_np(re)), np.stack(split_np(im))], axis=1)
    return np.stack(rows), cols


def band_tables():
    row_re, row_im = wave_np(TH, PR)
    spread = []
    for parity in (0, 1):
        re = row_re[:HALF, parity::2]
        im = row_im[:HALF, parity::2]
        rows_hi, rows_lo = split_np(np.block([[re, -im], [im, re]]))
        spread.append(np.concatenate([rows_hi, rows_hi, rows_lo, rows_lo], axis=1))
    order = np.concatenate([np.arange(0, PR, 2), np.arange(1, PR, 2)])
    gather = np.concatenate(split_np(np.concatenate([row_re.T[order], row_im.T[order]])))
    return np.stack(spread), gather


def split(x):
    hi = x.astype(BF16)
    return hi, (x - hi.astype(F32)).astype(BF16)


def dot(a, b):
    return jnp.dot(a, b, preferred_element_type=F32)


def box_corner(pat, lrow, lcol, frame, j):
    led = pat[j, frame]
    return lrow[led], lcol[led]


def row_order(index):
    return jnp.where(index < HR, 2 * index, 2 * index - (PR - 1))


def ones_where(condition):
    return jnp.where(condition, 1.0, 0.0).astype(BF16)


def column_select(col):
    x = lax.broadcasted_iota(jnp.int32, (TW, PC), 0)
    v = lax.broadcasted_iota(jnp.int32, (TW, PC), 1)
    return ones_where(x - v == col)


def column_place(col):
    v = lax.broadcasted_iota(jnp.int32, (PC, TW), 0)
    v = jnp.where(v < PC // 2, 2 * v, 2 * v - (PC - 1))
    x = lax.broadcasted_iota(jnp.int32, (PC, TW), 1)
    return ones_where(x - v == col)


def load_halves(spec, pup, halves, pd):
    for c in (0, 1):
        hi, lo = split(spec[c])
        halves[0, :, c * TW : (c + 1) * TW] = hi
        halves[1, :, c * TW : (c + 1) * TW] = lo
        for parity in (0, 1):
            pd[c, parity * HR : (parity + 1) * HR] = pup[c, pl.ds(parity, HR, stride=2), :]


def forward_frame(f, frame, pat, lrow, lcol, halves, pd, cols, spread, picked, lit, mid, field):
    y = lax.broadcasted_iota(jnp.int32, (PR, TH), 1)
    order = row_order(lax.broadcasted_iota(jnp.int32, (PR, TH), 0))
    corners = [box_corner(pat, lrow, lcol, frame, j) for j in range(LEDS)]
    choose = jnp.concatenate([ones_where(y - order == row) for row, _ in corners], axis=0)
    for h in (0, 1):
        picked[h, : LEDS * PR] = dot(choose, halves[h]).astype(BF16)
    p_re, p_im = pd[0], pd[1]
    for j in range(LEDS):
        rows = pl.ds(j * PR, PR)
        stack = jnp.concatenate(
            [picked[h, rows, c * TW : (c + 1) * TW] for h in (0, 1) for c in (0, 1)], axis=0
        )
        cut = dot(stack, column_select(corners[j][1]))
        b_re = cut[:PR] + cut[2 * PR : 3 * PR]
        b_im = cut[PR : 2 * PR] + cut[3 * PR :]
        lit[rows, :PC] = p_re * b_re - p_im * b_im
        lit[rows, PC:] = p_re * b_im + p_im * b_re
    hi, lo = split(lit[...])
    mid[...] = dot(hi, cols[0]) + dot(lo, cols[0]) + dot(hi, cols[1])
    estimate = None
    for j in range(LEDS):
        parts = []
        for parity in (0, 1):
            rows = pl.ds(j * PR + parity * HR, HR)
            re_hi, re_lo = split(mid[rows, :TW])
            im_hi, im_lo = split(mid[rows, TW:])
            both = jnp.concatenate([re_hi, im_hi, re_lo, im_lo], axis=0)
            parts.append(dot(spread[parity], jnp.concatenate([both, both], axis=0)))
        upper = parts[0] + parts[1]
        lower = parts[0] - parts[1]
        field[f, j, 0, :HALF] = upper[:HALF]
        field[f, j, 0, HALF:] = lower[:HALF]
        field[f, j, 1, :HALF] = upper[HALF:]
        field[f, j, 1, HALF:] = lower[HALF:]
        power = jnp.concatenate(
            [
                upper[:HALF] * upper[:HALF] + upper[HALF:] * upper[HALF:],
                lower[:HALF] * lower[:HALF] + lower[HALF:] * lower[HALF:],
            ],
            axis=0,
        )
        estimate = power if estimate is None else estimate + power
    return estimate


def backward_frame(f, frame, misfit, pat, lrow, lcol, pairs, fold, gather, field, bands, wide):
    for j in range(LEDS):
        weighted = [misfit * field[f, j, c] for c in (0, 1)]
        for parity in (0, 1):
            mix = [
                w[:, :TH] + w[:, TH:] if parity == 0 else w[:, :TH] - w[:, TH:]
                for w in weighted
            ]
            hi, lo = split(jnp.concatenate(mix, axis=1))
            first = dot(hi, fold[parity])
            total = first[:, :LANES] + first[:, LANES:] + dot(lo, fold[parity, :, :LANES])
            hi, lo = split(total)
            cut = slice((2 * j + parity) * LANES, (2 * j + parity + 1) * LANES)
            bands[0, :, cut] = hi
            bands[1, :, cut] = lo
    first = dot(gather[...], bands[0])
    second = dot(gather[: 2 * PR], bands[1])
    by_re = first[:PR] + first[2 * PR : 3 * PR] + second[:PR]
    by_im = first[PR : 2 * PR] + first[3 * PR :] + second[PR:]
    left = lax.broadcasted_iota(jnp.int32, (1, LANES), 1) < LANES // 2
    sign = jnp.where(left, 1.0, -1.0)
    turn = LANES // 2
    for j in range(LEDS):
        col = box_corner(pat, lrow, lcol, frame, j)[1]
        halves = []
        for parity in (0, 1):
            cut = slice((2 * j + parity) * LANES, (2 * j + parity + 1) * LANES)
            band = by_re[:, cut] + sign * pltpu.roll(by_im[:, cut], turn, 1)
            halves.append(
                pairs[0, parity] * band + sign * pairs[1, parity] * pltpu.roll(band, turn, 1)
            )
        even, odd = halves
        re_hi, re_lo = split(jnp.where(left, even, pltpu.roll(odd, turn, 1)))
        im_hi, im_lo = split(jnp.where(left, pltpu.roll(even, turn, 1), odd))
        stack = jnp.concatenate([re_hi, im_hi, re_lo, im_lo], axis=0)
        placed = dot(stack, column_place(col)).astype(BF16)
        rows = pl.ds(pl.multiple_of((f * LEDS + j) * PR, PR), PR)
        for h in (0, 1):
            for c in (0, 1):
                n = 2 * h + c
                wide[h, rows, c * TW : (c + 1) * TW] = placed[n * PR : (n + 1) * PR]


def place_rows(first_frame, frames, pat, lrow, lcol, wide, grad):
    total_rows = frames * LEDS * PR
    lane = lax.broadcasted_iota(jnp.int32, (1, total_rows), 1)
    box = lane // PR
    target = row_order(lane & (PR - 1))
    for f in range(frames):
        for j in range(LEDS):
            row = box_corner(pat, lrow, lcol, first_frame + f, j)[0]
            target = target + jnp.where(box == f * LEDS + j, row, 0)
    choose = ones_where(lax.broadcasted_iota(jnp.int32, (TH, total_rows), 0) == target)
    for k in range(BLOCKS):
        for c in (0, 1):
            cut = slice(c * TW + k * LANES, c * TW + (k + 1) * LANES)
            if k % 2 == 0:
                cut = slice(cut.start, cut.stop + LANES)
                both = dot(choose, wide[0, :, cut]) + dot(choose, wide[1, :, cut])
                grad[k, c] = both[:, :LANES]
                grad[k + 1, c] = both[:, LANES:]


def pack_edge(value, first):
    lane = lax.broadcasted_iota(jnp.int32, (TH // 8, LANES), 1) // MARGIN
    packed = jnp.zeros((TH // 8, LANES), F32)
    for b in range(8):
        piece = value[b * 32 : (b + 1) * 32]
        piece = pltpu.roll(piece, (MARGIN * b - first) % LANES, 1)
        packed = jnp.where(lane == b, piece, packed)
    return packed


def unpack_edge(packed, first):
    return jnp.concatenate(
        [pltpu.roll(packed, (first - MARGIN * b) % LANES, 1) for b in range(8)], axis=0
    )


def dequantize(raw, scales, dequant):
    frames, rows, width = raw.shape
    dequant[:, :LANES] = jnp.zeros((frames * rows, LANES), F32)
    dequant[:, LANES + width :] = jnp.zeros((frames * rows, LANES), F32)
    lane = lax.broadcasted_iota(jnp.int32, (rows, LANES), 1) // BC
    upper = lax.broadcasted_iota(jnp.int32, (rows, LANES), 0) < BR
    blocks = scales.shape[2]
    per = LANES // BC
    for first in range(0, blocks, LANES):
        count = min(LANES, blocks - first)
        for f in range(frames):
            pair = scales[f, :, first : first + count].astype(F32)
            if count < LANES:
                pair = jnp.concatenate([pair, jnp.zeros((2, LANES - count), F32)], axis=1)
            factors = jnp.where(
                upper,
                jnp.broadcast_to(pair[0:1], (rows, LANES)),
                jnp.broadcast_to(pair[1:2], (rows, LANES)),
            )
            for k in range(count // per):
                column = (first // per + k) * LANES
                spread = jnp.take_along_axis(factors, lane + per * k, axis=1)
                codes = raw[f, :, column : column + LANES].astype(F32)
                dequant[f * rows : (f + 1) * rows, LANES + column : 2 * LANES + column] = (
                    codes * spread
                )


def cut_message(dequant, tile):
    start = CORE * tile - MARGIN + LANES
    aligned = pl.multiple_of(start // LANES * LANES, LANES)
    offset = start - aligned + MARGIN
    wide = dequant[:, pl.ds(aligned, TW + LANES)]
    wide = pltpu.roll(wide, TW + LANES - offset, 1)
    lane = lax.broadcasted_iota(jnp.int32, (1, LANES), 1)
    last = jnp.where(lane < LANES - MARGIN, wide[:, TW - LANES : TW], wide[:, TW:])
    return jnp.concatenate([wide[:, : TW - LANES], last], axis=1).astype(BF16)


def centred():
    y = lax.broadcasted_iota(jnp.int32, (TH, 1), 0).astype(F32) - (TH - 1) / 2.0
    lane = lax.broadcasted_iota(jnp.int32, (1, TW), 1)
    x = lane.astype(F32) - (CORE - 1) / 2.0
    return y, x, lane


Y_NORM = float(np.sum((np.arange(TH) - (TH - 1) / 2.0) ** 2) * CORE)
X_NORM = float(np.sum((np.arange(CORE) - (CORE - 1) / 2.0) ** 2) * TH)


def parity_pick(parity):
    v = lax.broadcasted_iota(jnp.int32, (PC, LANES), 0)
    lane = lax.broadcasted_iota(jnp.int32, (PC, LANES), 1)
    return ones_where(v == 2 * (lane & (PC // 2 - 1)) + parity)


def build_band(half, pd, cols, fold, pairs):
    lane = lax.broadcasted_iota(jnp.int32, (1, TW), 1)
    sign = (2 - 4 * (lane & 1)).astype(F32)
    left = lane[:, :LANES] < LANES // 2
    for h in (0, 1):
        re, im = (
            jnp.concatenate(
                [
                    half[h, c, TH - PC // 2 :, :].astype(F32) * 2.0,
                    half[h, c, : PC // 2, :].astype(F32) * sign,
                ],
                axis=0,
            )
            for c in (0, 1)
        )
        cols[h, :PC, :TW] = re.astype(BF16)
        cols[h, :PC, TW:] = im.astype(BF16)
        cols[h, PC:, :TW] = (-im).astype(BF16)
        cols[h, PC:, TW:] = re.astype(BF16)
        turned = [part[:, :TH].T.astype(BF16) for part in (re, im)]
        for parity in (0, 1):
            a, b = (dot(part, parity_pick(parity)) for part in turned)
            cut = slice(h * LANES, (h + 1) * LANES)
            fold[parity, :TH, cut] = jnp.where(left, a, -b).astype(BF16)
            fold[parity, TH:, cut] = jnp.where(left, b, a).astype(BF16)
    for c in (0, 1):
        hi = pd[c].astype(BF16)
        lo, last = split(pd[c] - hi.astype(F32))
        for parity in (0, 1):
            pick = parity_pick(parity)
            pairs[c, parity] = dot(hi, pick) + dot(lo, pick) + dot(last, pick)


def build_columns(half, table):
    lane = lax.broadcasted_iota(jnp.int32, (1, TW), 1)
    sign = (1 - 2 * (lane & 1)).astype(F32)
    for i in (0, 1):
        rows = pl.ds(i * LANES, LANES)
        for h in (0, 1):
            re = half[h, 0, rows, :].astype(F32)
            im = half[h, 1, rows, :].astype(F32)
            for n, factor in ((0, None), (1, sign)):
                a = re if factor is None else re * factor
                b = im if factor is None else im * factor
                upper = pl.ds(n * LANES, LANES)
                lower = pl.ds((2 + n) * LANES, LANES)
                for k in range(BLOCKS):
                    cut = slice(k * LANES, (k + 1) * LANES)
                    table[i, h, k, upper, :LANES] = a[:, cut].astype(BF16)
                    table[i, h, k, upper, LANES:] = b[:, cut].astype(BF16)
                    table[i, h, k, lower, :LANES] = (-b[:, cut]).astype(BF16)
                    table[i, h, k, lower, LANES:] = a[:, cut].astype(BF16)


def object_rows(i, new, rows_table, lhs):
    parts = []
    for parity in (0, 1):
        data = [
            jnp.concatenate(
                [new[k, c, pl.ds(parity, HALF, stride=2), :] for k in (i, i + 2)], axis=1
            )
            for c in (0, 1)
        ]
        hi, lo = split(jnp.concatenate(data, axis=0))
        t_hi, t_lo = rows_table[parity, 0], rows_table[parity, 1]
        parts.append(dot(t_hi, hi) + dot(t_hi, lo) + dot(t_lo, hi))
    for n, value in enumerate((parts[0] + parts[1], parts[0] - parts[1])):
        hi, lo = split(value)
        rows = pl.ds(n * HALF, HALF)
        for h, part in enumerate((hi, lo)):
            lhs[h, rows, : 2 * LANES] = part[:HALF]
            lhs[h, rows, 2 * LANES :] = part[HALF:]


def object_block(i, k, lhs, table):
    hi, lo = lhs[0], lhs[1]
    return dot(hi, table[i, 0, k]) + dot(lo, table[i, 0, k]) + dot(hi, table[i, 1, k])


def encode(value, code, unit):
    for g in range(TH // CODE_ROWS):
        rows = slice(g * CODE_ROWS, (g + 1) * CODE_ROWS)
        piece = value[rows]
        top = jnp.max(jnp.abs(piece), axis=0, keepdims=True)
        unit[g : g + 1] = top * (1.0 / CODE_TOP)
        ratio = jnp.where(top > 0.0, CODE_TOP / top, 0.0)
        whole = jnp.clip(jnp.round(piece * ratio), -CODE_TOP, CODE_TOP)
        code[rows] = whole.astype(jnp.int32).astype(jnp.int16)


def decode(code, unit):
    return jnp.concatenate(
        [
            code[g * CODE_ROWS : (g + 1) * CODE_ROWS].astype(jnp.int32).astype(F32)
            * unit[g : g + 1]
            for g in range(TH // CODE_ROWS)
        ],
        axis=0,
    )


def update_kernel(
    tiles,
    pat_h,
    lrow_h,
    lcol_h,
    raw_h,
    scales_h,
    flat_h,
    spec_h,
    pup_h,
    spread_h,
    gather_h,
    rows_h,
    half_h,
    fresh,
    stitched,
    pat,
    lrow,
    lcol,
    raw,
    scales,
    flat,
    spec,
    pup,
    spread,
    gather,
    rows_table,
    half,
    cols,
    fold,
    pairs,
    bands,
    dequant,
    message,
    arrived,
    window,
    gains,
    flat_out,
    flat_in,
    slope_out,
    slope_in,
    halves,
    pd,
    wide,
    lit,
    mid,
    field,
    estimate,
    grad,
    got,
    code,
    unit,
    far_code,
    far_unit,
    new,
    table,
    lhs,
    image,
    edge_out,
    edge_in,
    load,
    send,
    recv,
    side_send,
    side_recv,
):
    frames = raw.shape[0]
    rows = raw.shape[1]
    group = lax.axis_index("grp")
    tile = lax.axis_index("tile")
    core = lax.rem(group, 2)
    mate = {"grp": group + 1 - 2 * core}
    partner = {"grp": group + 2 - 4 * lax.div(group, 2)}
    right = {"tile": lax.rem(tile + 1, tiles)}
    left = {"tile": lax.rem(tile + tiles - 1, tiles)}

    def side(number, src, dst, device):
        return pltpu.make_async_remote_copy(
            src_ref=src,
            dst_ref=dst,
            send_sem=side_send.at[number],
            recv_sem=side_recv.at[number],
            device_id=device,
            device_id_type=MESH,
        )

    def block(source, target):
        return pltpu.make_async_remote_copy(
            src_ref=message.at[target],
            dst_ref=arrived.at[source],
            send_sem=send.at[target],
            recv_sem=recv.at[source],
            device_id={"tile": target},
            device_id_type=MESH,
        )

    loads = [
        pltpu.make_async_copy(src, dst, load.at[n])
        for n, (src, dst) in enumerate(
            (
                (raw_h, raw),
                (scales_h, scales),
                (pat_h, pat),
                (lrow_h, lrow),
                (lcol_h, lcol),
                (flat_h, flat),
                (spec_h, spec),
                (pup_h, pup),
                (half_h, half),
                (spread_h, spread),
                (gather_h, gather),
                (rows_h, rows_table),
            )
        )
    ]
    for copy in loads:
        copy.start()
    barrier = pltpu.get_barrier_semaphore()

    @pl.loop(1, tiles)
    def _(i):
        pl.semaphore_signal(
            barrier, inc=1, device_id={"tile": lax.rem(tile + i, tiles)}, device_id_type=MESH
        )

    for device in (mate, partner):
        pl.semaphore_signal(barrier, inc=1, device_id=device, device_id_type=MESH)

    loads[0].wait()
    loads[1].wait()
    dequantize(raw, scales, dequant)
    pl.semaphore_wait(barrier, tiles + 1)

    @pl.loop(1, tiles)
    def _(i):
        target = lax.rem(tile + i, tiles)
        message[target] = cut_message(dequant, target)
        block(tile, target).start()

    arrived[tile] = cut_message(dequant, tile)
    loads[5].wait()
    for k in range(BLOCKS - 1):
        gains[:, k * LANES : (k + 1) * LANES] = flat[k * LANES : (k + 1) * LANES, :].T
    tail = jnp.concatenate(
        [flat[3 * LANES :, :], jnp.zeros((TW - CORE, TH), F32)], axis=0
    ).T
    gains[:, 3 * LANES :] = tail
    flat_out[0] = pack_edge(tail, 80)
    flat_out[1] = pack_edge(gains[:, :LANES], 0)
    flats = [
        side(0, flat_out.at[0], flat_in.at[0], right),
        side(1, flat_out.at[1], flat_in.at[1], left),
    ]
    for copy in flats:
        copy.start()

    for copy in loads[2:5] + loads[6:]:
        copy.wait()
    load_halves(spec, pup, halves, pd)
    build_band(half, pd, cols, fold, pairs)
    first_frame = group * frames

    def forward(f):
        estimate[f] = forward_frame(
            f, first_frame + f, pat, lrow, lcol, halves, pd, cols, spread, wide, lit, mid, field
        )

    pl.loop(0, frames - 1)(forward)
    build_columns(half, table)

    y, x, lane = centred()
    edge = lane[:, 3 * LANES :]
    for copy in flats:
        copy.wait_recv()
    outer = jnp.where(
        edge < CORE + MARGIN, unpack_edge(flat_in[1], 96), unpack_edge(flat_in[0], 112)
    )
    gains[:, 3 * LANES :] = jnp.where(edge < CORE, gains[:, 3 * LANES :], outer)

    @pl.loop(1, tiles + 1)
    def _(i):
        source = lax.rem(tile + tiles - i, tiles)

        @pl.when(i < tiles)
        def _():
            block(source, tile).wait_recv()

        here = pl.ds(pl.multiple_of(source * rows, rows), rows)
        values = arrived[source].astype(F32)
        for f in range(frames):
            window[f, here, :] = values[f * rows : (f + 1) * rows] * gains[here, :]

    inside = (lane < CORE).astype(F32)
    slopes = []
    for f in range(frames):
        flattened = window[f]
        columns = jnp.sum(flattened, axis=0, keepdims=True)
        tilted = jnp.sum(flattened * y, axis=0, keepdims=True)
        slope_y = jnp.sum(tilted * inside, axis=1, keepdims=True) / Y_NORM
        slope_x = jnp.sum(columns * (x * inside), axis=1, keepdims=True) / X_NORM
        slopes.append((slope_y, slope_x))
        slope_out[f : f + 1] = jnp.broadcast_to(slope_y, (1, LANES))
        slope_out[frames + f : frames + f + 1] = jnp.broadcast_to(slope_x, (1, LANES))
    copies = [side(2, slope_out, slope_in.at[0], right), side(3, slope_out, slope_in.at[1], left)]
    for copy in copies:
        copy.start()
    forward(frames - 1)
    for copy in copies:
        copy.wait_recv()
    x_edge = x[:, 3 * LANES :]
    own = edge < CORE
    after = edge < CORE + MARGIN
    blank = ((~own) & after & (tile == tiles - 1)) | ((~after) & (tile == 0))
    for f in range(frames):
        slope_y, slope_x = slopes[f]
        for k in range(BLOCKS - 1):
            cut = slice(k * LANES, (k + 1) * LANES)
            window[f, :, cut] = window[f, :, cut] - slope_y * y - slope_x * x[:, cut]
        row_y = jnp.where(
            own, slope_y, jnp.where(after, slope_in[1, f : f + 1], slope_in[0, f : f + 1])
        )
        row_x = jnp.where(
            own,
            slope_x * x_edge,
            jnp.where(
                after,
                slope_in[1, frames + f : frames + f + 1] * (x_edge - CORE),
                slope_in[0, frames + f : frames + f + 1] * (x_edge - 32.0),
            ),
        )
        value = window[f, :, 3 * LANES :] - row_y * y - row_x
        window[f, :, 3 * LANES :] = jnp.where(blank, 0.0, value)

    @pl.loop(0, frames)
    def _(f):
        misfit = estimate[f] - window[f]
        backward_frame(
            f, first_frame + f, misfit, pat, lrow, lcol, pairs, fold, gather, field, bands, wide
        )

    place_rows(first_frame, frames, pat, lrow, lcol, wide, grad)

    pieces = [(i, c) for i in (0, 1) for c in (0, 1)]
    first = [
        side(4 + n, grad.at[2 - 2 * core + i, c], got.at[i, c], mate)
        for n, (i, c) in enumerate(pieces)
    ]
    for copy in first:
        copy.start()
    second = []
    units = []
    for n, (i, c) in enumerate(pieces):
        first[n].wait_recv()
        encode(grad[2 * core + i, c] + got[i, c], code.at[n], unit.at[n])
        second.append(side(8 + n, code.at[n], far_code.at[n], partner))
        units.append(side(18 + n, unit.at[n], far_unit.at[n], partner))
        units[n].start()
        second[n].start()
    third = []
    for i in (0, 1):
        mine = 2 * core + i
        lanes = pl.ds(pl.multiple_of(mine * LANES, LANES), LANES)
        for c in (0, 1):
            n = 2 * i + c
            units[n].wait_recv()
            second[n].wait_recv()
            total = decode(code.at[n], unit.at[n]) + decode(far_code.at[n], far_unit.at[n])
            new[mine, c] = spec[c, :, lanes] - STEP * total
            third.append(side(12 + n, new.at[mine, c], new.at[mine, c], mate))
            third[n].start()
        for c in (0, 1):
            third[2 * i + c].wait_recv()
        for k in (i, i + 2):
            fresh[:, :, k * LANES : (k + 1) * LANES] = new[k]
        object_rows(i, new, rows_table, lhs)
        if i == 0:
            for k in range(BLOCKS):
                image[k] = object_block(i, k, lhs, table)
    image[3] += object_block(1, 3, lhs, table)
    for c in (0, 1):
        value = image[3, :, c * LANES : (c + 1) * LANES]
        edge_out[0, c] = pack_edge(value, 96)
        edge_out[1, c] = pack_edge(value, 112)
    edges = [
        side(16, edge_out.at[0], edge_in.at[0], right),
        side(17, edge_out.at[1], edge_in.at[1], left),
    ]
    for copy in edges:
        copy.start()
    for k in range(BLOCKS - 1):
        image[k] += object_block(1, k, lhs, table)
    for c in (0, 1):
        for k in (1, 2):
            stitched[c, k * LANES : (k + 1) * LANES, :] = image[
                k, :, c * LANES : (c + 1) * LANES
            ].T
    place = edge.astype(F32) - float(3 * LANES)
    at_head = (place < MARGIN) & (tile > 0)
    at_tail = (place >= 80) & (place < 96) & (tile < tiles - 1)
    for copy in edges:
        copy.wait_recv()
    for c in (0, 1):
        mine = image[0, :, c * LANES : (c + 1) * LANES]
        other = unpack_edge(edge_in[0, c], 0)
        blend = mine * ((place + 16.5) / OV) + other * ((15.5 - place) / OV)
        stitched[c, :LANES, :] = jnp.where(at_head, blend, mine).T
        mine = image[3, :, c * LANES : (c + 1) * LANES]
        other = unpack_edge(edge_in[1, c], 80)
        blend = mine * ((111.5 - place) / OV) + other * ((place - 79.5) / OV)
        stitched[c, 3 * LANES :, :] = jnp.where(at_tail, blend, mine).T[: CORE - 3 * LANES]
    for copy in flats + copies + first + second + units + third + edges:
        copy.wait_send()

    @pl.loop(1, tiles)
    def _(i):
        block(tile, lax.rem(tile + i, tiles)).wait_send()


def update(raw, scales, flat, spectrum, pupil, patterns, led_row, led_col):
    tiles = lax.axis_size("tile")
    frames, rows, width = raw.shape
    deep = frames * rows
    tables = [jnp.asarray(t) for t in band_tables() + object_tables()]
    picks = [patterns, led_row, led_col]
    hbm = pl.BlockSpec(memory_space=pltpu.MemorySpace.HBM)
    arrays = [
        pltpu.with_memory_space_constraint(a, pltpu.MemorySpace.HBM)
        for a in picks + [raw, scales, flat, spectrum, pupil] + tables
    ]
    small = (TH // 8, LANES)
    part = (2, TH, LANES)
    scratch = [pltpu.SMEM(a.shape, a.dtype) for a in picks]
    scratch += [pltpu.VMEM(a.shape, a.dtype) for a in arrays[3:]]
    scratch += [
        pltpu.VMEM((2, 2 * PC, 2 * TW), BF16),
        pltpu.VMEM((2, 2 * TH, 2 * LANES), BF16),
        pltpu.VMEM((2, 2, PR, LANES), F32),
        pltpu.VMEM((2, TH, 2 * LEDS * LANES), BF16),
        pltpu.VMEM((deep, width + 2 * LANES), F32),
        pltpu.VMEM((tiles, deep, TW), BF16),
        pltpu.VMEM((tiles, deep, TW), BF16),
        pltpu.VMEM((frames, TH, TW), F32),
        pltpu.VMEM((TH, TW), F32),
        pltpu.VMEM((2,) + small, F32),
        pltpu.VMEM((2,) + small, F32),
        pltpu.VMEM((2 * frames, LANES), F32),
        pltpu.VMEM((2, 2 * frames, LANES), F32),
        pltpu.VMEM((2, TH, 2 * TW), BF16),
        pltpu.VMEM((2, PR, PC), F32),
        pltpu.VMEM((2, frames * LEDS * PR, 2 * TW), BF16),
        pltpu.VMEM((LEDS * PR, 2 * PC), F32),
        pltpu.VMEM((LEDS * PR, 2 * TW), F32),
        pltpu.VMEM((frames, LEDS, 2, TH, TW), F32),
        pltpu.VMEM((frames, TH, TW), F32),
        pltpu.VMEM((BLOCKS,) + part, F32),
        pltpu.VMEM((2,) + part, F32),
        pltpu.VMEM((4, TH, LANES), jnp.int16),
        pltpu.VMEM((4, TH // CODE_ROWS, LANES), F32),
        pltpu.VMEM((4, TH, LANES), jnp.int16),
        pltpu.VMEM((4, TH // CODE_ROWS, LANES), F32),
        pltpu.VMEM((BLOCKS,) + part, F32),
        pltpu.VMEM((2, 2, BLOCKS, TW, 2 * LANES), BF16),
        pltpu.VMEM((2, TH, TW), BF16),
        pltpu.VMEM((BLOCKS, TH, 2 * LANES), F32),
        pltpu.VMEM((2, 2) + small, F32),
        pltpu.VMEM((2, 2) + small, F32),
        pltpu.SemaphoreType.DMA((12,)),
        pltpu.SemaphoreType.DMA((tiles,)),
        pltpu.SemaphoreType.DMA((tiles,)),
        pltpu.SemaphoreType.DMA((22,)),
        pltpu.SemaphoreType.DMA((22,)),
    ]
    return pl.pallas_call(
        functools.partial(update_kernel, tiles),
        in_specs=[hbm] * len(arrays),
        out_specs=[pl.BlockSpec(memory_space=pltpu.VMEM)] * 2,
        out_shape=[
            jax.ShapeDtypeStruct((2, TH, TW), F32),
            jax.ShapeDtypeStruct((2, CORE, TH), F32),
        ],
        scratch_shapes=scratch,
        compiler_params=pltpu.CompilerParams(
            collective_id=1, has_side_effects=True, vmem_limit_bytes=50 * 2**20
        ),
        name="update",
    )(*arrays)


def hand_over(first, second, first_out, second_out, sem):
    copies = [
        pltpu.make_async_copy(src.at[c], dst.at[c], sem.at[2 * n + c])
        for n, (src, dst) in enumerate(((first, first_out), (second, second_out)))
        for c in (0, 1)
    ]
    for copy in copies:
        copy.start()
    for copy in copies:
        copy.wait()


def deliver(fresh, stitched):
    hbm = pl.BlockSpec(memory_space=pltpu.MemorySpace.HBM)
    return pl.pallas_call(
        hand_over,
        in_specs=[pl.BlockSpec(memory_space=pltpu.VMEM)] * 2,
        out_specs=[hbm] * 2,
        out_shape=[jax.ShapeDtypeStruct(a.shape, a.dtype) for a in (fresh, stitched)],
        scratch_shapes=[pltpu.SemaphoreType.DMA((4,))],
        compiler_params=pltpu.CompilerParams(vmem_limit_bytes=4 * 2**20),
        name="deliver",
    )(fresh, stitched)


def body(raw, scales, flat, spectrum, pupil, patterns, led_row, led_col):
    fresh, stitched = update(
        raw, scales, flat.T, spectrum[0], pupil, patterns.T, led_row, led_col
    )
    fresh, stitched = deliver(fresh, stitched)
    return (fresh[None], jnp.swapaxes(stitched, 1, 2))


def solution(mesh):
    return jax.shard_map(
        body,
        mesh=mesh,
        in_specs=(
            P("grp", "tile", None),
            P("grp", "tile", None),
            P(None, "tile"),
            P("tile", None, None, None),
            P(),
            P(),
            P(),
            P(),
        ),
        out_specs=(P("tile", None, None, None), P(None, None, "tile")),
        check_vma=False,
    )
```

```python
import functools
import math

import jax
import jax.numpy as jnp
import ml_dtypes
import numpy as np
from jax import lax
from jax.experimental import pallas as pl
from jax.experimental.pallas import tpu as pltpu
from jax.sharding import PartitionSpec as P

TH = 256
TW = 512
OV = 32
BR = 4
BC = 32
PR = 64
PC = 128
FR_G = 4
LEDS = 4
HALF = TH // 2
HR = PR // 2
MARGIN = OV // 2
CORE = TW - OV
LANES = 128
BLOCKS = TW // LANES
MESH = pl.DeviceIdType.MESH
CODE_ROWS = 32
CODE_TOP = 32767.0
STEP = 0.02
F32 = jnp.float32
BF16 = jnp.bfloat16


def split_np(table):
    hi = table.astype(ml_dtypes.bfloat16)
    lo = (table - hi.astype(np.float64)).astype(ml_dtypes.bfloat16)
    return hi, lo


def wave_np(length, band):
    places = np.arange(length)[:, None]
    freqs = np.arange(band)[None, :] - band // 2
    angle = (places * freqs % length) * (2.0 * np.pi / length)
    return np.cos(angle) / math.sqrt(band), np.sin(angle) / math.sqrt(band)


def object_tables():
    re, im = wave_np(TH, TH)
    rows = []
    for parity in (0, 1):
        a, b = re[:HALF, parity::2], im[:HALF, parity::2]
        rows.append(np.stack(split_np(np.block([[a, -b], [b, a]]))))
    re, im = (np.roll(part.T, -MARGIN, axis=1)[:TH] for part in wave_np(TW, TW))
    cols = np.stack([np.stack(split_np(re)), np.stack(split_np(im))], axis=1)
    return np.stack(rows), cols


def band_tables():
    row_re, row_im = wave_np(TH, PR)
    spread = []
    for parity in (0, 1):
        re = row_re[:HALF, parity::2]
        im = row_im[:HALF, parity::2]
        rows_hi, rows_lo = split_np(np.block([[re, -im], [im, re]]))
        spread.append(np.concatenate([rows_hi, rows_hi, rows_lo, rows_lo], axis=1))
    order = np.concatenate([np.arange(0, PR, 2), np.arange(1, PR, 2)])
    gather = np.concatenate(split_np(np.concatenate([row_re.T[order], row_im.T[order]])))
    return np.stack(spread), gather


def split(x):
    hi = x.astype(BF16)
    return hi, (x - hi.astype(F32)).astype(BF16)


def dot(a, b):
    return jnp.dot(a, b, preferred_element_type=F32)


def box_corner(pat, lrow, lcol, frame, j):
    led = pat[j, frame]
    return lrow[led], lcol[led]


def row_order(index):
    return jnp.where(index < HR, 2 * index, 2 * index - (PR - 1))


def ones_where(condition):
    return jnp.where(condition, 1.0, 0.0).astype(BF16)


def column_select(col):
    x = lax.broadcasted_iota(jnp.int32, (TW, PC), 0)
    v = lax.broadcasted_iota(jnp.int32, (TW, PC), 1)
    return ones_where(x - v == col)


def column_place(col):
    v = lax.broadcasted_iota(jnp.int32, (PC, TW), 0)
    v = jnp.where(v < PC // 2, 2 * v, 2 * v - (PC - 1))
    x = lax.broadcasted_iota(jnp.int32, (PC, TW), 1)
    return ones_where(x - v == col)


def load_halves(spec, pup, halves, pd):
    for c in (0, 1):
        hi, lo = split(spec[c])
        halves[0, :, c * TW : (c + 1) * TW] = hi
        halves[1, :, c * TW : (c + 1) * TW] = lo
        for parity in (0, 1):
            pd[c, parity * HR : (parity + 1) * HR] = pup[c, pl.ds(parity, HR, stride=2), :]


def forward_frame(f, frame, pat, lrow, lcol, halves, pd, cols, spread, picked, lit, mid, field):
    y = lax.broadcasted_iota(jnp.int32, (PR, TH), 1)
    order = row_order(lax.broadcasted_iota(jnp.int32, (PR, TH), 0))
    corners = [box_corner(pat, lrow, lcol, frame, j) for j in range(LEDS)]
    choose = jnp.concatenate([ones_where(y - order == row) for row, _ in corners], axis=0)
    for h in (0, 1):
        picked[h, : LEDS * PR] = dot(choose, halves[h]).astype(BF16)
    p_re, p_im = pd[0], pd[1]
    for j in range(LEDS):
        rows = pl.ds(j * PR, PR)
        stack = jnp.concatenate(
            [picked[h, rows, c * TW : (c + 1) * TW] for h in (0, 1) for c in (0, 1)], axis=0
        )
        cut = dot(stack, column_select(corners[j][1]))
        b_re = cut[:PR] + cut[2 * PR : 3 * PR]
        b_im = cut[PR : 2 * PR] + cut[3 * PR :]
        lit[rows, :PC] = p_re * b_re - p_im * b_im
        lit[rows, PC:] = p_re * b_im + p_im * b_re
    hi, lo = split(lit[...])
    mid[...] = dot(hi, cols[0]) + dot(lo, cols[0]) + dot(hi, cols[1])
    estimate = None
    for j in range(LEDS):
        parts = []
        for parity in (0, 1):
            rows = pl.ds(j * PR + parity * HR, HR)
            re_hi, re_lo = split(mid[rows, :TW])
            im_hi, im_lo = split(mid[rows, TW:])
            both = jnp.concatenate([re_hi, im_hi, re_lo, im_lo], axis=0)
            parts.append(dot(spread[parity], jnp.concatenate([both, both], axis=0)))
        upper = parts[0] + parts[1]
        lower = parts[0] - parts[1]
        field[f, j, 0, :HALF] = upper[:HALF]
        field[f, j, 0, HALF:] = lower[:HALF]
        field[f, j, 1, :HALF] = upper[HALF:]
        field[f, j, 1, HALF:] = lower[HALF:]
        power = jnp.concatenate(
            [
                upper[:HALF] * upper[:HALF] + upper[HALF:] * upper[HALF:],
                lower[:HALF] * lower[:HALF] + lower[HALF:] * lower[HALF:],
            ],
            axis=0,
        )
        estimate = power if estimate is None else estimate + power
    return estimate


def backward_frame(f, frame, misfit, pat, lrow, lcol, pairs, fold, gather, field, bands, wide):
    for j in range(LEDS):
        weighted = [misfit * field[f, j, c] for c in (0, 1)]
        for parity in (0, 1):
            mix = [
                w[:, :TH] + w[:, TH:] if parity == 0 else w[:, :TH] - w[:, TH:]
                for w in weighted
            ]
            hi, lo = split(jnp.concatenate(mix, axis=1))
            first = dot(hi, fold[parity])
            total = first[:, :LANES] + first[:, LANES:] + dot(lo, fold[parity, :, :LANES])
            hi, lo = split(total)
            cut = slice((2 * j + parity) * LANES, (2 * j + parity + 1) * LANES)
            bands[0, :, cut] = hi
            bands[1, :, cut] = lo
    first = dot(gather[...], bands[0])
    second = dot(gather[: 2 * PR], bands[1])
    by_re = first[:PR] + first[2 * PR : 3 * PR] + second[:PR]
    by_im = first[PR : 2 * PR] + first[3 * PR :] + second[PR:]
    left = lax.broadcasted_iota(jnp.int32, (1, LANES), 1) < LANES // 2
    sign = jnp.where(left, 1.0, -1.0)
    turn = LANES // 2
    for j in range(LEDS):
        col = box_corner(pat, lrow, lcol, frame, j)[1]
        halves = []
        for parity in (0, 1):
            cut = slice((2 * j + parity) * LANES, (2 * j + parity + 1) * LANES)
            band = by_re[:, cut] + sign * pltpu.roll(by_im[:, cut], turn, 1)
            halves.append(
                pairs[0, parity] * band + sign * pairs[1, parity] * pltpu.roll(band, turn, 1)
            )
        even, odd = halves
        re_hi, re_lo = split(jnp.where(left, even, pltpu.roll(odd, turn, 1)))
        im_hi, im_lo = split(jnp.where(left, pltpu.roll(even, turn, 1), odd))
        stack = jnp.concatenate([re_hi, im_hi, re_lo, im_lo], axis=0)
        placed = dot(stack, column_place(col)).astype(BF16)
        rows = pl.ds(pl.multiple_of((f * LEDS + j) * PR, PR), PR)
        for h in (0, 1):
            for c in (0, 1):
                n = 2 * h + c
                wide[h, rows, c * TW : (c + 1) * TW] = placed[n * PR : (n + 1) * PR]


def row_places(first_frame, frames, pat, lrow, lcol):
    total_rows = frames * LEDS * PR
    lane = lax.broadcasted_iota(jnp.int32, (1, total_rows), 1)
    box = lane // PR
    target = row_order(lane & (PR - 1))
    for f in range(frames):
        for j in range(LEDS):
            row = box_corner(pat, lrow, lcol, first_frame + f, j)[0]
            target = target + jnp.where(box == f * LEDS + j, row, 0)
    return ones_where(lax.broadcasted_iota(jnp.int32, (TH, total_rows), 0) == target)


def place_pair(which, choose, wide, grad):
    for c in (0, 1):
        cut = pl.ds(pl.multiple_of(c * TW + which * (2 * LANES), LANES), 2 * LANES)
        both = dot(choose, wide[0, :, cut]) + dot(choose, wide[1, :, cut])
        for n in (0, 1):
            grad[2 * which + n, c] = both[:, n * LANES : (n + 1) * LANES]


def pack_edge(value, first):
    lane = lax.broadcasted_iota(jnp.int32, (TH // 8, LANES), 1) // MARGIN
    packed = jnp.zeros((TH // 8, LANES), F32)
    for b in range(8):
        piece = value[b * 32 : (b + 1) * 32]
        piece = pltpu.roll(piece, (MARGIN * b - first) % LANES, 1)
        packed = jnp.where(lane == b, piece, packed)
    return packed


def unpack_edge(packed, first):
    return jnp.concatenate(
        [pltpu.roll(packed, (first - MARGIN * b) % LANES, 1) for b in range(8)], axis=0
    )


def dequantize(raw, scales, dequant):
    frames, rows, width = raw.shape
    dequant[:, :LANES] = jnp.zeros((frames * rows, LANES), F32)
    dequant[:, LANES + width :] = jnp.zeros((frames * rows, LANES), F32)
    lane = lax.broadcasted_iota(jnp.int32, (rows, LANES), 1) // BC
    upper = lax.broadcasted_iota(jnp.int32, (rows, LANES), 0) < BR
    blocks = scales.shape[2]
    per = LANES // BC
    for first in range(0, blocks, LANES):
        count = min(LANES, blocks - first)
        for f in range(frames):
            pair = scales[f, :, first : first + count].astype(F32)
            if count < LANES:
                pair = jnp.concatenate([pair, jnp.zeros((2, LANES - count), F32)], axis=1)
            factors = jnp.where(
                upper,
                jnp.broadcast_to(pair[0:1], (rows, LANES)),
                jnp.broadcast_to(pair[1:2], (rows, LANES)),
            )
            for k in range(count // per):
                column = (first // per + k) * LANES
                spread = jnp.take_along_axis(factors, lane + per * k, axis=1)
                codes = raw[f, :, column : column + LANES].astype(F32)
                dequant[f * rows : (f + 1) * rows, LANES + column : 2 * LANES + column] = (
                    codes * spread
                )


def cut_message(dequant, tile):
    start = CORE * tile - MARGIN + LANES
    aligned = pl.multiple_of(start // LANES * LANES, LANES)
    offset = start - aligned + MARGIN
    wide = dequant[:, pl.ds(aligned, TW + LANES)]
    wide = pltpu.roll(wide, TW + LANES - offset, 1)
    lane = lax.broadcasted_iota(jnp.int32, (1, LANES), 1)
    last = jnp.where(lane < LANES - MARGIN, wide[:, TW - LANES : TW], wide[:, TW:])
    return jnp.concatenate([wide[:, : TW - LANES], last], axis=1).astype(BF16)


def centred():
    y = lax.broadcasted_iota(jnp.int32, (TH, 1), 0).astype(F32) - (TH - 1) / 2.0
    lane = lax.broadcasted_iota(jnp.int32, (1, TW), 1)
    x = lane.astype(F32) - (CORE - 1) / 2.0
    return y, x, lane


Y_NORM = float(np.sum((np.arange(TH) - (TH - 1) / 2.0) ** 2) * CORE)
X_NORM = float(np.sum((np.arange(CORE) - (CORE - 1) / 2.0) ** 2) * TH)


def parity_pick(parity):
    v = lax.broadcasted_iota(jnp.int32, (PC, LANES), 0)
    lane = lax.broadcasted_iota(jnp.int32, (PC, LANES), 1)
    return ones_where(v == 2 * (lane & (PC // 2 - 1)) + parity)


def build_band(half, pd, cols, fold, pairs):
    lane = lax.broadcasted_iota(jnp.int32, (1, TW), 1)
    sign = (2 - 4 * (lane & 1)).astype(F32)
    left = lane[:, :LANES] < LANES // 2
    for h in (0, 1):
        re, im = (
            jnp.concatenate(
                [
                    half[h, c, TH - PC // 2 :, :].astype(F32) * 2.0,
                    half[h, c, : PC // 2, :].astype(F32) * sign,
                ],
                axis=0,
            )
            for c in (0, 1)
        )
        cols[h, :PC, :TW] = re.astype(BF16)
        cols[h, :PC, TW:] = im.astype(BF16)
        cols[h, PC:, :TW] = (-im).astype(BF16)
        cols[h, PC:, TW:] = re.astype(BF16)
        turned = [part[:, :TH].T.astype(BF16) for part in (re, im)]
        for parity in (0, 1):
            a, b = (dot(part, parity_pick(parity)) for part in turned)
            cut = slice(h * LANES, (h + 1) * LANES)
            fold[parity, :TH, cut] = jnp.where(left, a, -b).astype(BF16)
            fold[parity, TH:, cut] = jnp.where(left, b, a).astype(BF16)
    for c in (0, 1):
        hi = pd[c].astype(BF16)
        lo, last = split(pd[c] - hi.astype(F32))
        for parity in (0, 1):
            pick = parity_pick(parity)
            pairs[c, parity] = dot(hi, pick) + dot(lo, pick) + dot(last, pick)


def build_columns(half, table):
    lane = lax.broadcasted_iota(jnp.int32, (1, TW), 1)
    sign = (1 - 2 * (lane & 1)).astype(F32)
    for i in (0, 1):
        rows = pl.ds(i * LANES, LANES)
        for h in (0, 1):
            re = half[h, 0, rows, :].astype(F32)
            im = half[h, 1, rows, :].astype(F32)
            for n, factor in ((0, None), (1, sign)):
                a = re if factor is None else re * factor
                b = im if factor is None else im * factor
                upper = pl.ds(n * LANES, LANES)
                lower = pl.ds((2 + n) * LANES, LANES)
                for k in range(BLOCKS):
                    cut = slice(k * LANES, (k + 1) * LANES)
                    table[i, h, k, upper, :LANES] = a[:, cut].astype(BF16)
                    table[i, h, k, upper, LANES:] = b[:, cut].astype(BF16)
                    table[i, h, k, lower, :LANES] = (-b[:, cut]).astype(BF16)
                    table[i, h, k, lower, LANES:] = a[:, cut].astype(BF16)


def object_rows(i, new, rows_table, lhs):
    parts = []
    for parity in (0, 1):
        data = [
            jnp.concatenate(
                [new[k, c, pl.ds(parity, HALF, stride=2), :] for k in (i, i + 2)], axis=1
            )
            for c in (0, 1)
        ]
        hi, lo = split(jnp.concatenate(data, axis=0))
        t_hi, t_lo = rows_table[parity, 0], rows_table[parity, 1]
        parts.append(dot(t_hi, hi) + dot(t_hi, lo) + dot(t_lo, hi))
    for n, value in enumerate((parts[0] + parts[1], parts[0] - parts[1])):
        hi, lo = split(value)
        rows = pl.ds(n * HALF, HALF)
        for h, part in enumerate((hi, lo)):
            lhs[h, rows, : 2 * LANES] = part[:HALF]
            lhs[h, rows, 2 * LANES :] = part[HALF:]


def object_block(i, k, lhs, table):
    hi, lo = lhs[0], lhs[1]
    return dot(hi, table[i, 0, k]) + dot(lo, table[i, 0, k]) + dot(hi, table[i, 1, k])


def encode(value, code, unit):
    for g in range(TH // CODE_ROWS):
        rows = slice(g * CODE_ROWS, (g + 1) * CODE_ROWS)
        piece = value[rows]
        top = jnp.max(jnp.abs(piece), axis=0, keepdims=True)
        unit[g : g + 1] = top * (1.0 / CODE_TOP)
        ratio = jnp.where(top > 0.0, CODE_TOP / top, 0.0)
        whole = jnp.clip(jnp.round(piece * ratio), -CODE_TOP, CODE_TOP)
        code[rows] = whole.astype(jnp.int32).astype(jnp.int16)


def decode(code, unit):
    return jnp.concatenate(
        [
            code[g * CODE_ROWS : (g + 1) * CODE_ROWS].astype(jnp.int32).astype(F32)
            * unit[g : g + 1]
            for g in range(TH // CODE_ROWS)
        ],
        axis=0,
    )


def update_kernel(
    tiles,
    pat_h,
    lrow_h,
    lcol_h,
    raw_h,
    scales_h,
    flat_h,
    spec_h,
    pup_h,
    spread_h,
    gather_h,
    rows_h,
    half_h,
    fresh,
    stitched,
    pat,
    lrow,
    lcol,
    raw,
    scales,
    flat,
    spec,
    pup,
    spread,
    gather,
    rows_table,
    half,
    cols,
    fold,
    pairs,
    bands,
    dequant,
    message,
    arrived,
    window,
    gains,
    flat_out,
    flat_in,
    slope_out,
    slope_in,
    sums,
    coef,
    halves,
    pd,
    wide,
    lit,
    mid,
    field,
    estimate,
    grad,
    got,
    code,
    unit,
    far_code,
    far_unit,
    new,
    table,
    lhs,
    image,
    edge_out,
    edge_in,
    load,
    send,
    recv,
    side_send,
    side_recv,
):
    frames = raw.shape[0]
    rows = raw.shape[1]
    group = lax.axis_index("grp")
    tile = lax.axis_index("tile")
    core = lax.rem(group, 2)
    mate = {"grp": group + 1 - 2 * core}
    partner = {"grp": group + 2 - 4 * lax.div(group, 2)}
    right = {"tile": lax.rem(tile + 1, tiles)}
    left = {"tile": lax.rem(tile + tiles - 1, tiles)}

    def side(number, src, dst, device):
        return pltpu.make_async_remote_copy(
            src_ref=src,
            dst_ref=dst,
            send_sem=side_send.at[number],
            recv_sem=side_recv.at[number],
            device_id=device,
            device_id_type=MESH,
        )

    def block(source, target):
        return pltpu.make_async_remote_copy(
            src_ref=message.at[target],
            dst_ref=arrived.at[source],
            send_sem=send.at[target],
            recv_sem=recv.at[source],
            device_id={"tile": target},
            device_id_type=MESH,
        )

    loads = [
        pltpu.make_async_copy(src, dst, load.at[n])
        for n, (src, dst) in enumerate(
            (
                (raw_h, raw),
                (scales_h, scales),
                (pat_h, pat),
                (lrow_h, lrow),
                (lcol_h, lcol),
                (flat_h, flat),
                (spec_h, spec),
                (pup_h, pup),
                (half_h, half),
                (spread_h, spread),
                (gather_h, gather),
                (rows_h, rows_table),
            )
        )
    ]
    for copy in loads:
        copy.start()
    barrier = pltpu.get_barrier_semaphore()

    @pl.loop(1, tiles)
    def _(i):
        pl.semaphore_signal(
            barrier, inc=1, device_id={"tile": lax.rem(tile + i, tiles)}, device_id_type=MESH
        )

    for device in (mate, partner):
        pl.semaphore_signal(barrier, inc=1, device_id=device, device_id_type=MESH)

    loads[0].wait()
    loads[1].wait()
    dequantize(raw, scales, dequant)
    pl.semaphore_wait(barrier, tiles + 1)

    @pl.loop(1, tiles)
    def _(i):
        target = lax.rem(tile + i, tiles)
        message[target] = cut_message(dequant, target)
        block(tile, target).start()

    arrived[tile] = cut_message(dequant, tile)
    loads[5].wait()
    for k in range(BLOCKS - 1):
        gains[:, k * LANES : (k + 1) * LANES] = flat[k * LANES : (k + 1) * LANES, :].T
    tail = jnp.concatenate(
        [flat[3 * LANES :, :], jnp.zeros((TW - CORE, TH), F32)], axis=0
    ).T
    gains[:, 3 * LANES :] = tail
    flat_out[0] = pack_edge(tail, 80)
    flat_out[1] = pack_edge(gains[:, :LANES], 0)
    flats = [
        side(0, flat_out.at[0], flat_in.at[0], right),
        side(1, flat_out.at[1], flat_in.at[1], left),
    ]
    for copy in flats:
        copy.start()

    for copy in loads[2:5] + loads[6:]:
        copy.wait()
    load_halves(spec, pup, halves, pd)
    build_band(half, pd, cols, fold, pairs)
    first_frame = group * frames

    def forward(f):
        estimate[f] = forward_frame(
            f, first_frame + f, pat, lrow, lcol, halves, pd, cols, spread, wide, lit, mid, field
        )

    pl.loop(0, frames - 1)(forward)
    build_columns(half, table)

    y, x, lane = centred()
    edge = lane[:, 3 * LANES :]
    for copy in flats:
        copy.wait_recv()
    outer = jnp.where(
        edge < CORE + MARGIN, unpack_edge(flat_in[1], 96), unpack_edge(flat_in[0], 112)
    )
    own = edge < CORE
    after = edge < CORE + MARGIN
    blank = ((~own) & after & (tile == tiles - 1)) | ((~after) & (tile == 0))
    gains[:, 3 * LANES :] = jnp.where(
        blank, 0.0, jnp.where(own, gains[:, 3 * LANES :], outer)
    )
    sums[...] = jnp.zeros_like(sums)

    @pl.loop(1, tiles + 1)
    def _(i):
        source = lax.rem(tile + tiles - i, tiles)

        @pl.when(i < tiles)
        def _():
            block(source, tile).wait_recv()

        here = pl.ds(pl.multiple_of(source * rows, rows), rows)
        values = arrived[source].astype(F32)
        for f in range(frames):
            flattened = values[f * rows : (f + 1) * rows] * gains[here, :]
            window[f, here, :] = flattened
            sums[0, f] += flattened
            sums[1, f] += flattened * (y[:rows] + (source * rows).astype(F32))

    inside = (lane < CORE).astype(F32)
    slopes = []
    for f in range(frames):
        columns = jnp.sum(sums[0, f], axis=0, keepdims=True)
        tilted = jnp.sum(sums[1, f], axis=0, keepdims=True)
        slope_y = jnp.sum(tilted * inside, axis=1, keepdims=True) / Y_NORM
        slope_x = jnp.sum(columns * (x * inside), axis=1, keepdims=True) / X_NORM
        slopes.append((slope_y, slope_x))
        slope_out[f : f + 1] = jnp.broadcast_to(slope_y, (1, LANES))
        slope_out[frames + f : frames + f + 1] = jnp.broadcast_to(slope_x, (1, LANES))
    copies = [side(2, slope_out, slope_in.at[0], right), side(3, slope_out, slope_in.at[1], left)]
    for copy in copies:
        copy.start()
    forward(frames - 1)
    for copy in copies:
        copy.wait_recv()
    x_edge = x[:, 3 * LANES :]
    for f in range(frames):
        slope_y, slope_x = slopes[f]
        coef[f, 0:1, : 3 * LANES] = jnp.broadcast_to(slope_y, (1, 3 * LANES))
        coef[f, 1:2, : 3 * LANES] = slope_x * x[:, : 3 * LANES]
        row_y = jnp.where(
            own, slope_y, jnp.where(after, slope_in[1, f : f + 1], slope_in[0, f : f + 1])
        )
        row_x = jnp.where(
            own,
            slope_x * x_edge,
            jnp.where(
                after,
                slope_in[1, frames + f : frames + f + 1] * (x_edge - CORE),
                slope_in[0, frames + f : frames + f + 1] * (x_edge - 32.0),
            ),
        )
        coef[f, 0:1, 3 * LANES :] = jnp.where(blank, 0.0, row_y)
        coef[f, 1:2, 3 * LANES :] = jnp.where(blank, 0.0, row_x)

    @pl.loop(0, frames)
    def _(f):
        misfit = estimate[f] - window[f] + coef[f, 0:1] * y + coef[f, 1:2]
        backward_frame(
            f, first_frame + f, misfit, pat, lrow, lcol, pairs, fold, gather, field, bands, wide
        )

    choose = row_places(first_frame, frames, pat, lrow, lcol)
    place_pair(1 - core, choose, wide, grad)

    pieces = [(i, c) for i in (0, 1) for c in (0, 1)]
    first = [
        side(4 + n, grad.at[2 - 2 * core + i, c], got.at[i, c], mate)
        for n, (i, c) in enumerate(pieces)
    ]
    for copy in first:
        copy.start()
    place_pair(core, choose, wide, grad)
    second = []
    units = []
    for n, (i, c) in enumerate(pieces):
        first[n].wait_recv()
        encode(grad[2 * core + i, c] + got[i, c], code.at[n], unit.at[n])
        second.append(side(8 + n, code.at[n], far_code.at[n], partner))
        units.append(side(18 + n, unit.at[n], far_unit.at[n], partner))
        units[n].start()
        second[n].start()
    third = []
    for i in (0, 1):
        mine = 2 * core + i
        lanes = pl.ds(pl.multiple_of(mine * LANES, LANES), LANES)
        for c in (0, 1):
            n = 2 * i + c
            units[n].wait_recv()
            second[n].wait_recv()
            total = decode(code.at[n], unit.at[n]) + decode(far_code.at[n], far_unit.at[n])
            new[mine, c] = spec[c, :, lanes] - STEP * total
            third.append(side(12 + n, new.at[mine, c], new.at[mine, c], mate))
            third[n].start()
        for c in (0, 1):
            third[2 * i + c].wait_recv()
        for k in (i, i + 2):
            fresh[:, :, k * LANES : (k + 1) * LANES] = new[k]
        object_rows(i, new, rows_table, lhs)
        if i == 0:
            for k in range(BLOCKS):
                image[k] = object_block(i, k, lhs, table)
    image[3] += object_block(1, 3, lhs, table)
    for c in (0, 1):
        value = image[3, :, c * LANES : (c + 1) * LANES]
        edge_out[0, c] = pack_edge(value, 96)
        edge_out[1, c] = pack_edge(value, 112)
    edges = [
        side(16, edge_out.at[0], edge_in.at[0], right),
        side(17, edge_out.at[1], edge_in.at[1], left),
    ]
    for copy in edges:
        copy.start()
    for k in range(BLOCKS - 1):
        image[k] += object_block(1, k, lhs, table)
    for c in (0, 1):
        for k in (1, 2):
            stitched[c, k * LANES : (k + 1) * LANES, :] = image[
                k, :, c * LANES : (c + 1) * LANES
            ].T
    place = edge.astype(F32) - float(3 * LANES)
    at_head = (place < MARGIN) & (tile > 0)
    at_tail = (place >= 80) & (place < 96) & (tile < tiles - 1)
    for copy in edges:
        copy.wait_recv()
    for c in (0, 1):
        mine = image[0, :, c * LANES : (c + 1) * LANES]
        other = unpack_edge(edge_in[0, c], 0)
        blend = mine * ((place + 16.5) / OV) + other * ((15.5 - place) / OV)
        stitched[c, :LANES, :] = jnp.where(at_head, blend, mine).T
        mine = image[3, :, c * LANES : (c + 1) * LANES]
        other = unpack_edge(edge_in[1, c], 80)
        blend = mine * ((111.5 - place) / OV) + other * ((place - 79.5) / OV)
        stitched[c, 3 * LANES :, :] = jnp.where(at_tail, blend, mine).T[: CORE - 3 * LANES]
    for copy in flats + copies + first + second + units + third + edges:
        copy.wait_send()

    @pl.loop(1, tiles)
    def _(i):
        block(tile, lax.rem(tile + i, tiles)).wait_send()


def update(raw, scales, flat, spectrum, pupil, patterns, led_row, led_col):
    tiles = lax.axis_size("tile")
    frames, rows, width = raw.shape
    deep = frames * rows
    tables = [jnp.asarray(t) for t in band_tables() + object_tables()]
    picks = [patterns, led_row, led_col]
    hbm = pl.BlockSpec(memory_space=pltpu.MemorySpace.HBM)
    arrays = [
        pltpu.with_memory_space_constraint(a, pltpu.MemorySpace.HBM)
        for a in picks + [raw, scales, flat, spectrum, pupil] + tables
    ]
    small = (TH // 8, LANES)
    part = (2, TH, LANES)
    scratch = [pltpu.SMEM(a.shape, a.dtype) for a in picks]
    scratch += [pltpu.VMEM(a.shape, a.dtype) for a in arrays[3:]]
    scratch += [
        pltpu.VMEM((2, 2 * PC, 2 * TW), BF16),
        pltpu.VMEM((2, 2 * TH, 2 * LANES), BF16),
        pltpu.VMEM((2, 2, PR, LANES), F32),
        pltpu.VMEM((2, TH, 2 * LEDS * LANES), BF16),
        pltpu.VMEM((deep, width + 2 * LANES), F32),
        pltpu.VMEM((tiles, deep, TW), BF16),
        pltpu.VMEM((tiles, deep, TW), BF16),
        pltpu.VMEM((frames, TH, TW), F32),
        pltpu.VMEM((TH, TW), F32),
        pltpu.VMEM((2,) + small, F32),
        pltpu.VMEM((2,) + small, F32),
        pltpu.VMEM((2 * frames, LANES), F32),
        pltpu.VMEM((2, 2 * frames, LANES), F32),
        pltpu.VMEM((2, frames, rows, TW), F32),
        pltpu.VMEM((frames, 8, TW), F32),
        pltpu.VMEM((2, TH, 2 * TW), BF16),
        pltpu.VMEM((2, PR, PC), F32),
        pltpu.VMEM((2, frames * LEDS * PR, 2 * TW), BF16),
        pltpu.VMEM((LEDS * PR, 2 * PC), F32),
        pltpu.VMEM((LEDS * PR, 2 * TW), F32),
        pltpu.VMEM((frames, LEDS, 2, TH, TW), F32),
        pltpu.VMEM((frames, TH, TW), F32),
        pltpu.VMEM((BLOCKS,) + part, F32),
        pltpu.VMEM((2,) + part, F32),
        pltpu.VMEM((4, TH, LANES), jnp.int16),
        pltpu.VMEM((4, TH // CODE_ROWS, LANES), F32),
        pltpu.VMEM((4, TH, LANES), jnp.int16),
        pltpu.VMEM((4, TH // CODE_ROWS, LANES), F32),
        pltpu.VMEM((BLOCKS,) + part, F32),
        pltpu.VMEM((2, 2, BLOCKS, TW, 2 * LANES), BF16),
        pltpu.VMEM((2, TH, TW), BF16),
        pltpu.VMEM((BLOCKS, TH, 2 * LANES), F32),
        pltpu.VMEM((2, 2) + small, F32),
        pltpu.VMEM((2, 2) + small, F32),
        pltpu.SemaphoreType.DMA((12,)),
        pltpu.SemaphoreType.DMA((tiles,)),
        pltpu.SemaphoreType.DMA((tiles,)),
        pltpu.SemaphoreType.DMA((22,)),
        pltpu.SemaphoreType.DMA((22,)),
    ]
    return pl.pallas_call(
        functools.partial(update_kernel, tiles),
        in_specs=[hbm] * len(arrays),
        out_specs=[pl.BlockSpec(memory_space=pltpu.VMEM)] * 2,
        out_shape=[
            jax.ShapeDtypeStruct((2, TH, TW), F32),
            jax.ShapeDtypeStruct((2, CORE, TH), F32),
        ],
        scratch_shapes=scratch,
        compiler_params=pltpu.CompilerParams(
            collective_id=1, has_side_effects=True, vmem_limit_bytes=50 * 2**20
        ),
        name="update",
    )(*arrays)


def hand_over(first, second, first_out, second_out, sem):
    copies = [
        pltpu.make_async_copy(src.at[c], dst.at[c], sem.at[2 * n + c])
        for n, (src, dst) in enumerate(((first, first_out), (second, second_out)))
        for c in (0, 1)
    ]
    for copy in copies:
        copy.start()
    for copy in copies:
        copy.wait()


def deliver(fresh, stitched):
    hbm = pl.BlockSpec(memory_space=pltpu.MemorySpace.HBM)
    return pl.pallas_call(
        hand_over,
        in_specs=[pl.BlockSpec(memory_space=pltpu.VMEM)] * 2,
        out_specs=[hbm] * 2,
        out_shape=[jax.ShapeDtypeStruct(a.shape, a.dtype) for a in (fresh, stitched)],
        scratch_shapes=[pltpu.SemaphoreType.DMA((4,))],
        compiler_params=pltpu.CompilerParams(vmem_limit_bytes=4 * 2**20),
        name="deliver",
    )(fresh, stitched)


def body(raw, scales, flat, spectrum, pupil, patterns, led_row, led_col):
    fresh, stitched = update(
        raw, scales, flat.T, spectrum[0], pupil, patterns.T, led_row, led_col
    )
    fresh, stitched = deliver(fresh, stitched)
    return (fresh[None], jnp.swapaxes(stitched, 1, 2))


def solution(mesh):
    return jax.shard_map(
        body,
        mesh=mesh,
        in_specs=(
            P("grp", "tile", None),
            P("grp", "tile", None),
            P(None, "tile"),
            P("tile", None, None, None),
            P(),
            P(),
            P(),
            P(),
        ),
        out_specs=(P("tile", None, None, None), P(None, None, "tile")),
        check_vma=False,
    )
```

```python
import functools
import math

import jax
import jax.numpy as jnp
import ml_dtypes
import numpy as np
from jax import lax
from jax.experimental import pallas as pl
from jax.experimental.pallas import tpu as pltpu
from jax.sharding import PartitionSpec as P

TH = 256
TW = 512
OV = 32
BR = 4
BC = 32
PR = 64
PC = 128
FR_G = 4
LEDS = 4
HALF = TH // 2
HR = PR // 2
MARGIN = OV // 2
CORE = TW - OV
LANES = 128
BLOCKS = TW // LANES
MESH = pl.DeviceIdType.MESH
CODE_ROWS = 32
CODE_TOP = 32767.0
STEP = 0.02
F32 = jnp.float32
BF16 = jnp.bfloat16


def split_np(table):
    hi = table.astype(ml_dtypes.bfloat16)
    lo = (table - hi.astype(np.float64)).astype(ml_dtypes.bfloat16)
    return hi, lo


def wave_np(length, band):
    places = np.arange(length)[:, None]
    freqs = np.arange(band)[None, :] - band // 2
    angle = (places * freqs % length) * (2.0 * np.pi / length)
    return np.cos(angle) / math.sqrt(band), np.sin(angle) / math.sqrt(band)


def object_tables():
    re, im = wave_np(TH, TH)
    rows = []
    for parity in (0, 1):
        a, b = re[:HALF, parity::2], im[:HALF, parity::2]
        rows.append(np.stack(split_np(np.block([[a, -b], [b, a]]))))
    re, im = (np.roll(part.T, -MARGIN, axis=1)[:TH] for part in wave_np(TW, TW))
    cols = np.stack([np.stack(split_np(re)), np.stack(split_np(im))], axis=1)
    return np.stack(rows), cols


def band_tables():
    row_re, row_im = wave_np(TH, PR)
    spread = []
    for parity in (0, 1):
        re = row_re[:HALF, parity::2]
        im = row_im[:HALF, parity::2]
        rows_hi, rows_lo = split_np(np.block([[re, -im], [im, re]]))
        spread.append(np.concatenate([rows_hi, rows_hi, rows_lo, rows_lo], axis=1))
    order = np.concatenate([np.arange(0, PR, 2), np.arange(1, PR, 2)])
    gather = np.concatenate(split_np(np.concatenate([row_re.T[order], row_im.T[order]])))
    return np.stack(spread), gather


def split(x):
    hi = x.astype(BF16)
    return hi, (x - hi.astype(F32)).astype(BF16)


def dot(a, b):
    return jnp.dot(a, b, preferred_element_type=F32)


def box_corner(pat, lrow, lcol, frame, j):
    led = pat[j, frame]
    return lrow[led], lcol[led]


def row_order(index):
    return jnp.where(index < HR, 2 * index, 2 * index - (PR - 1))


def ones_where(condition):
    return jnp.where(condition, 1.0, 0.0).astype(BF16)


def column_select(col):
    x = lax.broadcasted_iota(jnp.int32, (TW, PC), 0)
    v = lax.broadcasted_iota(jnp.int32, (TW, PC), 1)
    return ones_where(x - v == col)


def column_place(col):
    v = lax.broadcasted_iota(jnp.int32, (PC, TW), 0)
    v = jnp.where(v < PC // 2, 2 * v, 2 * v - (PC - 1))
    x = lax.broadcasted_iota(jnp.int32, (PC, TW), 1)
    return ones_where(x - v == col)


def load_halves(spec, pup, halves, pd):
    for c in (0, 1):
        hi, lo = split(spec[c])
        halves[0, :, c * TW : (c + 1) * TW] = hi
        halves[1, :, c * TW : (c + 1) * TW] = lo
        for parity in (0, 1):
            pd[c, parity * HR : (parity + 1) * HR] = pup[c, pl.ds(parity, HR, stride=2), :]


def forward_frame(f, frame, pat, lrow, lcol, halves, pd, cols, spread, picked, lit, mid, field):
    y = lax.broadcasted_iota(jnp.int32, (PR, TH), 1)
    order = row_order(lax.broadcasted_iota(jnp.int32, (PR, TH), 0))
    corners = [box_corner(pat, lrow, lcol, frame, j) for j in range(LEDS)]
    choose = jnp.concatenate([ones_where(y - order == row) for row, _ in corners], axis=0)
    for h in (0, 1):
        picked[h, : LEDS * PR] = dot(choose, halves[h]).astype(BF16)
    p_re, p_im = pd[0], pd[1]
    for j in range(LEDS):
        rows = pl.ds(j * PR, PR)
        stack = jnp.concatenate(
            [picked[h, rows, c * TW : (c + 1) * TW] for h in (0, 1) for c in (0, 1)], axis=0
        )
        cut = dot(stack, column_select(corners[j][1]))
        b_re = cut[:PR] + cut[2 * PR : 3 * PR]
        b_im = cut[PR : 2 * PR] + cut[3 * PR :]
        lit[rows, :PC] = p_re * b_re - p_im * b_im
        lit[rows, PC:] = p_re * b_im + p_im * b_re
    hi, lo = split(lit[...])
    mid[...] = dot(hi, cols[0]) + dot(lo, cols[0]) + dot(hi, cols[1])
    estimate = None
    for j in range(LEDS):
        parts = []
        for parity in (0, 1):
            rows = pl.ds(j * PR + parity * HR, HR)
            re_hi, re_lo = split(mid[rows, :TW])
            im_hi, im_lo = split(mid[rows, TW:])
            both = jnp.concatenate([re_hi, im_hi, re_lo, im_lo], axis=0)
            parts.append(dot(spread[parity], jnp.concatenate([both, both], axis=0)))
        upper = parts[0] + parts[1]
        lower = parts[0] - parts[1]
        field[f, j, 0, :HALF] = upper[:HALF]
        field[f, j, 0, HALF:] = lower[:HALF]
        field[f, j, 1, :HALF] = upper[HALF:]
        field[f, j, 1, HALF:] = lower[HALF:]
        power = jnp.concatenate(
            [
                upper[:HALF] * upper[:HALF] + upper[HALF:] * upper[HALF:],
                lower[:HALF] * lower[:HALF] + lower[HALF:] * lower[HALF:],
            ],
            axis=0,
        )
        estimate = power if estimate is None else estimate + power
    return estimate


def backward_frame(f, frame, misfit, pat, lrow, lcol, pairs, fold, gather, field, bands, wide):
    for j in range(LEDS):
        weighted = [misfit * field[f, j, c] for c in (0, 1)]
        for parity in (0, 1):
            mix = [
                w[:, :TH] + w[:, TH:] if parity == 0 else w[:, :TH] - w[:, TH:]
                for w in weighted
            ]
            hi, lo = split(jnp.concatenate(mix, axis=1))
            first = dot(hi, fold[parity])
            total = first[:, :LANES] + first[:, LANES:] + dot(lo, fold[parity, :, :LANES])
            hi, lo = split(total)
            cut = slice((2 * j + parity) * LANES, (2 * j + parity + 1) * LANES)
            bands[0, :, cut] = hi
            bands[1, :, cut] = lo
    first = dot(gather[...], bands[0])
    second = dot(gather[: 2 * PR], bands[1])
    by_re = first[:PR] + first[2 * PR : 3 * PR] + second[:PR]
    by_im = first[PR : 2 * PR] + first[3 * PR :] + second[PR:]
    left = lax.broadcasted_iota(jnp.int32, (1, LANES), 1) < LANES // 2
    sign = jnp.where(left, 1.0, -1.0)
    turn = LANES // 2
    for j in range(LEDS):
        col = box_corner(pat, lrow, lcol, frame, j)[1]
        halves = []
        for parity in (0, 1):
            cut = slice((2 * j + parity) * LANES, (2 * j + parity + 1) * LANES)
            band = by_re[:, cut] + sign * pltpu.roll(by_im[:, cut], turn, 1)
            halves.append(
                pairs[0, parity] * band + sign * pairs[1, parity] * pltpu.roll(band, turn, 1)
            )
        even, odd = halves
        re_hi, re_lo = split(jnp.where(left, even, pltpu.roll(odd, turn, 1)))
        im_hi, im_lo = split(jnp.where(left, pltpu.roll(even, turn, 1), odd))
        stack = jnp.concatenate([re_hi, im_hi, re_lo, im_lo], axis=0)
        placed = dot(stack, column_place(col)).astype(BF16)
        rows = pl.ds(pl.multiple_of((f * LEDS + j) * PR, PR), PR)
        for h in (0, 1):
            for c in (0, 1):
                n = 2 * h + c
                wide[h, rows, c * TW : (c + 1) * TW] = placed[n * PR : (n + 1) * PR]


def row_places(first_frame, frames, pat, lrow, lcol):
    total_rows = frames * LEDS * PR
    lane = lax.broadcasted_iota(jnp.int32, (1, total_rows), 1)
    box = lane // PR
    target = row_order(lane & (PR - 1))
    for f in range(frames):
        for j in range(LEDS):
            row = box_corner(pat, lrow, lcol, first_frame + f, j)[0]
            target = target + jnp.where(box == f * LEDS + j, row, 0)
    return ones_where(lax.broadcasted_iota(jnp.int32, (TH, total_rows), 0) == target)


def place_pair(which, choose, wide, grad):
    for c in (0, 1):
        cut = pl.ds(pl.multiple_of(c * TW + which * (2 * LANES), LANES), 2 * LANES)
        both = dot(choose, wide[0, :, cut]) + dot(choose, wide[1, :, cut])
        for n in (0, 1):
            grad[2 * which + n, c] = both[:, n * LANES : (n + 1) * LANES]


def pack_edge(value, first):
    lane = lax.broadcasted_iota(jnp.int32, (TH // 8, LANES), 1) // MARGIN
    packed = jnp.zeros((TH // 8, LANES), F32)
    for b in range(8):
        piece = value[b * 32 : (b + 1) * 32]
        piece = pltpu.roll(piece, (MARGIN * b - first) % LANES, 1)
        packed = jnp.where(lane == b, piece, packed)
    return packed


def unpack_edge(packed, first):
    return jnp.concatenate(
        [pltpu.roll(packed, (first - MARGIN * b) % LANES, 1) for b in range(8)], axis=0
    )


def dequantize(raw, scales, dequant):
    frames, rows, width = raw.shape
    dequant[:, :LANES] = jnp.zeros((frames * rows, LANES), F32)
    dequant[:, LANES + width :] = jnp.zeros((frames * rows, LANES), F32)
    lane = lax.broadcasted_iota(jnp.int32, (rows, LANES), 1) // BC
    upper = lax.broadcasted_iota(jnp.int32, (rows, LANES), 0) < BR
    blocks = scales.shape[2]
    per = LANES // BC
    for first in range(0, blocks, LANES):
        count = min(LANES, blocks - first)
        for f in range(frames):
            pair = scales[f, :, first : first + count].astype(F32)
            if count < LANES:
                pair = jnp.concatenate([pair, jnp.zeros((2, LANES - count), F32)], axis=1)
            factors = jnp.where(
                upper,
                jnp.broadcast_to(pair[0:1], (rows, LANES)),
                jnp.broadcast_to(pair[1:2], (rows, LANES)),
            )
            for k in range(count // per):
                column = (first // per + k) * LANES
                spread = jnp.take_along_axis(factors, lane + per * k, axis=1)
                codes = raw[f, :, column : column + LANES].astype(F32)
                dequant[f * rows : (f + 1) * rows, LANES + column : 2 * LANES + column] = (
                    codes * spread
                )


def cut_message(dequant, tile, h, count):
    start = CORE * tile - MARGIN + LANES
    aligned = pl.multiple_of(start // LANES * LANES, LANES)
    offset = start - aligned + MARGIN
    wide = dequant[h * count : (h + 1) * count, pl.ds(aligned, TW + LANES)]
    wide = pltpu.roll(wide, TW + LANES - offset, 1)
    lane = lax.broadcasted_iota(jnp.int32, (1, LANES), 1)
    last = jnp.where(lane < LANES - MARGIN, wide[:, TW - LANES : TW], wide[:, TW:])
    return jnp.concatenate([wide[:, : TW - LANES], last], axis=1).astype(BF16)


def centred():
    y = lax.broadcasted_iota(jnp.int32, (TH, 1), 0).astype(F32) - (TH - 1) / 2.0
    lane = lax.broadcasted_iota(jnp.int32, (1, TW), 1)
    x = lane.astype(F32) - (CORE - 1) / 2.0
    return y, x, lane


Y_NORM = float(np.sum((np.arange(TH) - (TH - 1) / 2.0) ** 2) * CORE)
X_NORM = float(np.sum((np.arange(CORE) - (CORE - 1) / 2.0) ** 2) * TH)


def parity_pick(parity):
    v = lax.broadcasted_iota(jnp.int32, (PC, LANES), 0)
    lane = lax.broadcasted_iota(jnp.int32, (PC, LANES), 1)
    return ones_where(v == 2 * (lane & (PC // 2 - 1)) + parity)


def build_band(half, pd, cols, fold, pairs):
    lane = lax.broadcasted_iota(jnp.int32, (1, TW), 1)
    sign = (2 - 4 * (lane & 1)).astype(F32)
    left = lane[:, :LANES] < LANES // 2
    for h in (0, 1):
        re, im = (
            jnp.concatenate(
                [
                    half[h, c, TH - PC // 2 :, :].astype(F32) * 2.0,
                    half[h, c, : PC // 2, :].astype(F32) * sign,
                ],
                axis=0,
            )
            for c in (0, 1)
        )
        cols[h, :PC, :TW] = re.astype(BF16)
        cols[h, :PC, TW:] = im.astype(BF16)
        cols[h, PC:, :TW] = (-im).astype(BF16)
        cols[h, PC:, TW:] = re.astype(BF16)
        turned = [part[:, :TH].T.astype(BF16) for part in (re, im)]
        for parity in (0, 1):
            a, b = (dot(part, parity_pick(parity)) for part in turned)
            cut = slice(h * LANES, (h + 1) * LANES)
            fold[parity, :TH, cut] = jnp.where(left, a, -b).astype(BF16)
            fold[parity, TH:, cut] = jnp.where(left, b, a).astype(BF16)
    for c in (0, 1):
        hi = pd[c].astype(BF16)
        lo, last = split(pd[c] - hi.astype(F32))
        for parity in (0, 1):
            pick = parity_pick(parity)
            pairs[c, parity] = dot(hi, pick) + dot(lo, pick) + dot(last, pick)


def build_columns(half, table):
    lane = lax.broadcasted_iota(jnp.int32, (1, TW), 1)
    sign = (1 - 2 * (lane & 1)).astype(F32)
    for i in (0, 1):
        rows = pl.ds(i * LANES, LANES)
        for h in (0, 1):
            re = half[h, 0, rows, :].astype(F32)
            im = half[h, 1, rows, :].astype(F32)
            for n, factor in ((0, None), (1, sign)):
                a = re if factor is None else re * factor
                b = im if factor is None else im * factor
                upper = pl.ds(n * LANES, LANES)
                lower = pl.ds((2 + n) * LANES, LANES)
                for k in range(BLOCKS):
                    cut = slice(k * LANES, (k + 1) * LANES)
                    table[i, h, k, upper, :LANES] = a[:, cut].astype(BF16)
                    table[i, h, k, upper, LANES:] = b[:, cut].astype(BF16)
                    table[i, h, k, lower, :LANES] = (-b[:, cut]).astype(BF16)
                    table[i, h, k, lower, LANES:] = a[:, cut].astype(BF16)


def object_rows(i, new, rows_table, lhs):
    parts = []
    for parity in (0, 1):
        data = [
            jnp.concatenate(
                [new[k, c, pl.ds(parity, HALF, stride=2), :] for k in (i, i + 2)], axis=1
            )
            for c in (0, 1)
        ]
        hi, lo = split(jnp.concatenate(data, axis=0))
        t_hi, t_lo = rows_table[parity, 0], rows_table[parity, 1]
        parts.append(dot(t_hi, hi) + dot(t_hi, lo) + dot(t_lo, hi))
    for n, value in enumerate((parts[0] + parts[1], parts[0] - parts[1])):
        hi, lo = split(value)
        rows = pl.ds(n * HALF, HALF)
        for h, part in enumerate((hi, lo)):
            lhs[h, rows, : 2 * LANES] = part[:HALF]
            lhs[h, rows, 2 * LANES :] = part[HALF:]


def object_block(i, k, lhs, table):
    hi, lo = lhs[0], lhs[1]
    return dot(hi, table[i, 0, k]) + dot(lo, table[i, 0, k]) + dot(hi, table[i, 1, k])


def encode(value, code, unit):
    for g in range(TH // CODE_ROWS):
        rows = slice(g * CODE_ROWS, (g + 1) * CODE_ROWS)
        piece = value[rows]
        top = jnp.max(jnp.abs(piece), axis=0, keepdims=True)
        unit[g : g + 1] = top * (1.0 / CODE_TOP)
        ratio = jnp.where(top > 0.0, CODE_TOP / top, 0.0)
        whole = jnp.clip(jnp.round(piece * ratio), -CODE_TOP, CODE_TOP)
        code[rows] = whole.astype(jnp.int32).astype(jnp.int16)


def decode(code, unit):
    return jnp.concatenate(
        [
            code[g * CODE_ROWS : (g + 1) * CODE_ROWS].astype(jnp.int32).astype(F32)
            * unit[g : g + 1]
            for g in range(TH // CODE_ROWS)
        ],
        axis=0,
    )


def update_kernel(
    tiles,
    pat_h,
    lrow_h,
    lcol_h,
    raw_h,
    scales_h,
    flat_h,
    spec_h,
    pup_h,
    spread_h,
    gather_h,
    rows_h,
    half_h,
    fresh,
    stitched,
    pat,
    lrow,
    lcol,
    raw,
    scales,
    flat,
    spec,
    pup,
    spread,
    gather,
    rows_table,
    half,
    cols,
    fold,
    pairs,
    bands,
    dequant,
    message,
    arrived,
    window,
    gains,
    flat_out,
    flat_in,
    slope_out,
    slope_in,
    sums,
    coef,
    halves,
    pd,
    wide,
    lit,
    mid,
    field,
    estimate,
    grad,
    got,
    code,
    unit,
    far_code,
    far_unit,
    new,
    table,
    lhs,
    image,
    edge_out,
    edge_in,
    load,
    send,
    recv,
    side_send,
    side_recv,
):
    frames = raw.shape[0]
    rows = raw.shape[1]
    group = lax.axis_index("grp")
    tile = lax.axis_index("tile")
    core = lax.rem(group, 2)
    mate = {"grp": group + 1 - 2 * core}
    partner = {"grp": group + 2 - 4 * lax.div(group, 2)}
    right = {"tile": lax.rem(tile + 1, tiles)}
    left = {"tile": lax.rem(tile + tiles - 1, tiles)}

    def side(number, src, dst, device):
        return pltpu.make_async_remote_copy(
            src_ref=src,
            dst_ref=dst,
            send_sem=side_send.at[number],
            recv_sem=side_recv.at[number],
            device_id=device,
            device_id_type=MESH,
        )

    def block(h, source, target):
        return pltpu.make_async_remote_copy(
            src_ref=message.at[h, target],
            dst_ref=arrived.at[h, source],
            send_sem=send.at[h, target],
            recv_sem=recv.at[h, source],
            device_id={"tile": target},
            device_id_type=MESH,
        )

    loads = [
        pltpu.make_async_copy(src, dst, load.at[n])
        for n, (src, dst) in enumerate(
            (
                (raw_h, raw),
                (scales_h, scales),
                (pat_h, pat),
                (lrow_h, lrow),
                (lcol_h, lcol),
                (flat_h, flat),
                (spec_h, spec),
                (pup_h, pup),
                (half_h, half),
                (spread_h, spread),
                (gather_h, gather),
                (rows_h, rows_table),
            )
        )
    ]
    for copy in loads:
        copy.start()
    barrier = pltpu.get_barrier_semaphore()

    @pl.loop(1, tiles)
    def _(i):
        pl.semaphore_signal(
            barrier, inc=1, device_id={"tile": lax.rem(tile + i, tiles)}, device_id_type=MESH
        )

    for device in (mate, partner):
        pl.semaphore_signal(barrier, inc=1, device_id=device, device_id_type=MESH)

    loads[0].wait()
    loads[1].wait()
    dequantize(raw, scales, dequant)
    pl.semaphore_wait(barrier, tiles + 1)

    each = frames // 2

    for h in (0, 1):

        @pl.loop(1, tiles)
        def _(i):
            target = lax.rem(tile + i, tiles)
            message[h, target] = cut_message(dequant, target, h, each * rows)
            block(h, tile, target).start()

        arrived[h, tile] = cut_message(dequant, tile, h, each * rows)

    loads[5].wait()
    for k in range(BLOCKS - 1):
        gains[:, k * LANES : (k + 1) * LANES] = flat[k * LANES : (k + 1) * LANES, :].T
    tail = jnp.concatenate(
        [flat[3 * LANES :, :], jnp.zeros((TW - CORE, TH), F32)], axis=0
    ).T
    gains[:, 3 * LANES :] = tail
    flat_out[0] = pack_edge(tail, 80)
    flat_out[1] = pack_edge(gains[:, :LANES], 0)
    flats = [
        side(0, flat_out.at[0], flat_in.at[0], right),
        side(1, flat_out.at[1], flat_in.at[1], left),
    ]
    for copy in flats:
        copy.start()

    for copy in loads[2:5] + loads[6:]:
        copy.wait()
    load_halves(spec, pup, halves, pd)
    build_band(half, pd, cols, fold, pairs)
    first_frame = group * frames

    def forward(f):
        estimate[f] = forward_frame(
            f, first_frame + f, pat, lrow, lcol, halves, pd, cols, spread, wide, lit, mid, field
        )

    pl.loop(0, frames)(forward)

    y, x, lane = centred()
    edge = lane[:, 3 * LANES :]
    for copy in flats:
        copy.wait_recv()
    outer = jnp.where(
        edge < CORE + MARGIN, unpack_edge(flat_in[1], 96), unpack_edge(flat_in[0], 112)
    )
    own = edge < CORE
    after = edge < CORE + MARGIN
    blank = ((~own) & after & (tile == tiles - 1)) | ((~after) & (tile == 0))
    gains[:, 3 * LANES :] = jnp.where(
        blank, 0.0, jnp.where(own, gains[:, 3 * LANES :], outer)
    )
    sums[...] = jnp.zeros_like(sums)
    slope_out[...] = jnp.zeros_like(slope_out)

    inside = (lane < CORE).astype(F32)
    x_edge = x[:, 3 * LANES :]

    def receive(h):
        @pl.loop(1, tiles + 1)
        def _(i):
            source = lax.rem(tile + tiles - i, tiles)

            @pl.when(i < tiles)
            def _():
                block(h, source, tile).wait_recv()

            here = pl.ds(pl.multiple_of(source * rows, rows), rows)
            values = arrived[h, source].astype(F32)
            place = y[:rows] + (source * rows).astype(F32)
            for n in range(each):
                f = h * each + n
                flattened = values[n * rows : (n + 1) * rows] * gains[here, :]
                window[f, here, :] = flattened
                sums[0, f] += flattened
                sums[1, f] += flattened * place

        slopes = []
        for n in range(each):
            f = h * each + n
            columns = jnp.sum(sums[0, f], axis=0, keepdims=True)
            tilted = jnp.sum(sums[1, f], axis=0, keepdims=True)
            slope_y = jnp.sum(tilted * inside, axis=1, keepdims=True) / Y_NORM
            slope_x = jnp.sum(columns * (x * inside), axis=1, keepdims=True) / X_NORM
            slopes.append((slope_y, slope_x))
            slope_out[h, n : n + 1] = jnp.broadcast_to(slope_y, (1, LANES))
            slope_out[h, each + n : each + n + 1] = jnp.broadcast_to(slope_x, (1, LANES))
        number = 2 if h == 0 else 22
        pair = [
            side(number, slope_out.at[h], slope_in.at[h, 0], right),
            side(number + 1, slope_out.at[h], slope_in.at[h, 1], left),
        ]
        for copy in pair:
            copy.start()
        return slopes, pair

    def backward(h, slopes, pair):
        for copy in pair:
            copy.wait_recv()
        for n in range(each):
            f = h * each + n
            slope_y, slope_x = slopes[n]
            coef[f, 0:1, : 3 * LANES] = jnp.broadcast_to(slope_y, (1, 3 * LANES))
            coef[f, 1:2, : 3 * LANES] = slope_x * x[:, : 3 * LANES]
            row_y = jnp.where(
                own,
                slope_y,
                jnp.where(after, slope_in[h, 1, n : n + 1], slope_in[h, 0, n : n + 1]),
            )
            row_x = jnp.where(
                own,
                slope_x * x_edge,
                jnp.where(
                    after,
                    slope_in[h, 1, each + n : each + n + 1] * (x_edge - CORE),
                    slope_in[h, 0, each + n : each + n + 1] * (x_edge - 32.0),
                ),
            )
            coef[f, 0:1, 3 * LANES :] = jnp.where(blank, 0.0, row_y)
            coef[f, 1:2, 3 * LANES :] = jnp.where(blank, 0.0, row_x)

        @pl.loop(h * each, (h + 1) * each)
        def _(f):
            misfit = estimate[f] - window[f] + coef[f, 0:1] * y + coef[f, 1:2]
            backward_frame(
                f, first_frame + f, misfit, pat, lrow, lcol, pairs, fold, gather, field, bands, wide
            )

    slopes, copies = receive(0)
    later_slopes, later = receive(1)
    backward(0, slopes, copies)
    backward(1, later_slopes, later)
    copies = copies + later

    choose = row_places(first_frame, frames, pat, lrow, lcol)
    place_pair(1 - core, choose, wide, grad)

    pieces = [(i, c) for i in (0, 1) for c in (0, 1)]
    first = [
        side(4 + n, grad.at[2 - 2 * core + i, c], got.at[i, c], mate)
        for n, (i, c) in enumerate(pieces)
    ]
    for copy in first:
        copy.start()
    place_pair(core, choose, wide, grad)
    second = []
    units = []
    for n, (i, c) in enumerate(pieces):
        first[n].wait_recv()
        encode(grad[2 * core + i, c] + got[i, c], code.at[n], unit.at[n])
        second.append(side(8 + n, code.at[n], far_code.at[n], partner))
        units.append(side(18 + n, unit.at[n], far_unit.at[n], partner))
        units[n].start()
        second[n].start()
    build_columns(half, table)
    third = []
    for i in (0, 1):
        mine = 2 * core + i
        lanes = pl.ds(pl.multiple_of(mine * LANES, LANES), LANES)
        for c in (0, 1):
            n = 2 * i + c
            units[n].wait_recv()
            second[n].wait_recv()
            total = decode(code.at[n], unit.at[n]) + decode(far_code.at[n], far_unit.at[n])
            new[mine, c] = spec[c, :, lanes] - STEP * total
            third.append(side(12 + n, new.at[mine, c], new.at[mine, c], mate))
            third[n].start()
        for c in (0, 1):
            third[2 * i + c].wait_recv()
        for k in (i, i + 2):
            fresh[:, :, k * LANES : (k + 1) * LANES] = new[k]
        object_rows(i, new, rows_table, lhs)
        if i == 0:
            for k in range(BLOCKS):
                image[k] = object_block(i, k, lhs, table)
    image[3] += object_block(1, 3, lhs, table)
    for c in (0, 1):
        value = image[3, :, c * LANES : (c + 1) * LANES]
        edge_out[0, c] = pack_edge(value, 96)
        edge_out[1, c] = pack_edge(value, 112)
    edges = [
        side(16, edge_out.at[0], edge_in.at[0], right),
        side(17, edge_out.at[1], edge_in.at[1], left),
    ]
    for copy in edges:
        copy.start()
    for k in range(BLOCKS - 1):
        image[k] += object_block(1, k, lhs, table)
    for c in (0, 1):
        for k in (1, 2):
            stitched[c, k * LANES : (k + 1) * LANES, :] = image[
                k, :, c * LANES : (c + 1) * LANES
            ].T
    place = edge.astype(F32) - float(3 * LANES)
    at_head = (place < MARGIN) & (tile > 0)
    at_tail = (place >= 80) & (place < 96) & (tile < tiles - 1)
    for copy in edges:
        copy.wait_recv()
    for c in (0, 1):
        mine = image[0, :, c * LANES : (c + 1) * LANES]
        other = unpack_edge(edge_in[0, c], 0)
        blend = mine * ((place + 16.5) / OV) + other * ((15.5 - place) / OV)
        stitched[c, :LANES, :] = jnp.where(at_head, blend, mine).T
        mine = image[3, :, c * LANES : (c + 1) * LANES]
        other = unpack_edge(edge_in[1, c], 80)
        blend = mine * ((111.5 - place) / OV) + other * ((place - 79.5) / OV)
        stitched[c, 3 * LANES :, :] = jnp.where(at_tail, blend, mine).T[: CORE - 3 * LANES]
    for copy in flats + copies + first + second + units + third + edges:
        copy.wait_send()

    for h in (0, 1):

        @pl.loop(1, tiles)
        def _(i):
            block(h, tile, lax.rem(tile + i, tiles)).wait_send()


def update(raw, scales, flat, spectrum, pupil, patterns, led_row, led_col):
    tiles = lax.axis_size("tile")
    frames, rows, width = raw.shape
    deep = frames * rows
    tables = [jnp.asarray(t) for t in band_tables() + object_tables()]
    picks = [patterns, led_row, led_col]
    hbm = pl.BlockSpec(memory_space=pltpu.MemorySpace.HBM)
    arrays = [
        pltpu.with_memory_space_constraint(a, pltpu.MemorySpace.HBM)
        for a in picks + [raw, scales, flat, spectrum, pupil] + tables
    ]
    small = (TH // 8, LANES)
    part = (2, TH, LANES)
    scratch = [pltpu.SMEM(a.shape, a.dtype) for a in picks]
    scratch += [pltpu.VMEM(a.shape, a.dtype) for a in arrays[3:]]
    scratch += [
        pltpu.VMEM((2, 2 * PC, 2 * TW), BF16),
        pltpu.VMEM((2, 2 * TH, 2 * LANES), BF16),
        pltpu.VMEM((2, 2, PR, LANES), F32),
        pltpu.VMEM((2, TH, 2 * LEDS * LANES), BF16),
        pltpu.VMEM((deep, width + 2 * LANES), F32),
        pltpu.VMEM((2, tiles, deep // 2, TW), BF16),
        pltpu.VMEM((2, tiles, deep // 2, TW), BF16),
        pltpu.VMEM((frames, TH, TW), F32),
        pltpu.VMEM((TH, TW), F32),
        pltpu.VMEM((2,) + small, F32),
        pltpu.VMEM((2,) + small, F32),
        pltpu.VMEM((2, 8, LANES), F32),
        pltpu.VMEM((2, 2, 8, LANES), F32),
        pltpu.VMEM((2, frames, rows, TW), F32),
        pltpu.VMEM((frames, 8, TW), F32),
        pltpu.VMEM((2, TH, 2 * TW), BF16),
        pltpu.VMEM((2, PR, PC), F32),
        pltpu.VMEM((2, frames * LEDS * PR, 2 * TW), BF16),
        pltpu.VMEM((LEDS * PR, 2 * PC), F32),
        pltpu.VMEM((LEDS * PR, 2 * TW), F32),
        pltpu.VMEM((frames, LEDS, 2, TH, TW), F32),
        pltpu.VMEM((frames, TH, TW), F32),
        pltpu.VMEM((BLOCKS,) + part, F32),
        pltpu.VMEM((2,) + part, F32),
        pltpu.VMEM((4, TH, LANES), jnp.int16),
        pltpu.VMEM((4, TH // CODE_ROWS, LANES), F32),
        pltpu.VMEM((4, TH, LANES), jnp.int16),
        pltpu.VMEM((4, TH // CODE_ROWS, LANES), F32),
        pltpu.VMEM((BLOCKS,) + part, F32),
        pltpu.VMEM((2, 2, BLOCKS, TW, 2 * LANES), BF16),
        pltpu.VMEM((2, TH, TW), BF16),
        pltpu.VMEM((BLOCKS, TH, 2 * LANES), F32),
        pltpu.VMEM((2, 2) + small, F32),
        pltpu.VMEM((2, 2) + small, F32),
        pltpu.SemaphoreType.DMA((12,)),
        pltpu.SemaphoreType.DMA((2, tiles)),
        pltpu.SemaphoreType.DMA((2, tiles)),
        pltpu.SemaphoreType.DMA((24,)),
        pltpu.SemaphoreType.DMA((24,)),
    ]
    return pl.pallas_call(
        functools.partial(update_kernel, tiles),
        in_specs=[hbm] * len(arrays),
        out_specs=[pl.BlockSpec(memory_space=pltpu.VMEM)] * 2,
        out_shape=[
            jax.ShapeDtypeStruct((2, TH, TW), F32),
            jax.ShapeDtypeStruct((2, CORE, TH), F32),
        ],
        scratch_shapes=scratch,
        compiler_params=pltpu.CompilerParams(
            collective_id=1, has_side_effects=True, vmem_limit_bytes=50 * 2**20
        ),
        name="update",
    )(*arrays)


def hand_over(first, second, first_out, second_out, sem):
    copies = [
        pltpu.make_async_copy(src.at[c], dst.at[c], sem.at[2 * n + c])
        for n, (src, dst) in enumerate(((first, first_out), (second, second_out)))
        for c in (0, 1)
    ]
    for copy in copies:
        copy.start()
    for copy in copies:
        copy.wait()


def deliver(fresh, stitched):
    hbm = pl.BlockSpec(memory_space=pltpu.MemorySpace.HBM)
    return pl.pallas_call(
        hand_over,
        in_specs=[pl.BlockSpec(memory_space=pltpu.VMEM)] * 2,
        out_specs=[hbm] * 2,
        out_shape=[jax.ShapeDtypeStruct(a.shape, a.dtype) for a in (fresh, stitched)],
        scratch_shapes=[pltpu.SemaphoreType.DMA((4,))],
        compiler_params=pltpu.CompilerParams(vmem_limit_bytes=4 * 2**20),
        name="deliver",
    )(fresh, stitched)


def body(raw, scales, flat, spectrum, pupil, patterns, led_row, led_col):
    fresh, stitched = update(
        raw, scales, flat.T, spectrum[0], pupil, patterns.T, led_row, led_col
    )
    fresh, stitched = deliver(fresh, stitched)
    return (fresh[None], jnp.swapaxes(stitched, 1, 2))


def solution(mesh):
    return jax.shard_map(
        body,
        mesh=mesh,
        in_specs=(
            P("grp", "tile", None),
            P("grp", "tile", None),
            P(None, "tile"),
            P("tile", None, None, None),
            P(),
            P(),
            P(),
            P(),
        ),
        out_specs=(P("tile", None, None, None), P(None, None, "tile")),
        check_vma=False,
    )
```

```python
import functools
import math

import jax
import jax.numpy as jnp
import ml_dtypes
import numpy as np
from jax import lax
from jax.experimental import pallas as pl
from jax.experimental.pallas import tpu as pltpu
from jax.sharding import PartitionSpec as P

TH = 256
TW = 512
OV = 32
BR = 4
BC = 32
PR = 64
PC = 128
FR_G = 4
LEDS = 4
HALF = TH // 2
HR = PR // 2
MARGIN = OV // 2
CORE = TW - OV
LANES = 128
BLOCKS = TW // LANES
MESH = pl.DeviceIdType.MESH
CODE_ROWS = 32
CODE_TOP = 32767.0
STEP = 0.02
F32 = jnp.float32
BF16 = jnp.bfloat16


def split_np(table):
    hi = table.astype(ml_dtypes.bfloat16)
    lo = (table - hi.astype(np.float64)).astype(ml_dtypes.bfloat16)
    return hi, lo


def wave_np(length, band):
    places = np.arange(length)[:, None]
    freqs = np.arange(band)[None, :] - band // 2
    angle = (places * freqs % length) * (2.0 * np.pi / length)
    return np.cos(angle) / math.sqrt(band), np.sin(angle) / math.sqrt(band)


def object_tables():
    re, im = wave_np(TH, TH)
    rows = []
    for parity in (0, 1):
        a, b = re[:HALF, parity::2], im[:HALF, parity::2]
        rows.append(np.stack(split_np(np.block([[a, -b], [b, a]]))))
    re, im = (np.roll(part.T, -MARGIN, axis=1)[:TH] for part in wave_np(TW, TW))
    cols = np.stack([np.stack(split_np(re)), np.stack(split_np(im))], axis=1)
    return np.stack(rows), cols


def band_tables():
    row_re, row_im = wave_np(TH, PR)
    spread = []
    for parity in (0, 1):
        re = row_re[:HALF, parity::2]
        im = row_im[:HALF, parity::2]
        rows_hi, rows_lo = split_np(np.block([[re, -im], [im, re]]))
        spread.append(np.concatenate([rows_hi, rows_hi, rows_lo, rows_lo], axis=1))
    order = np.concatenate([np.arange(0, PR, 2), np.arange(1, PR, 2)])
    gather = np.concatenate(split_np(np.concatenate([row_re.T[order], row_im.T[order]])))
    return np.stack(spread), gather


def split(x):
    hi = x.astype(BF16)
    return hi, (x - hi.astype(F32)).astype(BF16)


def dot(a, b):
    return jnp.dot(a, b, preferred_element_type=F32)


def box_corner(pat, lrow, lcol, frame, j):
    led = pat[j, frame]
    return lrow[led], lcol[led]


def row_order(index):
    return jnp.where(index < HR, 2 * index, 2 * index - (PR - 1))


def ones_where(condition):
    return jnp.where(condition, 1.0, 0.0).astype(BF16)


def column_select(col):
    x = lax.broadcasted_iota(jnp.int32, (TW, PC), 0)
    v = lax.broadcasted_iota(jnp.int32, (TW, PC), 1)
    return ones_where(x - v == col)


def column_place(col):
    v = lax.broadcasted_iota(jnp.int32, (PC, TW), 0)
    v = jnp.where(v < PC // 2, 2 * v, 2 * v - (PC - 1))
    x = lax.broadcasted_iota(jnp.int32, (PC, TW), 1)
    return ones_where(x - v == col)


def load_halves(spec, pup, halves, pd):
    for c in (0, 1):
        hi, lo = split(spec[c])
        halves[0, :, c * TW : (c + 1) * TW] = hi
        halves[1, :, c * TW : (c + 1) * TW] = lo
        for parity in (0, 1):
            pd[c, parity * HR : (parity + 1) * HR] = pup[c, pl.ds(parity, HR, stride=2), :]


def forward_frame(f, frame, pat, lrow, lcol, halves, pd, cols, spread, picked, lit, mid, field):
    y = lax.broadcasted_iota(jnp.int32, (PR, TH), 1)
    order = row_order(lax.broadcasted_iota(jnp.int32, (PR, TH), 0))
    corners = [box_corner(pat, lrow, lcol, frame, j) for j in range(LEDS)]
    choose = jnp.concatenate([ones_where(y - order == row) for row, _ in corners], axis=0)
    for h in (0, 1):
        picked[h, : LEDS * PR] = dot(choose, halves[h]).astype(BF16)
    p_re, p_im = pd[0], pd[1]
    for j in range(LEDS):
        rows = pl.ds(j * PR, PR)
        stack = jnp.concatenate(
            [picked[h, rows, c * TW : (c + 1) * TW] for h in (0, 1) for c in (0, 1)], axis=0
        )
        cut = dot(stack, column_select(corners[j][1]))
        b_re = cut[:PR] + cut[2 * PR : 3 * PR]
        b_im = cut[PR : 2 * PR] + cut[3 * PR :]
        lit[rows, :PC] = p_re * b_re - p_im * b_im
        lit[rows, PC:] = p_re * b_im + p_im * b_re
    hi, lo = split(lit[...])
    mid[...] = dot(hi, cols[0]) + dot(lo, cols[0]) + dot(hi, cols[1])
    estimate = None
    for j in range(LEDS):
        parts = []
        for parity in (0, 1):
            rows = pl.ds(j * PR + parity * HR, HR)
            re_hi, re_lo = split(mid[rows, :TW])
            im_hi, im_lo = split(mid[rows, TW:])
            both = jnp.concatenate([re_hi, im_hi, re_lo, im_lo], axis=0)
            parts.append(dot(spread[parity], jnp.concatenate([both, both], axis=0)))
        upper = parts[0] + parts[1]
        lower = parts[0] - parts[1]
        field[f, j, 0, :HALF] = upper[:HALF]
        field[f, j, 0, HALF:] = lower[:HALF]
        field[f, j, 1, :HALF] = upper[HALF:]
        field[f, j, 1, HALF:] = lower[HALF:]
        power = jnp.concatenate(
            [
                upper[:HALF] * upper[:HALF] + upper[HALF:] * upper[HALF:],
                lower[:HALF] * lower[:HALF] + lower[HALF:] * lower[HALF:],
            ],
            axis=0,
        )
        estimate = power if estimate is None else estimate + power
    return estimate


def backward_frame(f, frame, misfit, pat, lrow, lcol, pairs, fold, gather, field, bands, wide):
    for j in range(LEDS):
        weighted = [misfit * field[f, j, c] for c in (0, 1)]
        for parity in (0, 1):
            mix = [
                w[:, :TH] + w[:, TH:] if parity == 0 else w[:, :TH] - w[:, TH:]
                for w in weighted
            ]
            hi, lo = split(jnp.concatenate(mix, axis=1))
            first = dot(hi, fold[parity])
            total = first[:, :LANES] + first[:, LANES:] + dot(lo, fold[parity, :, :LANES])
            hi, lo = split(total)
            cut = slice((2 * j + parity) * LANES, (2 * j + parity + 1) * LANES)
            bands[0, :, cut] = hi
            bands[1, :, cut] = lo
    first = dot(gather[...], bands[0])
    second = dot(gather[: 2 * PR], bands[1])
    by_re = first[:PR] + first[2 * PR : 3 * PR] + second[:PR]
    by_im = first[PR : 2 * PR] + first[3 * PR :] + second[PR:]
    left = lax.broadcasted_iota(jnp.int32, (1, LANES), 1) < LANES // 2
    sign = jnp.where(left, 1.0, -1.0)
    turn = LANES // 2
    for j in range(LEDS):
        col = box_corner(pat, lrow, lcol, frame, j)[1]
        halves = []
        for parity in (0, 1):
            cut = slice((2 * j + parity) * LANES, (2 * j + parity + 1) * LANES)
            band = by_re[:, cut] + sign * pltpu.roll(by_im[:, cut], turn, 1)
            halves.append(
                pairs[0, parity] * band + sign * pairs[1, parity] * pltpu.roll(band, turn, 1)
            )
        even, odd = halves
        re_hi, re_lo = split(jnp.where(left, even, pltpu.roll(odd, turn, 1)))
        im_hi, im_lo = split(jnp.where(left, pltpu.roll(even, turn, 1), odd))
        stack = jnp.concatenate([re_hi, im_hi, re_lo, im_lo], axis=0)
        placed = dot(stack, column_place(col)).astype(BF16)
        rows = pl.ds(pl.multiple_of((f * LEDS + j) * PR, PR), PR)
        for h in (0, 1):
            for c in (0, 1):
                n = 2 * h + c
                wide[h, rows, c * TW : (c + 1) * TW] = placed[n * PR : (n + 1) * PR]


def row_places(first_frame, frames, pat, lrow, lcol):
    total_rows = frames * LEDS * PR
    lane = lax.broadcasted_iota(jnp.int32, (1, total_rows), 1)
    box = lane // PR
    target = row_order(lane & (PR - 1))
    for f in range(frames):
        for j in range(LEDS):
            row = box_corner(pat, lrow, lcol, first_frame + f, j)[0]
            target = target + jnp.where(box == f * LEDS + j, row, 0)
    return ones_where(lax.broadcasted_iota(jnp.int32, (TH, total_rows), 0) == target)


def place_pair(which, choose, wide, grad):
    for c in (0, 1):
        cut = pl.ds(pl.multiple_of(c * TW + which * (2 * LANES), LANES), 2 * LANES)
        both = dot(choose, wide[0, :, cut]) + dot(choose, wide[1, :, cut])
        for n in (0, 1):
            grad[2 * which + n, c] = both[:, n * LANES : (n + 1) * LANES]


def pack_edge(value, first):
    lane = lax.broadcasted_iota(jnp.int32, (TH // 8, LANES), 1) // MARGIN
    packed = jnp.zeros((TH // 8, LANES), F32)
    for b in range(8):
        piece = value[b * 32 : (b + 1) * 32]
        piece = pltpu.roll(piece, (MARGIN * b - first) % LANES, 1)
        packed = jnp.where(lane == b, piece, packed)
    return packed


def unpack_edge(packed, first):
    return jnp.concatenate(
        [pltpu.roll(packed, (first - MARGIN * b) % LANES, 1) for b in range(8)], axis=0
    )


def dequantize(raw, scales, dequant):
    frames, rows, width = raw.shape
    dequant[:, :LANES] = jnp.zeros((frames * rows, LANES), F32)
    dequant[:, LANES + width :] = jnp.zeros((frames * rows, LANES), F32)
    lane = lax.broadcasted_iota(jnp.int32, (rows, LANES), 1) // BC
    upper = lax.broadcasted_iota(jnp.int32, (rows, LANES), 0) < BR
    blocks = scales.shape[2]
    per = LANES // BC
    for first in range(0, blocks, LANES):
        count = min(LANES, blocks - first)
        for f in range(frames):
            pair = scales[f, :, first : first + count].astype(F32)
            if count < LANES:
                pair = jnp.concatenate([pair, jnp.zeros((2, LANES - count), F32)], axis=1)
            factors = jnp.where(
                upper,
                jnp.broadcast_to(pair[0:1], (rows, LANES)),
                jnp.broadcast_to(pair[1:2], (rows, LANES)),
            )
            for k in range(count // per):
                column = (first // per + k) * LANES
                spread = jnp.take_along_axis(factors, lane + per * k, axis=1)
                codes = raw[f, :, column : column + LANES].astype(F32)
                dequant[f * rows : (f + 1) * rows, LANES + column : 2 * LANES + column] = (
                    codes * spread
                )


def cut_message(dequant, tile, h, count):
    start = CORE * tile - MARGIN + LANES
    aligned = pl.multiple_of(start // LANES * LANES, LANES)
    offset = start - aligned + MARGIN
    wide = dequant[h * count : (h + 1) * count, pl.ds(aligned, TW + LANES)]
    wide = pltpu.roll(wide, TW + LANES - offset, 1)
    lane = lax.broadcasted_iota(jnp.int32, (1, LANES), 1)
    last = jnp.where(lane < LANES - MARGIN, wide[:, TW - LANES : TW], wide[:, TW:])
    return jnp.concatenate([wide[:, : TW - LANES], last], axis=1).astype(BF16)


def centred():
    y = lax.broadcasted_iota(jnp.int32, (TH, 1), 0).astype(F32) - (TH - 1) / 2.0
    lane = lax.broadcasted_iota(jnp.int32, (1, TW), 1)
    x = lane.astype(F32) - (CORE - 1) / 2.0
    return y, x, lane


Y_NORM = float(np.sum((np.arange(TH) - (TH - 1) / 2.0) ** 2) * CORE)
X_NORM = float(np.sum((np.arange(CORE) - (CORE - 1) / 2.0) ** 2) * TH)


def parity_pick(parity):
    v = lax.broadcasted_iota(jnp.int32, (PC, LANES), 0)
    lane = lax.broadcasted_iota(jnp.int32, (PC, LANES), 1)
    return ones_where(v == 2 * (lane & (PC // 2 - 1)) + parity)


def build_band(half, pd, cols, fold, pairs):
    lane = lax.broadcasted_iota(jnp.int32, (1, TW), 1)
    sign = (2 - 4 * (lane & 1)).astype(F32)
    left = lane[:, :LANES] < LANES // 2
    for h in (0, 1):
        re, im = (
            jnp.concatenate(
                [
                    half[h, c, TH - PC // 2 :, :].astype(F32) * 2.0,
                    half[h, c, : PC // 2, :].astype(F32) * sign,
                ],
                axis=0,
            )
            for c in (0, 1)
        )
        cols[h, :PC, :TW] = re.astype(BF16)
        cols[h, :PC, TW:] = im.astype(BF16)
        cols[h, PC:, :TW] = (-im).astype(BF16)
        cols[h, PC:, TW:] = re.astype(BF16)
        turned = [part[:, :TH].T.astype(BF16) for part in (re, im)]
        for parity in (0, 1):
            a, b = (dot(part, parity_pick(parity)) for part in turned)
            cut = slice(h * LANES, (h + 1) * LANES)
            fold[parity, :TH, cut] = jnp.where(left, a, -b).astype(BF16)
            fold[parity, TH:, cut] = jnp.where(left, b, a).astype(BF16)
    for c in (0, 1):
        hi = pd[c].astype(BF16)
        lo, last = split(pd[c] - hi.astype(F32))
        for parity in (0, 1):
            pick = parity_pick(parity)
            pairs[c, parity] = dot(hi, pick) + dot(lo, pick) + dot(last, pick)


def build_columns(half, table):
    lane = lax.broadcasted_iota(jnp.int32, (1, TW), 1)
    sign = (1 - 2 * (lane & 1)).astype(F32)
    for i in (0, 1):
        rows = pl.ds(i * LANES, LANES)
        for h in (0, 1):
            re = half[h, 0, rows, :].astype(F32)
            im = half[h, 1, rows, :].astype(F32)
            for n, factor in ((0, None), (1, sign)):
                a = re if factor is None else re * factor
                b = im if factor is None else im * factor
                upper = pl.ds(n * LANES, LANES)
                lower = pl.ds((2 + n) * LANES, LANES)
                for k in range(BLOCKS):
                    cut = slice(k * LANES, (k + 1) * LANES)
                    table[i, h, k, upper, :LANES] = a[:, cut].astype(BF16)
                    table[i, h, k, upper, LANES:] = b[:, cut].astype(BF16)
                    table[i, h, k, lower, :LANES] = (-b[:, cut]).astype(BF16)
                    table[i, h, k, lower, LANES:] = a[:, cut].astype(BF16)


def object_rows(i, new, rows_table, lhs):
    parts = []
    for parity in (0, 1):
        data = [
            jnp.concatenate(
                [new[k, c, pl.ds(parity, HALF, stride=2), :] for k in (i, i + 2)], axis=1
            )
            for c in (0, 1)
        ]
        hi, lo = split(jnp.concatenate(data, axis=0))
        t_hi, t_lo = rows_table[parity, 0], rows_table[parity, 1]
        parts.append(dot(t_hi, hi) + dot(t_hi, lo) + dot(t_lo, hi))
    for n, value in enumerate((parts[0] + parts[1], parts[0] - parts[1])):
        hi, lo = split(value)
        rows = pl.ds(n * HALF, HALF)
        for h, part in enumerate((hi, lo)):
            lhs[h, rows, : 2 * LANES] = part[:HALF]
            lhs[h, rows, 2 * LANES :] = part[HALF:]


def object_block(i, k, lhs, table):
    hi, lo = lhs[0], lhs[1]
    return dot(hi, table[i, 0, k]) + dot(lo, table[i, 0, k]) + dot(hi, table[i, 1, k])


def encode(value, code, unit):
    for g in range(TH // CODE_ROWS):
        rows = slice(g * CODE_ROWS, (g + 1) * CODE_ROWS)
        piece = value[rows]
        top = jnp.max(jnp.abs(piece), axis=0, keepdims=True)
        unit[g : g + 1] = top * (1.0 / CODE_TOP)
        ratio = jnp.where(top > 0.0, CODE_TOP / top, 0.0)
        whole = jnp.clip(jnp.round(piece * ratio), -CODE_TOP, CODE_TOP)
        code[rows] = whole.astype(jnp.int32).astype(jnp.int16)


def decode(code, unit):
    return jnp.concatenate(
        [
            code[g * CODE_ROWS : (g + 1) * CODE_ROWS].astype(jnp.int32).astype(F32)
            * unit[g : g + 1]
            for g in range(TH // CODE_ROWS)
        ],
        axis=0,
    )


def update_kernel(
    tiles,
    pat_h,
    lrow_h,
    lcol_h,
    raw_h,
    scales_h,
    flat_h,
    spec_h,
    pup_h,
    spread_h,
    gather_h,
    rows_h,
    half_h,
    fresh,
    stitched,
    pat,
    lrow,
    lcol,
    raw,
    scales,
    flat,
    spec,
    pup,
    spread,
    gather,
    rows_table,
    half,
    cols,
    fold,
    pairs,
    bands,
    dequant,
    message,
    arrived,
    window,
    gains,
    flat_out,
    flat_in,
    slope_out,
    slope_in,
    sums,
    coef,
    halves,
    pd,
    wide,
    lit,
    mid,
    field,
    estimate,
    grad,
    got,
    code,
    unit,
    far_code,
    far_unit,
    new,
    table,
    lhs,
    image,
    edge_out,
    edge_in,
    load,
    send,
    recv,
    side_send,
    side_recv,
):
    frames = raw.shape[0]
    rows = raw.shape[1]
    group = lax.axis_index("grp")
    tile = lax.axis_index("tile")
    core = lax.rem(group, 2)
    mate = {"grp": group + 1 - 2 * core}
    partner = {"grp": group + 2 - 4 * lax.div(group, 2)}
    right = {"tile": lax.rem(tile + 1, tiles)}
    left = {"tile": lax.rem(tile + tiles - 1, tiles)}

    def side(number, src, dst, device):
        return pltpu.make_async_remote_copy(
            src_ref=src,
            dst_ref=dst,
            send_sem=side_send.at[number],
            recv_sem=side_recv.at[number],
            device_id=device,
            device_id_type=MESH,
        )

    def block(h, source, target):
        return pltpu.make_async_remote_copy(
            src_ref=message.at[h, target],
            dst_ref=arrived.at[h, source],
            send_sem=send.at[h, target],
            recv_sem=recv.at[h, source],
            device_id={"tile": target},
            device_id_type=MESH,
        )

    loads = [
        pltpu.make_async_copy(src, dst, load.at[n])
        for n, (src, dst) in enumerate(
            (
                (raw_h, raw),
                (scales_h, scales),
                (pat_h, pat),
                (lrow_h, lrow),
                (lcol_h, lcol),
                (flat_h, flat),
                (spec_h, spec),
                (pup_h, pup),
                (half_h, half),
                (spread_h, spread),
                (gather_h, gather),
                (rows_h, rows_table),
            )
        )
    ]
    for copy in loads:
        copy.start()
    barrier = pltpu.get_barrier_semaphore()

    @pl.loop(1, tiles)
    def _(i):
        pl.semaphore_signal(
            barrier, inc=1, device_id={"tile": lax.rem(tile + i, tiles)}, device_id_type=MESH
        )

    for device in (mate, partner):
        pl.semaphore_signal(barrier, inc=1, device_id=device, device_id_type=MESH)

    loads[0].wait()
    loads[1].wait()
    dequantize(raw, scales, dequant)
    pl.semaphore_wait(barrier, tiles + 1)

    each = frames // 2

    for h in (0, 1):

        @pl.loop(1, tiles)
        def _(i):
            target = lax.rem(tile + i, tiles)
            message[h, target] = cut_message(dequant, target, h, each * rows)
            block(h, tile, target).start()

        arrived[h, tile] = cut_message(dequant, tile, h, each * rows)

    loads[5].wait()
    for k in range(BLOCKS - 1):
        gains[:, k * LANES : (k + 1) * LANES] = flat[k * LANES : (k + 1) * LANES, :].T
    tail = jnp.concatenate(
        [flat[3 * LANES :, :], jnp.zeros((TW - CORE, TH), F32)], axis=0
    ).T
    gains[:, 3 * LANES :] = tail
    flat_out[0] = pack_edge(tail, 80)
    flat_out[1] = pack_edge(gains[:, :LANES], 0)
    flats = [
        side(0, flat_out.at[0], flat_in.at[0], right),
        side(1, flat_out.at[1], flat_in.at[1], left),
    ]
    for copy in flats:
        copy.start()

    for copy in loads[2:5] + loads[6:]:
        copy.wait()
    load_halves(spec, pup, halves, pd)
    build_band(half, pd, cols, fold, pairs)
    first_frame = group * frames

    def forward(f):
        estimate[f] = forward_frame(
            f, first_frame + f, pat, lrow, lcol, halves, pd, cols, spread, wide, lit, mid, field
        )

    pl.loop(0, frames - 1)(forward)

    y, x, lane = centred()
    edge = lane[:, 3 * LANES :]
    for copy in flats:
        copy.wait_recv()
    outer = jnp.where(
        edge < CORE + MARGIN, unpack_edge(flat_in[1], 96), unpack_edge(flat_in[0], 112)
    )
    own = edge < CORE
    after = edge < CORE + MARGIN
    blank = ((~own) & after & (tile == tiles - 1)) | ((~after) & (tile == 0))
    gains[:, 3 * LANES :] = jnp.where(
        blank, 0.0, jnp.where(own, gains[:, 3 * LANES :], outer)
    )
    sums[...] = jnp.zeros_like(sums)
    slope_out[...] = jnp.zeros_like(slope_out)

    inside = (lane < CORE).astype(F32)
    x_edge = x[:, 3 * LANES :]

    def receive(h):
        @pl.loop(1, tiles + 1)
        def _(i):
            source = lax.rem(tile + tiles - i, tiles)

            @pl.when(i < tiles)
            def _():
                block(h, source, tile).wait_recv()

            here = pl.ds(pl.multiple_of(source * rows, rows), rows)
            values = arrived[h, source].astype(F32)
            place = y[:rows] + (source * rows).astype(F32)
            for n in range(each):
                f = h * each + n
                flattened = values[n * rows : (n + 1) * rows] * gains[here, :]
                window[f, here, :] = flattened
                sums[0, f] += flattened
                sums[1, f] += flattened * place

        slopes = []
        for n in range(each):
            f = h * each + n
            columns = jnp.sum(sums[0, f], axis=0, keepdims=True)
            tilted = jnp.sum(sums[1, f], axis=0, keepdims=True)
            slope_y = jnp.sum(tilted * inside, axis=1, keepdims=True) / Y_NORM
            slope_x = jnp.sum(columns * (x * inside), axis=1, keepdims=True) / X_NORM
            slopes.append((slope_y, slope_x))
            slope_out[h, n : n + 1] = jnp.broadcast_to(slope_y, (1, LANES))
            slope_out[h, each + n : each + n + 1] = jnp.broadcast_to(slope_x, (1, LANES))
        number = 2 if h == 0 else 22
        pair = [
            side(number, slope_out.at[h], slope_in.at[h, 0], right),
            side(number + 1, slope_out.at[h], slope_in.at[h, 1], left),
        ]
        for copy in pair:
            copy.start()
        return slopes, pair

    def settle(h, slopes, pair):
        for copy in pair:
            copy.wait_recv()
        for n in range(each):
            f = h * each + n
            slope_y, slope_x = slopes[n]
            coef[f, 0:1, : 3 * LANES] = jnp.broadcast_to(slope_y, (1, 3 * LANES))
            coef[f, 1:2, : 3 * LANES] = slope_x * x[:, : 3 * LANES]
            row_y = jnp.where(
                own,
                slope_y,
                jnp.where(after, slope_in[h, 1, n : n + 1], slope_in[h, 0, n : n + 1]),
            )
            row_x = jnp.where(
                own,
                slope_x * x_edge,
                jnp.where(
                    after,
                    slope_in[h, 1, each + n : each + n + 1] * (x_edge - CORE),
                    slope_in[h, 0, each + n : each + n + 1] * (x_edge - 32.0),
                ),
            )
            coef[f, 0:1, 3 * LANES :] = jnp.where(blank, 0.0, row_y)
            coef[f, 1:2, 3 * LANES :] = jnp.where(blank, 0.0, row_x)

    def backward(start, stop):
        @pl.loop(start, stop)
        def _(f):
            misfit = estimate[f] - window[f] + coef[f, 0:1] * y + coef[f, 1:2]
            backward_frame(
                f, first_frame + f, misfit, pat, lrow, lcol, pairs, fold, gather, field, bands, wide
            )

    slopes, copies = receive(0)
    forward(frames - 1)
    settle(0, slopes, copies)
    backward(0, 1)
    slopes, later = receive(1)
    backward(1, each)
    settle(1, slopes, later)
    backward(each, frames)
    copies = copies + later

    choose = row_places(first_frame, frames, pat, lrow, lcol)
    place_pair(1 - core, choose, wide, grad)

    pieces = [(i, c) for i in (0, 1) for c in (0, 1)]
    first = [
        side(4 + n, grad.at[2 - 2 * core + i, c], got.at[i, c], mate)
        for n, (i, c) in enumerate(pieces)
    ]
    for copy in first:
        copy.start()
    place_pair(core, choose, wide, grad)
    second = []
    units = []
    for n, (i, c) in enumerate(pieces):
        first[n].wait_recv()
        encode(grad[2 * core + i, c] + got[i, c], code.at[n], unit.at[n])
        second.append(side(8 + n, code.at[n], far_code.at[n], partner))
        units.append(side(18 + n, unit.at[n], far_unit.at[n], partner))
        units[n].start()
        second[n].start()
    build_columns(half, table)
    third = []
    for i in (0, 1):
        mine = 2 * core + i
        lanes = pl.ds(pl.multiple_of(mine * LANES, LANES), LANES)
        for c in (0, 1):
            n = 2 * i + c
            units[n].wait_recv()
            second[n].wait_recv()
            total = decode(code.at[n], unit.at[n]) + decode(far_code.at[n], far_unit.at[n])
            new[mine, c] = spec[c, :, lanes] - STEP * total
            third.append(side(12 + n, new.at[mine, c], new.at[mine, c], mate))
            third[n].start()
        for c in (0, 1):
            third[2 * i + c].wait_recv()
        for k in (i, i + 2):
            fresh[:, :, k * LANES : (k + 1) * LANES] = new[k]
        object_rows(i, new, rows_table, lhs)
        if i == 0:
            for k in range(BLOCKS):
                image[k] = object_block(i, k, lhs, table)
    image[3] += object_block(1, 3, lhs, table)
    for c in (0, 1):
        value = image[3, :, c * LANES : (c + 1) * LANES]
        edge_out[0, c] = pack_edge(value, 96)
        edge_out[1, c] = pack_edge(value, 112)
    edges = [
        side(16, edge_out.at[0], edge_in.at[0], right),
        side(17, edge_out.at[1], edge_in.at[1], left),
    ]
    for copy in edges:
        copy.start()
    for k in range(BLOCKS - 1):
        image[k] += object_block(1, k, lhs, table)
    for c in (0, 1):
        for k in (1, 2):
            stitched[c, k * LANES : (k + 1) * LANES, :] = image[
                k, :, c * LANES : (c + 1) * LANES
            ].T
    place = edge.astype(F32) - float(3 * LANES)
    at_head = (place < MARGIN) & (tile > 0)
    at_tail = (place >= 80) & (place < 96) & (tile < tiles - 1)
    for copy in edges:
        copy.wait_recv()
    for c in (0, 1):
        mine = image[0, :, c * LANES : (c + 1) * LANES]
        other = unpack_edge(edge_in[0, c], 0)
        blend = mine * ((place + 16.5) / OV) + other * ((15.5 - place) / OV)
        stitched[c, :LANES, :] = jnp.where(at_head, blend, mine).T
        mine = image[3, :, c * LANES : (c + 1) * LANES]
        other = unpack_edge(edge_in[1, c], 80)
        blend = mine * ((111.5 - place) / OV) + other * ((place - 79.5) / OV)
        stitched[c, 3 * LANES :, :] = jnp.where(at_tail, blend, mine).T[: CORE - 3 * LANES]
    for copy in flats + copies + first + second + units + third + edges:
        copy.wait_send()

    for h in (0, 1):

        @pl.loop(1, tiles)
        def _(i):
            block(h, tile, lax.rem(tile + i, tiles)).wait_send()


def update(raw, scales, flat, spectrum, pupil, patterns, led_row, led_col):
    tiles = lax.axis_size("tile")
    frames, rows, width = raw.shape
    deep = frames * rows
    tables = [jnp.asarray(t) for t in band_tables() + object_tables()]
    picks = [patterns, led_row, led_col]
    hbm = pl.BlockSpec(memory_space=pltpu.MemorySpace.HBM)
    arrays = [
        pltpu.with_memory_space_constraint(a, pltpu.MemorySpace.HBM)
        for a in picks + [raw, scales, flat, spectrum, pupil] + tables
    ]
    small = (TH // 8, LANES)
    part = (2, TH, LANES)
    scratch = [pltpu.SMEM(a.shape, a.dtype) for a in picks]
    scratch += [pltpu.VMEM(a.shape, a.dtype) for a in arrays[3:]]
    scratch += [
        pltpu.VMEM((2, 2 * PC, 2 * TW), BF16),
        pltpu.VMEM((2, 2 * TH, 2 * LANES), BF16),
        pltpu.VMEM((2, 2, PR, LANES), F32),
        pltpu.VMEM((2, TH, 2 * LEDS * LANES), BF16),
        pltpu.VMEM((deep, width + 2 * LANES), F32),
        pltpu.VMEM((2, tiles, deep // 2, TW), BF16),
        pltpu.VMEM((2, tiles, deep // 2, TW), BF16),
        pltpu.VMEM((frames, TH, TW), F32),
        pltpu.VMEM((TH, TW), F32),
        pltpu.VMEM((2,) + small, F32),
        pltpu.VMEM((2,) + small, F32),
        pltpu.VMEM((2, 8, LANES), F32),
        pltpu.VMEM((2, 2, 8, LANES), F32),
        pltpu.VMEM((2, frames, rows, TW), F32),
        pltpu.VMEM((frames, 8, TW), F32),
        pltpu.VMEM((2, TH, 2 * TW), BF16),
        pltpu.VMEM((2, PR, PC), F32),
        pltpu.VMEM((2, frames * LEDS * PR, 2 * TW), BF16),
        pltpu.VMEM((LEDS * PR, 2 * PC), F32),
        pltpu.VMEM((LEDS * PR, 2 * TW), F32),
        pltpu.VMEM((frames, LEDS, 2, TH, TW), F32),
        pltpu.VMEM((frames, TH, TW), F32),
        pltpu.VMEM((BLOCKS,) + part, F32),
        pltpu.VMEM((2,) + part, F32),
        pltpu.VMEM((4, TH, LANES), jnp.int16),
        pltpu.VMEM((4, TH // CODE_ROWS, LANES), F32),
        pltpu.VMEM((4, TH, LANES), jnp.int16),
        pltpu.VMEM((4, TH // CODE_ROWS, LANES), F32),
        pltpu.VMEM((BLOCKS,) + part, F32),
        pltpu.VMEM((2, 2, BLOCKS, TW, 2 * LANES), BF16),
        pltpu.VMEM((2, TH, TW), BF16),
        pltpu.VMEM((BLOCKS, TH, 2 * LANES), F32),
        pltpu.VMEM((2, 2) + small, F32),
        pltpu.VMEM((2, 2) + small, F32),
        pltpu.SemaphoreType.DMA((12,)),
        pltpu.SemaphoreType.DMA((2, tiles)),
        pltpu.SemaphoreType.DMA((2, tiles)),
        pltpu.SemaphoreType.DMA((24,)),
        pltpu.SemaphoreType.DMA((24,)),
    ]
    return pl.pallas_call(
        functools.partial(update_kernel, tiles),
        in_specs=[hbm] * len(arrays),
        out_specs=[pl.BlockSpec(memory_space=pltpu.VMEM)] * 2,
        out_shape=[
            jax.ShapeDtypeStruct((2, TH, TW), F32),
            jax.ShapeDtypeStruct((2, CORE, TH), F32),
        ],
        scratch_shapes=scratch,
        compiler_params=pltpu.CompilerParams(
            collective_id=1, has_side_effects=True, vmem_limit_bytes=50 * 2**20
        ),
        name="update",
    )(*arrays)


def hand_over(first, second, first_out, second_out, sem):
    copies = [
        pltpu.make_async_copy(src.at[c], dst.at[c], sem.at[2 * n + c])
        for n, (src, dst) in enumerate(((first, first_out), (second, second_out)))
        for c in (0, 1)
    ]
    for copy in copies:
        copy.start()
    for copy in copies:
        copy.wait()


def deliver(fresh, stitched):
    hbm = pl.BlockSpec(memory_space=pltpu.MemorySpace.HBM)
    return pl.pallas_call(
        hand_over,
        in_specs=[pl.BlockSpec(memory_space=pltpu.VMEM)] * 2,
        out_specs=[hbm] * 2,
        out_shape=[jax.ShapeDtypeStruct(a.shape, a.dtype) for a in (fresh, stitched)],
        scratch_shapes=[pltpu.SemaphoreType.DMA((4,))],
        compiler_params=pltpu.CompilerParams(vmem_limit_bytes=4 * 2**20),
        name="deliver",
    )(fresh, stitched)


def body(raw, scales, flat, spectrum, pupil, patterns, led_row, led_col):
    fresh, stitched = update(
        raw, scales, flat.T, spectrum[0], pupil, patterns.T, led_row, led_col
    )
    fresh, stitched = deliver(fresh, stitched)
    return (fresh[None], jnp.swapaxes(stitched, 1, 2))


def solution(mesh):
    return jax.shard_map(
        body,
        mesh=mesh,
        in_specs=(
            P("grp", "tile", None),
            P("grp", "tile", None),
            P(None, "tile"),
            P("tile", None, None, None),
            P(),
            P(),
            P(),
            P(),
        ),
        out_specs=(P("tile", None, None, None), P(None, None, "tile")),
        check_vma=False,
    )
```

```python
import functools
import math

import jax
import jax.numpy as jnp
import ml_dtypes
import numpy as np
from jax import lax
from jax.experimental import pallas as pl
from jax.experimental.pallas import tpu as pltpu
from jax.sharding import PartitionSpec as P

TH = 256
TW = 512
OV = 32
BR = 4
BC = 32
PR = 64
PC = 128
FR_G = 4
LEDS = 4
HALF = TH // 2
HR = PR // 2
MARGIN = OV // 2
CORE = TW - OV
LANES = 128
BLOCKS = TW // LANES
MESH = pl.DeviceIdType.MESH
CODE_ROWS = 32
CODE_TOP = 32767.0
STEP = 0.02
F32 = jnp.float32
BF16 = jnp.bfloat16


def split_np(table):
    hi = table.astype(ml_dtypes.bfloat16)
    lo = (table - hi.astype(np.float64)).astype(ml_dtypes.bfloat16)
    return hi, lo


def wave_np(length, band):
    places = np.arange(length)[:, None]
    freqs = np.arange(band)[None, :] - band // 2
    angle = (places * freqs % length) * (2.0 * np.pi / length)
    return np.cos(angle) / math.sqrt(band), np.sin(angle) / math.sqrt(band)


def object_tables():
    re, im = wave_np(TH, TH)
    rows = []
    for parity in (0, 1):
        a, b = re[:HALF, parity::2], im[:HALF, parity::2]
        rows.append(np.stack(split_np(np.block([[a, -b], [b, a]]))))
    re, im = (np.roll(part.T, -MARGIN, axis=1)[:TH] for part in wave_np(TW, TW))
    cols = np.stack([np.stack(split_np(re)), np.stack(split_np(im))], axis=1)
    return np.stack(rows), cols


def band_tables():
    row_re, row_im = wave_np(TH, PR)
    spread = []
    for parity in (0, 1):
        re = row_re[:HALF, parity::2]
        im = row_im[:HALF, parity::2]
        rows_hi, rows_lo = split_np(np.block([[re, -im], [im, re]]))
        spread.append(np.concatenate([rows_hi, rows_hi, rows_lo, rows_lo], axis=1))
    order = np.concatenate([np.arange(0, PR, 2), np.arange(1, PR, 2)])
    gather = np.concatenate(split_np(np.concatenate([row_re.T[order], row_im.T[order]])))
    return np.stack(spread), gather


def split(x):
    hi = x.astype(BF16)
    return hi, (x - hi.astype(F32)).astype(BF16)


def dot(a, b):
    return jnp.dot(a, b, preferred_element_type=F32)


def box_corner(pat, lrow, lcol, frame, j):
    led = pat[j, frame]
    return lrow[led], lcol[led]


def row_order(index):
    return jnp.where(index < HR, 2 * index, 2 * index - (PR - 1))


def ones_where(condition):
    return jnp.where(condition, 1.0, 0.0).astype(BF16)


def column_select(col):
    x = lax.broadcasted_iota(jnp.int32, (TW, PC), 0)
    v = lax.broadcasted_iota(jnp.int32, (TW, PC), 1)
    return ones_where(x - v == col)


def column_place(col):
    v = lax.broadcasted_iota(jnp.int32, (PC, TW), 0)
    v = jnp.where(v < PC // 2, 2 * v, 2 * v - (PC - 1))
    x = lax.broadcasted_iota(jnp.int32, (PC, TW), 1)
    return ones_where(x - v == col)


def load_halves(spec, pup, halves, pd):
    for c in (0, 1):
        hi, lo = split(spec[c])
        halves[0, :, c * TW : (c + 1) * TW] = hi
        halves[1, :, c * TW : (c + 1) * TW] = lo
        for parity in (0, 1):
            pd[c, parity * HR : (parity + 1) * HR] = pup[c, pl.ds(parity, HR, stride=2), :]


def forward_frame(f, frame, pat, lrow, lcol, halves, pd, cols, spread, picked, lit, mid, field):
    y = lax.broadcasted_iota(jnp.int32, (PR, TH), 1)
    order = row_order(lax.broadcasted_iota(jnp.int32, (PR, TH), 0))
    corners = [box_corner(pat, lrow, lcol, frame, j) for j in range(LEDS)]
    choose = jnp.concatenate([ones_where(y - order == row) for row, _ in corners], axis=0)
    for h in (0, 1):
        picked[h, : LEDS * PR] = dot(choose, halves[h]).astype(BF16)
    p_re, p_im = pd[0], pd[1]
    for j in range(LEDS):
        rows = pl.ds(j * PR, PR)
        stack = jnp.concatenate(
            [picked[h, rows, c * TW : (c + 1) * TW] for h in (0, 1) for c in (0, 1)], axis=0
        )
        cut = dot(stack, column_select(corners[j][1]))
        b_re = cut[:PR] + cut[2 * PR : 3 * PR]
        b_im = cut[PR : 2 * PR] + cut[3 * PR :]
        lit[rows, :PC] = p_re * b_re - p_im * b_im
        lit[rows, PC:] = p_re * b_im + p_im * b_re
    hi, lo = split(lit[...])
    mid[...] = dot(hi, cols[0]) + dot(lo, cols[0]) + dot(hi, cols[1])
    estimate = None
    for j in range(LEDS):
        parts = []
        for parity in (0, 1):
            rows = pl.ds(j * PR + parity * HR, HR)
            re_hi, re_lo = split(mid[rows, :TW])
            im_hi, im_lo = split(mid[rows, TW:])
            both = jnp.concatenate([re_hi, im_hi, re_lo, im_lo], axis=0)
            parts.append(dot(spread[parity], jnp.concatenate([both, both], axis=0)))
        upper = parts[0] + parts[1]
        lower = parts[0] - parts[1]
        field[f, j, 0, :HALF] = upper[:HALF]
        field[f, j, 0, HALF:] = lower[:HALF]
        field[f, j, 1, :HALF] = upper[HALF:]
        field[f, j, 1, HALF:] = lower[HALF:]
        power = jnp.concatenate(
            [
                upper[:HALF] * upper[:HALF] + upper[HALF:] * upper[HALF:],
                lower[:HALF] * lower[:HALF] + lower[HALF:] * lower[HALF:],
            ],
            axis=0,
        )
        estimate = power if estimate is None else estimate + power
    return estimate


def backward_frame(f, frame, misfit, pat, lrow, lcol, pairs, fold, gather, field, bands, wide):
    for j in range(LEDS):
        weighted = [misfit * field[f, j, c] for c in (0, 1)]
        for parity in (0, 1):
            mix = [
                w[:, :TH] + w[:, TH:] if parity == 0 else w[:, :TH] - w[:, TH:]
                for w in weighted
            ]
            hi, lo = split(jnp.concatenate(mix, axis=1))
            first = dot(hi, fold[parity])
            total = first[:, :LANES] + first[:, LANES:] + dot(lo, fold[parity, :, :LANES])
            hi, lo = split(total)
            cut = slice((2 * j + parity) * LANES, (2 * j + parity + 1) * LANES)
            bands[0, :, cut] = hi
            bands[1, :, cut] = lo
    first = dot(gather[...], bands[0])
    second = dot(gather[: 2 * PR], bands[1])
    by_re = first[:PR] + first[2 * PR : 3 * PR] + second[:PR]
    by_im = first[PR : 2 * PR] + first[3 * PR :] + second[PR:]
    left = lax.broadcasted_iota(jnp.int32, (1, LANES), 1) < LANES // 2
    sign = jnp.where(left, 1.0, -1.0)
    turn = LANES // 2
    for j in range(LEDS):
        col = box_corner(pat, lrow, lcol, frame, j)[1]
        halves = []
        for parity in (0, 1):
            cut = slice((2 * j + parity) * LANES, (2 * j + parity + 1) * LANES)
            band = by_re[:, cut] + sign * pltpu.roll(by_im[:, cut], turn, 1)
            halves.append(
                pairs[0, parity] * band + sign * pairs[1, parity] * pltpu.roll(band, turn, 1)
            )
        even, odd = halves
        re_hi, re_lo = split(jnp.where(left, even, pltpu.roll(odd, turn, 1)))
        im_hi, im_lo = split(jnp.where(left, pltpu.roll(even, turn, 1), odd))
        stack = jnp.concatenate([re_hi, im_hi, re_lo, im_lo], axis=0)
        placed = dot(stack, column_place(col)).astype(BF16)
        rows = pl.ds(pl.multiple_of((f * LEDS + j) * PR, PR), PR)
        for h in (0, 1):
            for c in (0, 1):
                n = 2 * h + c
                wide[h, rows, c * TW : (c + 1) * TW] = placed[n * PR : (n + 1) * PR]


def row_places(first_frame, frames, pat, lrow, lcol):
    total_rows = frames * LEDS * PR
    lane = lax.broadcasted_iota(jnp.int32, (1, total_rows), 1)
    box = lane // PR
    target = row_order(lane & (PR - 1))
    for f in range(frames):
        for j in range(LEDS):
            row = box_corner(pat, lrow, lcol, first_frame + f, j)[0]
            target = target + jnp.where(box == f * LEDS + j, row, 0)
    return ones_where(lax.broadcasted_iota(jnp.int32, (TH, total_rows), 0) == target)


def place_pair(which, choose, wide, grad):
    for c in (0, 1):
        cut = pl.ds(pl.multiple_of(c * TW + which * (2 * LANES), LANES), 2 * LANES)
        both = dot(choose, wide[0, :, cut]) + dot(choose, wide[1, :, cut])
        for n in (0, 1):
            grad[2 * which + n, c] = both[:, n * LANES : (n + 1) * LANES]


def pack_edge(value, first):
    lane = lax.broadcasted_iota(jnp.int32, (TH // 8, LANES), 1) // MARGIN
    packed = jnp.zeros((TH // 8, LANES), F32)
    for b in range(8):
        piece = value[b * 32 : (b + 1) * 32]
        piece = pltpu.roll(piece, (MARGIN * b - first) % LANES, 1)
        packed = jnp.where(lane == b, piece, packed)
    return packed


def unpack_edge(packed, first):
    return jnp.concatenate(
        [pltpu.roll(packed, (first - MARGIN * b) % LANES, 1) for b in range(8)], axis=0
    )


def dequantize(raw, scales, dequant):
    frames, rows, width = raw.shape
    dequant[:, :LANES] = jnp.zeros((frames * rows, LANES), F32)
    dequant[:, LANES + width :] = jnp.zeros((frames * rows, LANES), F32)
    lane = lax.broadcasted_iota(jnp.int32, (rows, LANES), 1) // BC
    upper = lax.broadcasted_iota(jnp.int32, (rows, LANES), 0) < BR
    blocks = scales.shape[2]
    per = LANES // BC
    for first in range(0, blocks, LANES):
        count = min(LANES, blocks - first)
        for f in range(frames):
            pair = scales[f, :, first : first + count].astype(F32)
            if count < LANES:
                pair = jnp.concatenate([pair, jnp.zeros((2, LANES - count), F32)], axis=1)
            factors = jnp.where(
                upper,
                jnp.broadcast_to(pair[0:1], (rows, LANES)),
                jnp.broadcast_to(pair[1:2], (rows, LANES)),
            )
            for k in range(count // per):
                column = (first // per + k) * LANES
                spread = jnp.take_along_axis(factors, lane + per * k, axis=1)
                codes = raw[f, :, column : column + LANES].astype(F32)
                dequant[f * rows : (f + 1) * rows, LANES + column : 2 * LANES + column] = (
                    codes * spread
                )


def cut_message(dequant, tile):
    start = CORE * tile - MARGIN + LANES
    aligned = pl.multiple_of(start // LANES * LANES, LANES)
    offset = start - aligned + MARGIN
    wide = dequant[:, pl.ds(aligned, TW + LANES)]
    wide = pltpu.roll(wide, TW + LANES - offset, 1)
    lane = lax.broadcasted_iota(jnp.int32, (1, LANES), 1)
    last = jnp.where(lane < LANES - MARGIN, wide[:, TW - LANES : TW], wide[:, TW:])
    return jnp.concatenate([wide[:, : TW - LANES], last], axis=1).astype(BF16)


def centred():
    y = lax.broadcasted_iota(jnp.int32, (TH, 1), 0).astype(F32) - (TH - 1) / 2.0
    lane = lax.broadcasted_iota(jnp.int32, (1, TW), 1)
    x = lane.astype(F32) - (CORE - 1) / 2.0
    return y, x, lane


Y_NORM = float(np.sum((np.arange(TH) - (TH - 1) / 2.0) ** 2) * CORE)
X_NORM = float(np.sum((np.arange(CORE) - (CORE - 1) / 2.0) ** 2) * TH)


def parity_pick(parity):
    v = lax.broadcasted_iota(jnp.int32, (PC, LANES), 0)
    lane = lax.broadcasted_iota(jnp.int32, (PC, LANES), 1)
    return ones_where(v == 2 * (lane & (PC // 2 - 1)) + parity)


def build_band(half, pd, cols, fold, pairs):
    lane = lax.broadcasted_iota(jnp.int32, (1, TW), 1)
    sign = (2 - 4 * (lane & 1)).astype(F32)
    left = lane[:, :LANES] < LANES // 2
    for h in (0, 1):
        re, im = (
            jnp.concatenate(
                [
                    half[h, c, TH - PC // 2 :, :].astype(F32) * 2.0,
                    half[h, c, : PC // 2, :].astype(F32) * sign,
                ],
                axis=0,
            )
            for c in (0, 1)
        )
        cols[h, :PC, :TW] = re.astype(BF16)
        cols[h, :PC, TW:] = im.astype(BF16)
        cols[h, PC:, :TW] = (-im).astype(BF16)
        cols[h, PC:, TW:] = re.astype(BF16)
        turned = [part[:, :TH].T.astype(BF16) for part in (re, im)]
        for parity in (0, 1):
            a, b = (dot(part, parity_pick(parity)) for part in turned)
            cut = slice(h * LANES, (h + 1) * LANES)
            fold[parity, :TH, cut] = jnp.where(left, a, -b).astype(BF16)
            fold[parity, TH:, cut] = jnp.where(left, b, a).astype(BF16)
    for c in (0, 1):
        hi = pd[c].astype(BF16)
        lo, last = split(pd[c] - hi.astype(F32))
        for parity in (0, 1):
            pick = parity_pick(parity)
            pairs[c, parity] = dot(hi, pick) + dot(lo, pick) + dot(last, pick)


def build_columns(half, table):
    lane = lax.broadcasted_iota(jnp.int32, (1, TW), 1)
    sign = (1 - 2 * (lane & 1)).astype(F32)
    for i in (0, 1):
        rows = pl.ds(i * LANES, LANES)
        for h in (0, 1):
            re = half[h, 0, rows, :].astype(F32)
            im = half[h, 1, rows, :].astype(F32)
            for n, factor in ((0, None), (1, sign)):
                a = re if factor is None else re * factor
                b = im if factor is None else im * factor
                upper = pl.ds(n * LANES, LANES)
                lower = pl.ds((2 + n) * LANES, LANES)
                for k in range(BLOCKS):
                    cut = slice(k * LANES, (k + 1) * LANES)
                    table[i, h, k, upper, :LANES] = a[:, cut].astype(BF16)
                    table[i, h, k, upper, LANES:] = b[:, cut].astype(BF16)
                    table[i, h, k, lower, :LANES] = (-b[:, cut]).astype(BF16)
                    table[i, h, k, lower, LANES:] = a[:, cut].astype(BF16)


def object_rows(i, new, rows_table, lhs):
    parts = []
    for parity in (0, 1):
        data = [
            jnp.concatenate(
                [new[k, c, pl.ds(parity, HALF, stride=2), :] for k in (i, i + 2)], axis=1
            )
            for c in (0, 1)
        ]
        hi, lo = split(jnp.concatenate(data, axis=0))
        t_hi, t_lo = rows_table[parity, 0], rows_table[parity, 1]
        parts.append(dot(t_hi, hi) + dot(t_hi, lo) + dot(t_lo, hi))
    for n, value in enumerate((parts[0] + parts[1], parts[0] - parts[1])):
        hi, lo = split(value)
        rows = pl.ds(n * HALF, HALF)
        for h, part in enumerate((hi, lo)):
            lhs[h, rows, : 2 * LANES] = part[:HALF]
            lhs[h, rows, 2 * LANES :] = part[HALF:]


def object_block(i, k, lhs, table):
    hi, lo = lhs[0], lhs[1]
    return dot(hi, table[i, 0, k]) + dot(lo, table[i, 0, k]) + dot(hi, table[i, 1, k])


def encode(value, code, unit):
    for g in range(TH // CODE_ROWS):
        rows = slice(g * CODE_ROWS, (g + 1) * CODE_ROWS)
        piece = value[rows]
        top = jnp.max(jnp.abs(piece), axis=0, keepdims=True)
        unit[g : g + 1] = top * (1.0 / CODE_TOP)
        ratio = jnp.where(top > 0.0, CODE_TOP / top, 0.0)
        whole = jnp.clip(jnp.round(piece * ratio), -CODE_TOP, CODE_TOP)
        code[rows] = whole.astype(jnp.int32).astype(jnp.int16)


def decode(code, unit):
    return jnp.concatenate(
        [
            code[g * CODE_ROWS : (g + 1) * CODE_ROWS].astype(jnp.int32).astype(F32)
            * unit[g : g + 1]
            for g in range(TH // CODE_ROWS)
        ],
        axis=0,
    )


def update_kernel(
    tiles,
    pat_h,
    lrow_h,
    lcol_h,
    raw_h,
    scales_h,
    flat_h,
    spec_h,
    pup_h,
    spread_h,
    gather_h,
    rows_h,
    half_h,
    fresh,
    stitched,
    pat,
    lrow,
    lcol,
    raw,
    scales,
    flat,
    spec,
    pup,
    spread,
    gather,
    rows_table,
    half,
    cols,
    fold,
    pairs,
    bands,
    dequant,
    message,
    arrived,
    window,
    gains,
    flat_out,
    flat_in,
    slope_out,
    slope_in,
    sums,
    coef,
    halves,
    pd,
    wide,
    lit,
    mid,
    field,
    estimate,
    grad,
    got,
    code,
    unit,
    far_code,
    far_unit,
    new,
    table,
    lhs,
    image,
    edge_out,
    edge_in,
    load,
    send,
    recv,
    side_send,
    side_recv,
):
    frames = raw.shape[0]
    rows = raw.shape[1]
    group = lax.axis_index("grp")
    tile = lax.axis_index("tile")
    core = lax.rem(group, 2)
    mate = {"grp": group + 1 - 2 * core}
    partner = {"grp": group + 2 - 4 * lax.div(group, 2)}
    right = {"tile": lax.rem(tile + 1, tiles)}
    left = {"tile": lax.rem(tile + tiles - 1, tiles)}

    def side(number, src, dst, device):
        return pltpu.make_async_remote_copy(
            src_ref=src,
            dst_ref=dst,
            send_sem=side_send.at[number],
            recv_sem=side_recv.at[number],
            device_id=device,
            device_id_type=MESH,
        )

    def block(source, target):
        return pltpu.make_async_remote_copy(
            src_ref=message.at[target],
            dst_ref=arrived.at[source],
            send_sem=send.at[target],
            recv_sem=recv.at[source],
            device_id={"tile": target},
            device_id_type=MESH,
        )

    loads = [
        pltpu.make_async_copy(src, dst, load.at[n])
        for n, (src, dst) in enumerate(
            (
                (raw_h, raw),
                (scales_h, scales),
                (pat_h, pat),
                (lrow_h, lrow),
                (lcol_h, lcol),
                (flat_h, flat),
                (spec_h, spec),
                (pup_h, pup),
                (half_h, half),
                (spread_h, spread),
                (gather_h, gather),
                (rows_h, rows_table),
            )
        )
    ]
    for copy in loads:
        copy.start()
    barrier = pltpu.get_barrier_semaphore()

    @pl.loop(1, tiles)
    def _(i):
        pl.semaphore_signal(
            barrier, inc=1, device_id={"tile": lax.rem(tile + i, tiles)}, device_id_type=MESH
        )

    for device in (mate, partner):
        pl.semaphore_signal(barrier, inc=1, device_id=device, device_id_type=MESH)

    loads[0].wait()
    loads[1].wait()
    dequantize(raw, scales, dequant)
    pl.semaphore_wait(barrier, tiles + 1)

    @pl.loop(1, tiles)
    def _(i):
        target = lax.rem(tile + 11 * i, tiles)
        message[target] = cut_message(dequant, target)
        block(tile, target).start()

    arrived[tile] = cut_message(dequant, tile)
    loads[5].wait()
    for k in range(BLOCKS - 1):
        gains[:, k * LANES : (k + 1) * LANES] = flat[k * LANES : (k + 1) * LANES, :].T
    tail = jnp.concatenate(
        [flat[3 * LANES :, :], jnp.zeros((TW - CORE, TH), F32)], axis=0
    ).T
    gains[:, 3 * LANES :] = tail
    flat_out[0] = pack_edge(tail, 80)
    flat_out[1] = pack_edge(gains[:, :LANES], 0)
    flats = [
        side(0, flat_out.at[0], flat_in.at[0], right),
        side(1, flat_out.at[1], flat_in.at[1], left),
    ]
    for copy in flats:
        copy.start()

    for copy in loads[2:5] + loads[6:]:
        copy.wait()
    load_halves(spec, pup, halves, pd)
    build_band(half, pd, cols, fold, pairs)
    first_frame = group * frames

    def forward(f):
        estimate[f] = forward_frame(
            f, first_frame + f, pat, lrow, lcol, halves, pd, cols, spread, wide, lit, mid, field
        )

    pl.loop(0, frames - 1)(forward)

    y, x, lane = centred()
    edge = lane[:, 3 * LANES :]
    for copy in flats:
        copy.wait_recv()
    outer = jnp.where(
        edge < CORE + MARGIN, unpack_edge(flat_in[1], 96), unpack_edge(flat_in[0], 112)
    )
    own = edge < CORE
    after = edge < CORE + MARGIN
    blank = ((~own) & after & (tile == tiles - 1)) | ((~after) & (tile == 0))
    gains[:, 3 * LANES :] = jnp.where(
        blank, 0.0, jnp.where(own, gains[:, 3 * LANES :], outer)
    )
    sums[...] = jnp.zeros_like(sums)

    @pl.loop(1, tiles + 1)
    def _(i):
        source = lax.rem(tile + 11 * (tiles - i), tiles)

        @pl.when(i < tiles)
        def _():
            block(source, tile).wait_recv()

        here = pl.ds(pl.multiple_of(source * rows, rows), rows)
        values = arrived[source].astype(F32)
        for f in range(frames):
            flattened = values[f * rows : (f + 1) * rows] * gains[here, :]
            window[f, here, :] = flattened
            sums[0, f] += flattened
            sums[1, f] += flattened * (y[:rows] + (source * rows).astype(F32))

    inside = (lane < CORE).astype(F32)
    slopes = []
    for f in range(frames):
        columns = jnp.sum(sums[0, f], axis=0, keepdims=True)
        tilted = jnp.sum(sums[1, f], axis=0, keepdims=True)
        slope_y = jnp.sum(tilted * inside, axis=1, keepdims=True) / Y_NORM
        slope_x = jnp.sum(columns * (x * inside), axis=1, keepdims=True) / X_NORM
        slopes.append((slope_y, slope_x))
        slope_out[f : f + 1] = jnp.broadcast_to(slope_y, (1, LANES))
        slope_out[frames + f : frames + f + 1] = jnp.broadcast_to(slope_x, (1, LANES))
    copies = [side(2, slope_out, slope_in.at[0], right), side(3, slope_out, slope_in.at[1], left)]
    for copy in copies:
        copy.start()
    forward(frames - 1)
    for copy in copies:
        copy.wait_recv()
    x_edge = x[:, 3 * LANES :]
    for f in range(frames):
        slope_y, slope_x = slopes[f]
        coef[f, 0:1, : 3 * LANES] = jnp.broadcast_to(slope_y, (1, 3 * LANES))
        coef[f, 1:2, : 3 * LANES] = slope_x * x[:, : 3 * LANES]
        row_y = jnp.where(
            own, slope_y, jnp.where(after, slope_in[1, f : f + 1], slope_in[0, f : f + 1])
        )
        row_x = jnp.where(
            own,
            slope_x * x_edge,
            jnp.where(
                after,
                slope_in[1, frames + f : frames + f + 1] * (x_edge - CORE),
                slope_in[0, frames + f : frames + f + 1] * (x_edge - 32.0),
            ),
        )
        coef[f, 0:1, 3 * LANES :] = jnp.where(blank, 0.0, row_y)
        coef[f, 1:2, 3 * LANES :] = jnp.where(blank, 0.0, row_x)

    @pl.loop(0, frames)
    def _(f):
        misfit = estimate[f] - window[f] + coef[f, 0:1] * y + coef[f, 1:2]
        backward_frame(
            f, first_frame + f, misfit, pat, lrow, lcol, pairs, fold, gather, field, bands, wide
        )

    choose = row_places(first_frame, frames, pat, lrow, lcol)
    place_pair(1 - core, choose, wide, grad)

    pieces = [(i, c) for i in (0, 1) for c in (0, 1)]
    first = [
        side(4 + n, grad.at[2 - 2 * core + i, c], got.at[i, c], mate)
        for n, (i, c) in enumerate(pieces)
    ]
    for copy in first:
        copy.start()
    place_pair(core, choose, wide, grad)
    second = []
    units = []
    for n, (i, c) in enumerate(pieces):
        first[n].wait_recv()
        encode(grad[2 * core + i, c] + got[i, c], code.at[n], unit.at[n])
        second.append(side(8 + n, code.at[n], far_code.at[n], partner))
        units.append(side(18 + n, unit.at[n], far_unit.at[n], partner))
        units[n].start()
        second[n].start()
    build_columns(half, table)
    third = []
    for i in (0, 1):
        mine = 2 * core + i
        lanes = pl.ds(pl.multiple_of(mine * LANES, LANES), LANES)
        for c in (0, 1):
            n = 2 * i + c
            units[n].wait_recv()
            second[n].wait_recv()
            total = decode(code.at[n], unit.at[n]) + decode(far_code.at[n], far_unit.at[n])
            new[mine, c] = spec[c, :, lanes] - STEP * total
            third.append(side(12 + n, new.at[mine, c], new.at[mine, c], mate))
            third[n].start()
        for c in (0, 1):
            third[2 * i + c].wait_recv()
        for k in (i, i + 2):
            fresh[:, :, k * LANES : (k + 1) * LANES] = new[k]
        object_rows(i, new, rows_table, lhs)
        if i == 0:
            for k in range(BLOCKS):
                image[k] = object_block(i, k, lhs, table)
    image[3] += object_block(1, 3, lhs, table)
    for c in (0, 1):
        value = image[3, :, c * LANES : (c + 1) * LANES]
        edge_out[0, c] = pack_edge(value, 96)
        edge_out[1, c] = pack_edge(value, 112)
    edges = [
        side(16, edge_out.at[0], edge_in.at[0], right),
        side(17, edge_out.at[1], edge_in.at[1], left),
    ]
    for copy in edges:
        copy.start()
    for k in range(BLOCKS - 1):
        image[k] += object_block(1, k, lhs, table)
    for c in (0, 1):
        for k in (1, 2):
            stitched[c, k * LANES : (k + 1) * LANES, :] = image[
                k, :, c * LANES : (c + 1) * LANES
            ].T
    place = edge.astype(F32) - float(3 * LANES)
    at_head = (place < MARGIN) & (tile > 0)
    at_tail = (place >= 80) & (place < 96) & (tile < tiles - 1)
    for copy in edges:
        copy.wait_recv()
    for c in (0, 1):
        mine = image[0, :, c * LANES : (c + 1) * LANES]
        other = unpack_edge(edge_in[0, c], 0)
        blend = mine * ((place + 16.5) / OV) + other * ((15.5 - place) / OV)
        stitched[c, :LANES, :] = jnp.where(at_head, blend, mine).T
        mine = image[3, :, c * LANES : (c + 1) * LANES]
        other = unpack_edge(edge_in[1, c], 80)
        blend = mine * ((111.5 - place) / OV) + other * ((place - 79.5) / OV)
        stitched[c, 3 * LANES :, :] = jnp.where(at_tail, blend, mine).T[: CORE - 3 * LANES]
    for copy in flats + copies + first + second + units + third + edges:
        copy.wait_send()

    @pl.loop(1, tiles)
    def _(i):
        block(tile, lax.rem(tile + i, tiles)).wait_send()


def update(raw, scales, flat, spectrum, pupil, patterns, led_row, led_col):
    tiles = lax.axis_size("tile")
    frames, rows, width = raw.shape
    deep = frames * rows
    tables = [jnp.asarray(t) for t in band_tables() + object_tables()]
    picks = [patterns, led_row, led_col]
    hbm = pl.BlockSpec(memory_space=pltpu.MemorySpace.HBM)
    arrays = [
        pltpu.with_memory_space_constraint(a, pltpu.MemorySpace.HBM)
        for a in picks + [raw, scales, flat, spectrum, pupil] + tables
    ]
    small = (TH // 8, LANES)
    part = (2, TH, LANES)
    scratch = [pltpu.SMEM(a.shape, a.dtype) for a in picks]
    scratch += [pltpu.VMEM(a.shape, a.dtype) for a in arrays[3:]]
    scratch += [
        pltpu.VMEM((2, 2 * PC, 2 * TW), BF16),
        pltpu.VMEM((2, 2 * TH, 2 * LANES), BF16),
        pltpu.VMEM((2, 2, PR, LANES), F32),
        pltpu.VMEM((2, TH, 2 * LEDS * LANES), BF16),
        pltpu.VMEM((deep, width + 2 * LANES), F32),
        pltpu.VMEM((tiles, deep, TW), BF16),
        pltpu.VMEM((tiles, deep, TW), BF16),
        pltpu.VMEM((frames, TH, TW), F32),
        pltpu.VMEM((TH, TW), F32),
        pltpu.VMEM((2,) + small, F32),
        pltpu.VMEM((2,) + small, F32),
        pltpu.VMEM((2 * frames, LANES), F32),
        pltpu.VMEM((2, 2 * frames, LANES), F32),
        pltpu.VMEM((2, frames, rows, TW), F32),
        pltpu.VMEM((frames, 8, TW), F32),
        pltpu.VMEM((2, TH, 2 * TW), BF16),
        pltpu.VMEM((2, PR, PC), F32),
        pltpu.VMEM((2, frames * LEDS * PR, 2 * TW), BF16),
        pltpu.VMEM((LEDS * PR, 2 * PC), F32),
        pltpu.VMEM((LEDS * PR, 2 * TW), F32),
        pltpu.VMEM((frames, LEDS, 2, TH, TW), F32),
        pltpu.VMEM((frames, TH, TW), F32),
        pltpu.VMEM((BLOCKS,) + part, F32),
        pltpu.VMEM((2,) + part, F32),
        pltpu.VMEM((4, TH, LANES), jnp.int16),
        pltpu.VMEM((4, TH // CODE_ROWS, LANES), F32),
        pltpu.VMEM((4, TH, LANES), jnp.int16),
        pltpu.VMEM((4, TH // CODE_ROWS, LANES), F32),
        pltpu.VMEM((BLOCKS,) + part, F32),
        pltpu.VMEM((2, 2, BLOCKS, TW, 2 * LANES), BF16),
        pltpu.VMEM((2, TH, TW), BF16),
        pltpu.VMEM((BLOCKS, TH, 2 * LANES), F32),
        pltpu.VMEM((2, 2) + small, F32),
        pltpu.VMEM((2, 2) + small, F32),
        pltpu.SemaphoreType.DMA((12,)),
        pltpu.SemaphoreType.DMA((tiles,)),
        pltpu.SemaphoreType.DMA((tiles,)),
        pltpu.SemaphoreType.DMA((22,)),
        pltpu.SemaphoreType.DMA((22,)),
    ]
    return pl.pallas_call(
        functools.partial(update_kernel, tiles),
        in_specs=[hbm] * len(arrays),
        out_specs=[pl.BlockSpec(memory_space=pltpu.VMEM)] * 2,
        out_shape=[
            jax.ShapeDtypeStruct((2, TH, TW), F32),
            jax.ShapeDtypeStruct((2, CORE, TH), F32),
        ],
        scratch_shapes=scratch,
        compiler_params=pltpu.CompilerParams(
            collective_id=1, has_side_effects=True, vmem_limit_bytes=50 * 2**20
        ),
        name="update",
    )(*arrays)


def hand_over(first, second, first_out, second_out, sem):
    copies = [
        pltpu.make_async_copy(src.at[c], dst.at[c], sem.at[2 * n + c])
        for n, (src, dst) in enumerate(((first, first_out), (second, second_out)))
        for c in (0, 1)
    ]
    for copy in copies:
        copy.start()
    for copy in copies:
        copy.wait()


def deliver(fresh, stitched):
    hbm = pl.BlockSpec(memory_space=pltpu.MemorySpace.HBM)
    return pl.pallas_call(
        hand_over,
        in_specs=[pl.BlockSpec(memory_space=pltpu.VMEM)] * 2,
        out_specs=[hbm] * 2,
        out_shape=[jax.ShapeDtypeStruct(a.shape, a.dtype) for a in (fresh, stitched)],
        scratch_shapes=[pltpu.SemaphoreType.DMA((4,))],
        compiler_params=pltpu.CompilerParams(vmem_limit_bytes=4 * 2**20),
        name="deliver",
    )(fresh, stitched)


def body(raw, scales, flat, spectrum, pupil, patterns, led_row, led_col):
    fresh, stitched = update(
        raw, scales, flat.T, spectrum[0], pupil, patterns.T, led_row, led_col
    )
    fresh, stitched = deliver(fresh, stitched)
    return (fresh[None], jnp.swapaxes(stitched, 1, 2))


def solution(mesh):
    return jax.shard_map(
        body,
        mesh=mesh,
        in_specs=(
            P("grp", "tile", None),
            P("grp", "tile", None),
            P(None, "tile"),
            P("tile", None, None, None),
            P(),
            P(),
            P(),
            P(),
        ),
        out_specs=(P("tile", None, None, None), P(None, None, "tile")),
        check_vma=False,
    )
```

```python
import functools
import math

import jax
import jax.numpy as jnp
import ml_dtypes
import numpy as np
from jax import lax
from jax.experimental import pallas as pl
from jax.experimental.pallas import tpu as pltpu
from jax.sharding import PartitionSpec as P

TH = 256
TW = 512
OV = 32
BR = 4
BC = 32
PR = 64
PC = 128
FR_G = 4
LEDS = 4
HALF = TH // 2
HR = PR // 2
MARGIN = OV // 2
CORE = TW - OV
LANES = 128
BLOCKS = TW // LANES
MESH = pl.DeviceIdType.MESH
CODE_ROWS = 32
CODE_TOP = 32767.0
STEP = 0.02
F32 = jnp.float32
BF16 = jnp.bfloat16


def split_np(table):
    hi = table.astype(ml_dtypes.bfloat16)
    lo = (table - hi.astype(np.float64)).astype(ml_dtypes.bfloat16)
    return hi, lo


def wave_np(length, band):
    places = np.arange(length)[:, None]
    freqs = np.arange(band)[None, :] - band // 2
    angle = (places * freqs % length) * (2.0 * np.pi / length)
    return np.cos(angle) / math.sqrt(band), np.sin(angle) / math.sqrt(band)


def object_tables():
    re, im = wave_np(TH, TH)
    rows = []
    for parity in (0, 1):
        a, b = re[:HALF, parity::2], im[:HALF, parity::2]
        rows.append(np.stack(split_np(np.block([[a, -b], [b, a]]))))
    re, im = (np.roll(part.T, -MARGIN, axis=1)[:TH] for part in wave_np(TW, TW))
    cols = np.stack([np.stack(split_np(re)), np.stack(split_np(im))], axis=1)
    return np.stack(rows), cols


def band_tables():
    row_re, row_im = wave_np(TH, PR)
    spread = []
    for parity in (0, 1):
        re = row_re[:HALF, parity::2]
        im = row_im[:HALF, parity::2]
        rows_hi, rows_lo = split_np(np.block([[re, -im], [im, re]]))
        spread.append(np.concatenate([rows_hi, rows_hi, rows_lo, rows_lo], axis=1))
    order = np.concatenate([np.arange(0, PR, 2), np.arange(1, PR, 2)])
    gather = np.concatenate(split_np(np.concatenate([row_re.T[order], row_im.T[order]])))
    return np.stack(spread), gather


def split(x):
    hi = x.astype(BF16)
    return hi, (x - hi.astype(F32)).astype(BF16)


def dot(a, b):
    return jnp.dot(a, b, preferred_element_type=F32)


def box_corner(pat, lrow, lcol, frame, j):
    led = pat[j, frame]
    return lrow[led], lcol[led]


def row_order(index):
    return jnp.where(index < HR, 2 * index, 2 * index - (PR - 1))


def ones_where(condition):
    return jnp.where(condition, 1.0, 0.0).astype(BF16)


def column_select(col):
    x = lax.broadcasted_iota(jnp.int32, (TW, PC), 0)
    v = lax.broadcasted_iota(jnp.int32, (TW, PC), 1)
    return ones_where(x - v == col)


def column_place(col):
    v = lax.broadcasted_iota(jnp.int32, (PC, TW), 0)
    v = jnp.where(v < PC // 2, 2 * v, 2 * v - (PC - 1))
    x = lax.broadcasted_iota(jnp.int32, (PC, TW), 1)
    return ones_where(x - v == col)


def load_halves(spec, pup, halves, pd):
    for c in (0, 1):
        hi, lo = split(spec[c])
        halves[0, :, c * TW : (c + 1) * TW] = hi
        halves[1, :, c * TW : (c + 1) * TW] = lo
        for parity in (0, 1):
            pd[c, parity * HR : (parity + 1) * HR] = pup[c, pl.ds(parity, HR, stride=2), :]


def forward_frame(f, frame, pat, lrow, lcol, halves, pd, cols, spread, picked, lit, mid, field):
    y = lax.broadcasted_iota(jnp.int32, (PR, TH), 1)
    order = row_order(lax.broadcasted_iota(jnp.int32, (PR, TH), 0))
    corners = [box_corner(pat, lrow, lcol, frame, j) for j in range(LEDS)]
    choose = jnp.concatenate([ones_where(y - order == row) for row, _ in corners], axis=0)
    for h in (0, 1):
        picked[h, : LEDS * PR] = dot(choose, halves[h]).astype(BF16)
    p_re, p_im = pd[0], pd[1]
    for j in range(LEDS):
        rows = pl.ds(j * PR, PR)
        stack = jnp.concatenate(
            [picked[h, rows, c * TW : (c + 1) * TW] for h in (0, 1) for c in (0, 1)], axis=0
        )
        cut = dot(stack, column_select(corners[j][1]))
        b_re = cut[:PR] + cut[2 * PR : 3 * PR]
        b_im = cut[PR : 2 * PR] + cut[3 * PR :]
        lit[rows, :PC] = p_re * b_re - p_im * b_im
        lit[rows, PC:] = p_re * b_im + p_im * b_re
    hi, lo = split(lit[...])
    mid[...] = dot(hi, cols[0]) + dot(lo, cols[0]) + dot(hi, cols[1])
    estimate = None
    for j in range(LEDS):
        parts = []
        for parity in (0, 1):
            rows = pl.ds(j * PR + parity * HR, HR)
            re_hi, re_lo = split(mid[rows, :TW])
            im_hi, im_lo = split(mid[rows, TW:])
            both = jnp.concatenate([re_hi, im_hi, re_lo, im_lo], axis=0)
            parts.append(dot(spread[parity], jnp.concatenate([both, both], axis=0)))
        upper = parts[0] + parts[1]
        lower = parts[0] - parts[1]
        field[f, j, 0, :HALF] = upper[:HALF]
        field[f, j, 0, HALF:] = lower[:HALF]
        field[f, j, 1, :HALF] = upper[HALF:]
        field[f, j, 1, HALF:] = lower[HALF:]
        power = jnp.concatenate(
            [
                upper[:HALF] * upper[:HALF] + upper[HALF:] * upper[HALF:],
                lower[:HALF] * lower[:HALF] + lower[HALF:] * lower[HALF:],
            ],
            axis=0,
        )
        estimate = power if estimate is None else estimate + power
    return estimate


def backward_frame(f, frame, misfit, pat, lrow, lcol, pairs, fold, gather, field, bands, wide):
    for j in range(LEDS):
        weighted = [misfit * field[f, j, c] for c in (0, 1)]
        for parity in (0, 1):
            mix = [
                w[:, :TH] + w[:, TH:] if parity == 0 else w[:, :TH] - w[:, TH:]
                for w in weighted
            ]
            hi, lo = split(jnp.concatenate(mix, axis=1))
            first = dot(hi, fold[parity])
            total = first[:, :LANES] + first[:, LANES:] + dot(lo, fold[parity, :, :LANES])
            hi, lo = split(total)
            cut = slice((2 * j + parity) * LANES, (2 * j + parity + 1) * LANES)
            bands[0, :, cut] = hi
            bands[1, :, cut] = lo
    first = dot(gather[...], bands[0])
    second = dot(gather[: 2 * PR], bands[1])
    by_re = first[:PR] + first[2 * PR : 3 * PR] + second[:PR]
    by_im = first[PR : 2 * PR] + first[3 * PR :] + second[PR:]
    left = lax.broadcasted_iota(jnp.int32, (1, LANES), 1) < LANES // 2
    sign = jnp.where(left, 1.0, -1.0)
    turn = LANES // 2
    for j in range(LEDS):
        col = box_corner(pat, lrow, lcol, frame, j)[1]
        halves = []
        for parity in (0, 1):
            cut = slice((2 * j + parity) * LANES, (2 * j + parity + 1) * LANES)
            band = by_re[:, cut] + sign * pltpu.roll(by_im[:, cut], turn, 1)
            halves.append(
                pairs[0, parity] * band + sign * pairs[1, parity] * pltpu.roll(band, turn, 1)
            )
        even, odd = halves
        re_hi, re_lo = split(jnp.where(left, even, pltpu.roll(odd, turn, 1)))
        im_hi, im_lo = split(jnp.where(left, pltpu.roll(even, turn, 1), odd))
        stack = jnp.concatenate([re_hi, im_hi, re_lo, im_lo], axis=0)
        placed = dot(stack, column_place(col)).astype(BF16)
        rows = pl.ds(pl.multiple_of((f * LEDS + j) * PR, PR), PR)
        for h in (0, 1):
            for c in (0, 1):
                n = 2 * h + c
                wide[h, rows, c * TW : (c + 1) * TW] = placed[n * PR : (n + 1) * PR]


def row_places(first_frame, frames, pat, lrow, lcol):
    total_rows = frames * LEDS * PR
    lane = lax.broadcasted_iota(jnp.int32, (1, total_rows), 1)
    box = lane // PR
    target = row_order(lane & (PR - 1))
    for f in range(frames):
        for j in range(LEDS):
            row = box_corner(pat, lrow, lcol, first_frame + f, j)[0]
            target = target + jnp.where(box == f * LEDS + j, row, 0)
    return ones_where(lax.broadcasted_iota(jnp.int32, (TH, total_rows), 0) == target)


def place_pair(which, choose, wide, grad):
    for c in (0, 1):
        cut = pl.ds(pl.multiple_of(c * TW + which * (2 * LANES), LANES), 2 * LANES)
        both = dot(choose, wide[0, :, cut]) + dot(choose, wide[1, :, cut])
        for n in (0, 1):
            grad[2 * which + n, c] = both[:, n * LANES : (n + 1) * LANES]


def pack_edge(value, first):
    lane = lax.broadcasted_iota(jnp.int32, (TH // 8, LANES), 1) // MARGIN
    packed = jnp.zeros((TH // 8, LANES), F32)
    for b in range(8):
        piece = value[b * 32 : (b + 1) * 32]
        piece = pltpu.roll(piece, (MARGIN * b - first) % LANES, 1)
        packed = jnp.where(lane == b, piece, packed)
    return packed


def unpack_edge(packed, first):
    return jnp.concatenate(
        [pltpu.roll(packed, (first - MARGIN * b) % LANES, 1) for b in range(8)], axis=0
    )


def dequantize(raw, scales, dequant):
    frames, rows, width = raw.shape
    dequant[:, :LANES] = jnp.zeros((frames * rows, LANES), F32)
    dequant[:, LANES + width :] = jnp.zeros((frames * rows, LANES), F32)
    lane = lax.broadcasted_iota(jnp.int32, (rows, LANES), 1) // BC
    upper = lax.broadcasted_iota(jnp.int32, (rows, LANES), 0) < BR
    blocks = scales.shape[2]
    per = LANES // BC
    for first in range(0, blocks, LANES):
        count = min(LANES, blocks - first)
        for f in range(frames):
            pair = scales[f, :, first : first + count].astype(F32)
            if count < LANES:
                pair = jnp.concatenate([pair, jnp.zeros((2, LANES - count), F32)], axis=1)
            factors = jnp.where(
                upper,
                jnp.broadcast_to(pair[0:1], (rows, LANES)),
                jnp.broadcast_to(pair[1:2], (rows, LANES)),
            )
            for k in range(count // per):
                column = (first // per + k) * LANES
                spread = jnp.take_along_axis(factors, lane + per * k, axis=1)
                codes = raw[f, :, column : column + LANES].astype(F32)
                dequant[f * rows : (f + 1) * rows, LANES + column : 2 * LANES + column] = (
                    codes * spread
                )


def cut_message(dequant, tile):
    start = CORE * tile - MARGIN + LANES
    aligned = pl.multiple_of(start // LANES * LANES, LANES)
    offset = start - aligned + MARGIN
    wide = dequant[:, pl.ds(aligned, TW + LANES)]
    wide = pltpu.roll(wide, TW + LANES - offset, 1)
    lane = lax.broadcasted_iota(jnp.int32, (1, LANES), 1)
    last = jnp.where(lane < LANES - MARGIN, wide[:, TW - LANES : TW], wide[:, TW:])
    return jnp.concatenate([wide[:, : TW - LANES], last], axis=1).astype(BF16)


def centred():
    y = lax.broadcasted_iota(jnp.int32, (TH, 1), 0).astype(F32) - (TH - 1) / 2.0
    lane = lax.broadcasted_iota(jnp.int32, (1, TW), 1)
    x = lane.astype(F32) - (CORE - 1) / 2.0
    return y, x, lane


Y_NORM = float(np.sum((np.arange(TH) - (TH - 1) / 2.0) ** 2) * CORE)
X_NORM = float(np.sum((np.arange(CORE) - (CORE - 1) / 2.0) ** 2) * TH)


def parity_pick(parity):
    v = lax.broadcasted_iota(jnp.int32, (PC, LANES), 0)
    lane = lax.broadcasted_iota(jnp.int32, (PC, LANES), 1)
    return ones_where(v == 2 * (lane & (PC // 2 - 1)) + parity)


def build_band(half, pd, cols, fold, pairs):
    lane = lax.broadcasted_iota(jnp.int32, (1, TW), 1)
    sign = (2 - 4 * (lane & 1)).astype(F32)
    left = lane[:, :LANES] < LANES // 2
    for h in (0, 1):
        re, im = (
            jnp.concatenate(
                [
                    half[h, c, TH - PC // 2 :, :].astype(F32) * 2.0,
                    half[h, c, : PC // 2, :].astype(F32) * sign,
                ],
                axis=0,
            )
            for c in (0, 1)
        )
        cols[h, :PC, :TW] = re.astype(BF16)
        cols[h, :PC, TW:] = im.astype(BF16)
        cols[h, PC:, :TW] = (-im).astype(BF16)
        cols[h, PC:, TW:] = re.astype(BF16)
        turned = [part[:, :TH].T.astype(BF16) for part in (re, im)]
        for parity in (0, 1):
            a, b = (dot(part, parity_pick(parity)) for part in turned)
            cut = slice(h * LANES, (h + 1) * LANES)
            fold[parity, :TH, cut] = jnp.where(left, a, -b).astype(BF16)
            fold[parity, TH:, cut] = jnp.where(left, b, a).astype(BF16)
    for c in (0, 1):
        hi = pd[c].astype(BF16)
        lo, last = split(pd[c] - hi.astype(F32))
        for parity in (0, 1):
            pick = parity_pick(parity)
            pairs[c, parity] = dot(hi, pick) + dot(lo, pick) + dot(last, pick)


def build_columns(half, table):
    lane = lax.broadcasted_iota(jnp.int32, (1, TW), 1)
    sign = (1 - 2 * (lane & 1)).astype(F32)
    for i in (0, 1):
        rows = pl.ds(i * LANES, LANES)
        for h in (0, 1):
            re = half[h, 0, rows, :].astype(F32)
            im = half[h, 1, rows, :].astype(F32)
            for n, factor in ((0, None), (1, sign)):
                a = re if factor is None else re * factor
                b = im if factor is None else im * factor
                upper = pl.ds(n * LANES, LANES)
                lower = pl.ds((2 + n) * LANES, LANES)
                for k in range(BLOCKS):
                    cut = slice(k * LANES, (k + 1) * LANES)
                    table[i, h, k, upper, :LANES] = a[:, cut].astype(BF16)
                    table[i, h, k, upper, LANES:] = b[:, cut].astype(BF16)
                    table[i, h, k, lower, :LANES] = (-b[:, cut]).astype(BF16)
                    table[i, h, k, lower, LANES:] = a[:, cut].astype(BF16)


def object_rows(i, new, rows_table, lhs):
    parts = []
    for parity in (0, 1):
        data = [
            jnp.concatenate(
                [new[k, c, pl.ds(parity, HALF, stride=2), :] for k in (i, i + 2)], axis=1
            )
            for c in (0, 1)
        ]
        hi, lo = split(jnp.concatenate(data, axis=0))
        t_hi, t_lo = rows_table[parity, 0], rows_table[parity, 1]
        parts.append(dot(t_hi, hi) + dot(t_hi, lo) + dot(t_lo, hi))
    for n, value in enumerate((parts[0] + parts[1], parts[0] - parts[1])):
        hi, lo = split(value)
        rows = pl.ds(n * HALF, HALF)
        for h, part in enumerate((hi, lo)):
            lhs[h, rows, : 2 * LANES] = part[:HALF]
            lhs[h, rows, 2 * LANES :] = part[HALF:]


def object_block(i, k, lhs, table):
    hi, lo = lhs[0], lhs[1]
    return dot(hi, table[i, 0, k]) + dot(lo, table[i, 0, k]) + dot(hi, table[i, 1, k])


def encode(value, code, unit):
    for g in range(TH // CODE_ROWS):
        rows = slice(g * CODE_ROWS, (g + 1) * CODE_ROWS)
        piece = value[rows]
        top = jnp.max(jnp.abs(piece), axis=0, keepdims=True)
        unit[g : g + 1] = top * (1.0 / CODE_TOP)
        ratio = jnp.where(top > 0.0, CODE_TOP / top, 0.0)
        whole = jnp.clip(jnp.round(piece * ratio), -CODE_TOP, CODE_TOP)
        code[rows] = whole.astype(jnp.int32).astype(jnp.int16)


def decode(code, unit):
    return jnp.concatenate(
        [
            code[g * CODE_ROWS : (g + 1) * CODE_ROWS].astype(jnp.int32).astype(F32)
            * unit[g : g + 1]
            for g in range(TH // CODE_ROWS)
        ],
        axis=0,
    )


def update_kernel(
    tiles,
    pat_h,
    lrow_h,
    lcol_h,
    raw_h,
    scales_h,
    flat_h,
    spec_h,
    pup_h,
    spread_h,
    gather_h,
    rows_h,
    half_h,
    fresh,
    stitched,
    pat,
    lrow,
    lcol,
    raw,
    scales,
    flat,
    spec,
    pup,
    spread,
    gather,
    rows_table,
    half,
    cols,
    fold,
    pairs,
    bands,
    dequant,
    message,
    arrived,
    window,
    gains,
    flat_out,
    flat_in,
    slope_out,
    slope_in,
    sums,
    coef,
    halves,
    pd,
    wide,
    lit,
    mid,
    field,
    estimate,
    grad,
    got,
    code,
    unit,
    far_code,
    far_unit,
    new,
    table,
    lhs,
    image,
    edge_out,
    edge_in,
    load,
    send,
    recv,
    side_send,
    side_recv,
):
    frames = raw.shape[0]
    rows = raw.shape[1]
    group = lax.axis_index("grp")
    tile = lax.axis_index("tile")
    core = lax.rem(group, 2)
    mate = {"grp": group + 1 - 2 * core}
    partner = {"grp": group + 2 - 4 * lax.div(group, 2)}
    right = {"tile": lax.rem(tile + 1, tiles)}
    left = {"tile": lax.rem(tile + tiles - 1, tiles)}

    def side(number, src, dst, device):
        return pltpu.make_async_remote_copy(
            src_ref=src,
            dst_ref=dst,
            send_sem=side_send.at[number],
            recv_sem=side_recv.at[number],
            device_id=device,
            device_id_type=MESH,
        )

    def block(source, target):
        return pltpu.make_async_remote_copy(
            src_ref=message.at[target],
            dst_ref=arrived.at[source],
            send_sem=send.at[target],
            recv_sem=recv.at[source],
            device_id={"tile": target},
            device_id_type=MESH,
        )

    loads = [
        pltpu.make_async_copy(src, dst, load.at[n])
        for n, (src, dst) in enumerate(
            (
                (raw_h, raw),
                (scales_h, scales),
                (pat_h, pat),
                (lrow_h, lrow),
                (lcol_h, lcol),
                (flat_h, flat),
                (spec_h, spec),
                (pup_h, pup),
                (half_h, half),
                (spread_h, spread),
                (gather_h, gather),
                (rows_h, rows_table),
            )
        )
    ]
    for copy in loads:
        copy.start()
    barrier = pltpu.get_barrier_semaphore()

    @pl.loop(1, tiles)
    def _(i):
        pl.semaphore_signal(
            barrier, inc=1, device_id={"tile": lax.rem(tile + i, tiles)}, device_id_type=MESH
        )

    for device in (mate, partner):
        pl.semaphore_signal(barrier, inc=1, device_id=device, device_id_type=MESH)

    loads[0].wait()
    loads[1].wait()
    dequantize(raw, scales, dequant)
    pl.semaphore_wait(barrier, tiles + 1)

    @pl.loop(1, tiles)
    def _(i):
        target = lax.rem(tile + i, tiles)
        message[target] = cut_message(dequant, target)
        block(tile, target).start()

    arrived[tile] = cut_message(dequant, tile)
    loads[5].wait()
    for k in range(BLOCKS - 1):
        gains[:, k * LANES : (k + 1) * LANES] = flat[k * LANES : (k + 1) * LANES, :].T
    tail = jnp.concatenate(
        [flat[3 * LANES :, :], jnp.zeros((TW - CORE, TH), F32)], axis=0
    ).T
    gains[:, 3 * LANES :] = tail
    flat_out[0] = pack_edge(tail, 80)
    flat_out[1] = pack_edge(gains[:, :LANES], 0)
    flats = [
        side(0, flat_out.at[0], flat_in.at[0], right),
        side(1, flat_out.at[1], flat_in.at[1], left),
    ]
    for copy in flats:
        copy.start()

    for copy in loads[2:5] + loads[6:]:
        copy.wait()
    load_halves(spec, pup, halves, pd)
    build_band(half, pd, cols, fold, pairs)
    first_frame = group * frames

    def forward(f):
        estimate[f] = forward_frame(
            f, first_frame + f, pat, lrow, lcol, halves, pd, cols, spread, wide, lit, mid, field
        )

    pl.loop(0, frames - 1)(forward)
    build_columns(half, table)

    y, x, lane = centred()
    edge = lane[:, 3 * LANES :]
    for copy in flats:
        copy.wait_recv()
    outer = jnp.where(
        edge < CORE + MARGIN, unpack_edge(flat_in[1], 96), unpack_edge(flat_in[0], 112)
    )
    own = edge < CORE
    after = edge < CORE + MARGIN
    blank = ((~own) & after & (tile == tiles - 1)) | ((~after) & (tile == 0))
    gains[:, 3 * LANES :] = jnp.where(
        blank, 0.0, jnp.where(own, gains[:, 3 * LANES :], outer)
    )
    sums[...] = jnp.zeros_like(sums)

    @pl.loop(1, tiles + 1)
    def _(i):
        source = lax.rem(tile + tiles - i, tiles)

        @pl.when(i < tiles)
        def _():
            block(source, tile).wait_recv()

        here = pl.ds(pl.multiple_of(source * rows, rows), rows)
        values = arrived[source].astype(F32)
        for f in range(frames):
            flattened = values[f * rows : (f + 1) * rows] * gains[here, :]
            window[f, here, :] = flattened
            sums[0, f] += flattened
            sums[1, f] += flattened * (y[:rows] + (source * rows).astype(F32))

    inside = (lane < CORE).astype(F32)
    slopes = []
    for f in range(frames):
        columns = jnp.sum(sums[0, f], axis=0, keepdims=True)
        tilted = jnp.sum(sums[1, f], axis=0, keepdims=True)
        slope_y = jnp.sum(tilted * inside, axis=1, keepdims=True) / Y_NORM
        slope_x = jnp.sum(columns * (x * inside), axis=1, keepdims=True) / X_NORM
        slopes.append((slope_y, slope_x))
        slope_out[f : f + 1] = jnp.broadcast_to(slope_y, (1, LANES))
        slope_out[frames + f : frames + f + 1] = jnp.broadcast_to(slope_x, (1, LANES))
    copies = [side(2, slope_out, slope_in.at[0], right), side(3, slope_out, slope_in.at[1], left)]
    for copy in copies:
        copy.start()
    forward(frames - 1)
    for copy in copies:
        copy.wait_recv()
    x_edge = x[:, 3 * LANES :]
    for f in range(frames):
        slope_y, slope_x = slopes[f]
        coef[f, 0:1, : 3 * LANES] = jnp.broadcast_to(slope_y, (1, 3 * LANES))
        coef[f, 1:2, : 3 * LANES] = slope_x * x[:, : 3 * LANES]
        row_y = jnp.where(
            own, slope_y, jnp.where(after, slope_in[1, f : f + 1], slope_in[0, f : f + 1])
        )
        row_x = jnp.where(
            own,
            slope_x * x_edge,
            jnp.where(
                after,
                slope_in[1, frames + f : frames + f + 1] * (x_edge - CORE),
                slope_in[0, frames + f : frames + f + 1] * (x_edge - 32.0),
            ),
        )
        coef[f, 0:1, 3 * LANES :] = jnp.where(blank, 0.0, row_y)
        coef[f, 1:2, 3 * LANES :] = jnp.where(blank, 0.0, row_x)

    @pl.loop(0, frames)
    def _(f):
        misfit = estimate[f] - window[f] + coef[f, 0:1] * y + coef[f, 1:2]
        backward_frame(
            f, first_frame + f, misfit, pat, lrow, lcol, pairs, fold, gather, field, bands, wide
        )

    choose = row_places(first_frame, frames, pat, lrow, lcol)
    place_pair(1 - core, choose, wide, grad)

    pieces = [(i, c) for i in (0, 1) for c in (0, 1)]
    first = [
        side(4 + n, grad.at[2 - 2 * core + i, c], got.at[i, c], mate)
        for n, (i, c) in enumerate(pieces)
    ]
    for copy in first:
        copy.start()
    place_pair(core, choose, wide, grad)
    second = []
    units = []
    for n, (i, c) in enumerate(pieces):
        first[n].wait_recv()
        encode(grad[2 * core + i, c] + got[i, c], code.at[n], unit.at[n])
        second.append(side(8 + n, code.at[n], far_code.at[n], partner))
        units.append(side(18 + n, unit.at[n], far_unit.at[n], partner))
        units[n].start()
        second[n].start()
    third = []
    for i in (0, 1):
        mine = 2 * core + i
        lanes = pl.ds(pl.multiple_of(mine * LANES, LANES), LANES)
        for c in (0, 1):
            n = 2 * i + c
            units[n].wait_recv()
            second[n].wait_recv()
            total = decode(code.at[n], unit.at[n]) + decode(far_code.at[n], far_unit.at[n])
            new[mine, c] = spec[c, :, lanes] - STEP * total
            third.append(side(12 + n, new.at[mine, c], new.at[mine, c], mate))
            third[n].start()
        for c in (0, 1):
            third[2 * i + c].wait_recv()
        for k in (i, i + 2):
            fresh[:, :, k * LANES : (k + 1) * LANES] = new[k]
        object_rows(i, new, rows_table, lhs)
        if i == 0:
            for k in range(BLOCKS):
                image[k] = object_block(i, k, lhs, table)
    image[3] += object_block(1, 3, lhs, table)
    for c in (0, 1):
        value = image[3, :, c * LANES : (c + 1) * LANES]
        edge_out[0, c] = pack_edge(value, 96)
        edge_out[1, c] = pack_edge(value, 112)
    edges = [
        side(16, edge_out.at[0], edge_in.at[0], right),
        side(17, edge_out.at[1], edge_in.at[1], left),
    ]
    for copy in edges:
        copy.start()
    for k in range(BLOCKS - 1):
        image[k] += object_block(1, k, lhs, table)
    for c in (0, 1):
        for k in (1, 2):
            stitched[c, k * LANES : (k + 1) * LANES, :] = image[
                k, :, c * LANES : (c + 1) * LANES
            ].T
    place = edge.astype(F32) - float(3 * LANES)
    at_head = (place < MARGIN) & (tile > 0)
    at_tail = (place >= 80) & (place < 96) & (tile < tiles - 1)
    for copy in edges:
        copy.wait_recv()
    for c in (0, 1):
        mine = image[0, :, c * LANES : (c + 1) * LANES]
        other = unpack_edge(edge_in[0, c], 0)
        blend = mine * ((place + 16.5) / OV) + other * ((15.5 - place) / OV)
        stitched[c, :LANES, :] = jnp.where(at_head, blend, mine).T
        mine = image[3, :, c * LANES : (c + 1) * LANES]
        other = unpack_edge(edge_in[1, c], 80)
        blend = mine * ((111.5 - place) / OV) + other * ((place - 79.5) / OV)
        stitched[c, 3 * LANES :, :] = jnp.where(at_tail, blend, mine).T[: CORE - 3 * LANES]
    for copy in flats + copies + first + second + units + third + edges:
        copy.wait_send()

    @pl.loop(1, tiles)
    def _(i):
        block(tile, lax.rem(tile + i, tiles)).wait_send()


def update(raw, scales, flat, spectrum, pupil, patterns, led_row, led_col):
    tiles = lax.axis_size("tile")
    frames, rows, width = raw.shape
    deep = frames * rows
    tables = [jnp.asarray(t) for t in band_tables() + object_tables()]
    picks = [patterns, led_row, led_col]
    hbm = pl.BlockSpec(memory_space=pltpu.MemorySpace.HBM)
    arrays = [
        pltpu.with_memory_space_constraint(a, pltpu.MemorySpace.HBM)
        for a in picks + [raw, scales, flat, spectrum, pupil] + tables
    ]
    small = (TH // 8, LANES)
    part = (2, TH, LANES)
    scratch = [pltpu.SMEM(a.shape, a.dtype) for a in picks]
    scratch += [pltpu.VMEM(a.shape, a.dtype) for a in arrays[3:]]
    scratch += [
        pltpu.VMEM((2, 2 * PC, 2 * TW), BF16),
        pltpu.VMEM((2, 2 * TH, 2 * LANES), BF16),
        pltpu.VMEM((2, 2, PR, LANES), F32),
        pltpu.VMEM((2, TH, 2 * LEDS * LANES), BF16),
        pltpu.VMEM((deep, width + 2 * LANES), F32),
        pltpu.VMEM((tiles, deep, TW), BF16),
        pltpu.VMEM((tiles, deep, TW), BF16),
        pltpu.VMEM((frames, TH, TW), F32),
        pltpu.VMEM((TH, TW), F32),
        pltpu.VMEM((2,) + small, F32),
        pltpu.VMEM((2,) + small, F32),
        pltpu.VMEM((2 * frames, LANES), F32),
        pltpu.VMEM((2, 2 * frames, LANES), F32),
        pltpu.VMEM((2, frames, rows, TW), F32),
        pltpu.VMEM((frames, 8, TW), F32),
        pltpu.VMEM((2, TH, 2 * TW), BF16),
        pltpu.VMEM((2, PR, PC), F32),
        pltpu.VMEM((2, frames * LEDS * PR, 2 * TW), BF16),
        pltpu.VMEM((LEDS * PR, 2 * PC), F32),
        pltpu.VMEM((LEDS * PR, 2 * TW), F32),
        pltpu.VMEM((frames, LEDS, 2, TH, TW), F32),
        pltpu.VMEM((frames, TH, TW), F32),
        pltpu.VMEM((BLOCKS,) + part, F32),
        pltpu.VMEM((2,) + part, F32),
        pltpu.VMEM((4, TH, LANES), jnp.int16),
        pltpu.VMEM((4, TH // CODE_ROWS, LANES), F32),
        pltpu.VMEM((4, TH, LANES), jnp.int16),
        pltpu.VMEM((4, TH // CODE_ROWS, LANES), F32),
        pltpu.VMEM((BLOCKS,) + part, F32),
        pltpu.VMEM((2, 2, BLOCKS, TW, 2 * LANES), BF16),
        pltpu.VMEM((2, TH, TW), BF16),
        pltpu.VMEM((BLOCKS, TH, 2 * LANES), F32),
        pltpu.VMEM((2, 2) + small, F32),
        pltpu.VMEM((2, 2) + small, F32),
        pltpu.SemaphoreType.DMA((12,)),
        pltpu.SemaphoreType.DMA((tiles,)),
        pltpu.SemaphoreType.DMA((tiles,)),
        pltpu.SemaphoreType.DMA((22,)),
        pltpu.SemaphoreType.DMA((22,)),
    ]
    return pl.pallas_call(
        functools.partial(update_kernel, tiles),
        in_specs=[hbm] * len(arrays),
        out_specs=[pl.BlockSpec(memory_space=pltpu.VMEM)] * 2,
        out_shape=[
            jax.ShapeDtypeStruct((2, TH, TW), F32),
            jax.ShapeDtypeStruct((2, CORE, TH), F32),
        ],
        scratch_shapes=scratch,
        compiler_params=pltpu.CompilerParams(
            collective_id=1, has_side_effects=True, vmem_limit_bytes=50 * 2**20
        ),
        name="update",
    )(*arrays)


def hand_over(first, second, first_out, second_out, sem):
    copies = [
        pltpu.make_async_copy(
            src.at[c, q * (src.shape[1] // 4) : (q + 1) * (src.shape[1] // 4)],
            dst.at[c, q * (src.shape[1] // 4) : (q + 1) * (src.shape[1] // 4)],
            sem.at[8 * n + 4 * c + q],
        )
        for n, (src, dst) in enumerate(((first, first_out), (second, second_out)))
        for c in (0, 1)
        for q in range(4)
    ]
    for copy in copies:
        copy.start()
    for copy in copies:
        copy.wait()


def deliver(fresh, stitched):
    hbm = pl.BlockSpec(memory_space=pltpu.MemorySpace.HBM)
    return pl.pallas_call(
        hand_over,
        in_specs=[pl.BlockSpec(memory_space=pltpu.VMEM)] * 2,
        out_specs=[hbm] * 2,
        out_shape=[jax.ShapeDtypeStruct(a.shape, a.dtype) for a in (fresh, stitched)],
        scratch_shapes=[pltpu.SemaphoreType.DMA((16,))],
        compiler_params=pltpu.CompilerParams(vmem_limit_bytes=4 * 2**20),
        name="deliver",
    )(fresh, stitched)


def body(raw, scales, flat, spectrum, pupil, patterns, led_row, led_col):
    fresh, stitched = update(
        raw, scales, flat.T, spectrum[0], pupil, patterns.T, led_row, led_col
    )
    fresh, stitched = deliver(fresh, stitched)
    return (fresh[None], jnp.swapaxes(stitched, 1, 2))


def solution(mesh):
    return jax.shard_map(
        body,
        mesh=mesh,
        in_specs=(
            P("grp", "tile", None),
            P("grp", "tile", None),
            P(None, "tile"),
            P("tile", None, None, None),
            P(),
            P(),
            P(),
            P(),
        ),
        out_specs=(P("tile", None, None, None), P(None, None, "tile")),
        check_vma=False,
    )
```
